128 devices in a mesh: seq: 16 (over y, x_hi, core), head: 8 (over z, x_lo).
Axes of the slice: x: 4 (x_hi: 2, x_lo: 2; x = x_hi * 2 + x_lo), y: 4, z: 4, core: 2. Of those that a mesh axis runs over, the one named last changes fastest.
Arguments:
- queries: bfloat16 [2048, 8192], P('seq', 'head'), may hold values from -24 to 24
- key_rows: bfloat16 [2048, 1024], P('seq', 'head'), may hold values from -6 to 6
- value_rows: bfloat16 [2048, 1024], P('seq', 'head'), may hold values from -6 to 6
- out_weight: bfloat16 [8192, 8192], P('head'), may hold values from -0.5 to 0.5
- residual: bfloat16 [2048, 8192], P('seq', 'head'), may hold values from -54 to 54
- norm_gain: float32 [8192], replicated, may hold values from 0.1 to 1.9
- gate_weight: bfloat16 [8192, 28672], P(None, ('seq', 'head')), may hold values from -0.0625 to 0.0625
- up_weight: bfloat16 [8192, 28672], P(None, ('seq', 'head')), may hold values from -0.0625 to 0.0625
Outputs:
- edit_keys: bfloat16 [2048, 28672], P(None, ('seq', 'head'))
- hidden_state: bfloat16 [2048, 8192], P('seq', 'head')
The draws below stay inside these ranges and needn't reach their ends.
All inputs are finite; a program needn't handle non-finite values.
Results may differ from the reference program's by a relative error of at most 0.019.
Values may be sent and summed in bfloat16 or wider, within the bound.
No kernel may reach another device: no remote copies, remote signals or barrier semaphores. Data moves between devices by JAX's collectives and lax.ppermute only.
A program may use at most 128 MiB of HBM per device.

```python
import math
import jax
import jax.numpy as jnp
from jax import lax

D = 8192
QH = 64
KVH = 8
HD = 128
FF = 28672
TOKENS = 2048


def attention_draw(key):
    base_key = jax.random.fold_in(key, 17)
    query_key, keys_key = jax.random.split(base_key, 2)
    query_vals = jnp.clip(1.5 * jax.random.normal(query_key, (TOKENS, QH * HD), jnp.float32), -9.0, 9.0)
    key_vals = jnp.clip(jax.random.normal(keys_key, (TOKENS, KVH * HD), jnp.float32), -6.0, 6.0)
    return (query_vals, key_vals)


def draw_queries(key, part):
    return attention_draw(key)[0].astype(jnp.bfloat16)


def draw_key_rows(key, part):
    return attention_draw(key)[1].astype(jnp.bfloat16)


def draw_residual(key, part):
    base_key = jax.random.fold_in(key, 29)
    row_key, column_key, value_key = jax.random.split(base_key, 3)
    row_scale = jnp.exp(jax.random.uniform(row_key, (TOKENS, 1), jnp.float32, math.log(0.3), math.log(3.0)))
    ramp = 0.5 + jnp.arange(D, dtype=jnp.float32)[None, :] / D
    column_scale = ramp * jnp.exp(jax.random.uniform(column_key, (1, D), jnp.float32, math.log(0.3), math.log(3.0)))
    values = jnp.clip(jax.random.normal(value_key, (TOKENS, D), jnp.float32), -4.0, 4.0)
    return (values * row_scale * column_scale).astype(jnp.bfloat16)


def strengthened(entries, key, source, target, parts, factor):
    def block_of(dim):
        return (jnp.arange(entries.shape[dim]) // (entries.shape[dim] // parts)).reshape((-1,) + (1,) * (entries.ndim - 1 - dim))

    near = jax.random.permutation(key, parts)[block_of(target)]
    other_side = (block_of(target) + parts // 2) % parts
    return jnp.where((block_of(source) == near) | (block_of(source) == other_side), factor * entries, entries)


def shard_levels(stream_key, extent, pieces, low, high):
    gain, own = 1.0, jax.random.fold_in(stream_key, 6)
    for dim, shards_of in pieces:
        heights = jnp.exp(jax.random.uniform(jax.random.fold_in(own, dim), (shards_of,), jnp.float32, low / len(pieces), high / len(pieces)))
        gain = gain * jnp.repeat(heights, extent[dim] // shards_of).reshape([-1 if axis == dim else 1 for axis in range(len(extent))])
    return gain


def bell_draw(own_key, shape, spread, most, shards=(), kind=jnp.bfloat16):
    entries = jax.random.normal(own_key, shape, jnp.float32) * spread
    if len(shards) > 0:
        entries = shard_levels(own_key, shape, shards, -0.22, 0.18) * entries
    return jnp.clip(entries, min=-most, max=most).astype(kind)


def bell_draw_with(rng, extent, deviation, bound, pieces, heavy, kind=jnp.bfloat16):
    drawn = deviation * jax.random.normal(rng, extent, jnp.float32)
    if pieces:
        drawn = drawn * shard_levels(rng, extent, pieces, -0.22, 0.18)
    return jnp.clip(strengthened(drawn, jax.random.fold_in(rng, 3), *heavy), -bound, bound).astype(kind)


def setup_inputs(seed: int = 0) -> dict:
    keys = jax.random.split(jax.random.key(seed), 9)
    return {
        "queries": draw_queries(jax.random.fold_in(keys[8], 71), 0),
        "key_rows": draw_key_rows(jax.random.fold_in(keys[8], 71), 0),
        "value_rows": bell_draw(keys[2], (TOKENS, KVH * HD), 1.0, 6.0, ((0, 16), (1, 8))),
        "out_weight": bell_draw_with(keys[3], (QH * HD, D), (2 * HD) ** -0.5, 0.5, ((0, 8),), (0, 1, 8, 2.0)),
        "residual": draw_residual(jax.random.fold_in(keys[8], 71), 0),
        "norm_gain": jnp.clip(1.0 + 0.18 * jax.random.normal(keys[5], (D,), jnp.float32), 0.1, 1.9),
        "gate_weight": bell_draw(keys[6], (D, FF), D ** -0.5, 0.0625, ((1, 128),)),
        "up_weight": bell_draw(keys[7], (D, FF), D ** -0.5, 0.0625, ((1, 128),)),
    }


very_low = -1e+30

def group_attend(group_item):
    group_queries, group_keys, group_values = group_item
    length = group_queries.shape[1]
    scores = jnp.einsum('gqd,kd->gqk', group_queries.astype(jnp.float32), group_keys.astype(jnp.float32), precision=lax.Precision.HIGHEST) / jnp.sqrt(jnp.float32(HD))
    query_places = jnp.arange(length, dtype=jnp.int32)
    visible = query_places[:, None] >= query_places[None, :]
    scores = jnp.where(visible[None], scores, jnp.float32(very_low))
    maxima = lax.optimization_barrier(jnp.max(scores, axis=-1, keepdims=True))
    weights = jnp.exp(scores - maxima)
    totals = lax.optimization_barrier(jnp.sum(weights, axis=-1))
    summed = jnp.einsum('gqk,kd->gqd', weights, group_values.astype(jnp.float32), precision=lax.Precision.HIGHEST)
    return summed / totals[..., None]

def reference(queries, key_rows, value_rows, out_weight, residual, norm_gain, gate_weight, up_weight):
    length = queries.shape[0]
    group_size = QH // KVH
    query_groups = queries.reshape(length, KVH, group_size, HD).transpose(1, 2, 0, 3)
    key_groups = key_rows.reshape(length, KVH, HD).transpose(1, 0, 2)
    value_groups = value_rows.reshape(length, KVH, HD).transpose(1, 0, 2)
    results = lax.map(group_attend, (query_groups, key_groups, value_groups))
    attended = results.transpose(2, 0, 1, 3).reshape(length, QH * HD).astype(jnp.bfloat16)
    projected = jnp.dot(attended, out_weight, preferred_element_type=jnp.float32)
    hidden_state = (residual.astype(jnp.float32) + projected).astype(jnp.bfloat16)
    widened = hidden_state.astype(jnp.float32)
    mean_square = lax.optimization_barrier(jnp.sum(widened * widened, axis=-1, keepdims=True)) / D
    normed = (widened * lax.rsqrt(mean_square + 1e-05) * norm_gain[None, :]).astype(jnp.bfloat16)
    gate_sums = jnp.dot(normed, gate_weight, preferred_element_type=jnp.float32)
    up_sums = jnp.dot(normed, up_weight, preferred_element_type=jnp.float32)
    edit_keys = (jax.nn.silu(gate_sums) * up_sums).astype(jnp.bfloat16)
    return (edit_keys, hidden_state)
```

```python
import functools
import math

import jax
import jax.numpy as jnp
from jax import lax
from jax.experimental import pallas as pl
from jax.experimental.pallas import tpu as pltpu
from jax.sharding import Mesh, PartitionSpec as P

HD = 128
LOW = -1e30
EPS = 1e-5
SEQ = ("y", "xh", "c")
HEAD = ("z", "xl")
RING = {"x": ("xh", "xl"), "y": ("y",), "z": ("z",)}
ORDERS = ("yzx", "zxy", "xyz")
WIDTHS = (384, 384, 256)
STARTS = (0, 384, 768)
OFFSETS = (0, -1, 1, 2)
BF = jnp.bfloat16
F32 = jnp.float32


def shift(x, axis, by):
    return lax.ppermute(x, RING[axis], [(i, (i + by) % 4) for i in range(4)])


def swap_core(x):
    return lax.ppermute(x, "c", [(0, 1), (1, 0)])


def attend_kernel(pos_ref, q_ref, own_ref, oth_ref, w_hbm, out_ref, w_buf, qs, acc, att, sems):
    blocks = w_buf.shape[0]
    width = w_buf.shape[2]
    for b in range(blocks):
        pltpu.make_async_copy(w_hbm.at[:, pl.ds(b * width, width)], w_buf.at[b], sems.at[b]).start()
    heads = q_ref.shape[1] // HD
    rows = q_ref.shape[0]
    cols = heads * rows
    for h in range(heads):
        qs[pl.ds(h * rows, rows), :] = q_ref[:, h * HD:(h + 1) * HD]
    group = pos_ref[0]
    core = pos_ref[1]
    factor = math.log2(math.e) / math.sqrt(HD)
    qv = qs[...]

    def scores(ref, g):
        return lax.dot_general(
            ref[g, :, :HD], qv, (((1,), (1,)), ((), ())), preferred_element_type=F32
        ) * factor

    def weigh(ref, g, p):
        return lax.dot_general(
            ref[g, :, HD:], p.astype(BF), (((0,), (0,)), ((), ())), preferred_element_type=F32
        )

    key_at = lax.broadcasted_iota(jnp.int32, (rows, cols), 0)
    row_at = lax.broadcasted_iota(jnp.int32, (rows, cols), 1) % rows
    s1 = jnp.where(key_at <= row_at, scores(own_ref, group), LOW)
    s2 = jnp.where(core == 1, scores(oth_ref, group), LOW)
    top = jnp.maximum(jnp.max(s1, axis=0, keepdims=True), jnp.max(s2, axis=0, keepdims=True))
    p1 = jnp.exp2(s1 - top)
    p2 = jnp.where(core == 1, jnp.exp2(s2 - top), 0.0)
    total = jnp.sum(p1, axis=0, keepdims=True) + jnp.sum(p2, axis=0, keepdims=True)
    acc[...] = weigh(own_ref, group, p1) + weigh(oth_ref, group, p2)

    def step(g, carry):
        top, total = carry
        s1 = scores(own_ref, g)
        s2 = scores(oth_ref, g)
        new = jnp.maximum(
            top, jnp.maximum(jnp.max(s1, axis=0, keepdims=True), jnp.max(s2, axis=0, keepdims=True))
        )
        alpha = jnp.exp2(top - new)
        p1 = jnp.exp2(s1 - new)
        p2 = jnp.exp2(s2 - new)
        total = total * alpha + jnp.sum(p1, axis=0, keepdims=True) + jnp.sum(p2, axis=0, keepdims=True)
        acc[...] = acc[...] * alpha + weigh(own_ref, g, p1) + weigh(oth_ref, g, p2)
        return new, total

    top, total = lax.fori_loop(0, group, step, (top, total))
    final = acc[...] / total
    for h in range(heads):
        att[:, h * HD:(h + 1) * HD] = final[:, h * rows:(h + 1) * rows].T.astype(BF)

    def project(b, _):
        pltpu.make_async_copy(w_hbm.at[:, pl.ds(0, width)], w_buf.at[b], sems.at[b]).wait()
        out_ref[b] = jnp.dot(att[...], w_buf[b], preferred_element_type=F32).astype(BF)
        return 0

    lax.fori_loop(0, blocks, project, 0)


def attend_project(pos, q, own, oth, w, blocks):
    rows, cols = q.shape
    depth, wide = w.shape
    width = wide // blocks
    vm = pl.BlockSpec(memory_space=pltpu.VMEM)
    return pl.pallas_call(
        attend_kernel,
        out_shape=jax.ShapeDtypeStruct((blocks, rows, width), BF),
        in_specs=[pl.BlockSpec(memory_space=pltpu.SMEM), vm, vm, vm, pl.BlockSpec(memory_space=pl.ANY)],
        out_specs=vm,
        scratch_shapes=[
            pltpu.VMEM((blocks, depth, width), BF),
            pltpu.VMEM((rows * cols // HD, HD), BF),
            pltpu.VMEM((HD, rows * cols // HD), F32),
            pltpu.VMEM((rows, cols), BF),
            pltpu.SemaphoreType.DMA((blocks,)),
        ],
        compiler_params=pltpu.CompilerParams(vmem_limit_bytes=48 << 20),
        cost_estimate=pl.CostEstimate(flops=4 << 30, bytes_accessed=20 << 20, transcendentals=2 << 20),
        name="attend_project",
    )(pos, q, own, oth, w)


def rel_heads():
    return [(sz, par) for par in (0, 1) for sz in range(4)]


def gate_kernel(pos_ref, blk_ref, *refs):
    pieces = refs[:21]
    g_ref, u_ref, pg_ref, pu_ref, gain_ref = refs[21:26]
    own_ref, par_ref = refs[26:28]
    hid, wsc, acc, ssq, sems = refs[28:]
    i = pl.program_id(0)
    steps = pl.num_programs(0)
    x_at, y_at = pos_ref[0], pos_ref[1]

    def copies():
        for t, (sz, par) in enumerate(rel_heads()):
            for sx in ((0, 3), (1, 2))[par]:
                xg = ((x_at + OFFSETS[sx] + 4) % 4) // 2
                for sy in range(4):
                    yg = (y_at + OFFSETS[sy] + 4) % 4
                    row = pl.multiple_of((yg * 2 + xg) * 128, 128)
                    slot = {"x": sx, "y": sy, "z": sz}
                    for k in range(3):
                        a, b, c = (slot[n] for n in ORDERS[k])
                        names = pieces[7 * k:7 * k + 7]
                        half = b // 2
                        at = (b % 2) * 4 + a
                        if c == 0:
                            src = names[0].at[b * 4 + a]
                        else:
                            src = names[{1: (1, 2), 2: (4, 3), 3: (5, 6)}[c][half]].at[at]
                        dst = hid.at[t, pl.ds(row, 128), pl.ds(STARTS[k], WIDTHS[k])]
                        yield pltpu.make_async_copy(src, dst, sems.at[t])

    @pl.when(i == 0)
    def _():
        for cp in copies():
            cp.start()
        acc[...] = jnp.zeros_like(acc)
        ssq[...] = jnp.zeros_like(ssq)

    gain = gain_ref[...]
    n = g_ref.shape[0]
    for j, ref in enumerate((g_ref, u_ref, pg_ref, pu_ref)):
        wsc[pl.ds(j * n, n), :] = (ref[...].astype(F32) * gain).astype(BF)
    pltpu.make_async_copy(hid.at[i], hid.at[i], sems.at[i]).wait()
    block = hid[i]
    wide = block.astype(F32)
    sq = wide * wide
    part = sq[:, :128]
    for j in range(1, sq.shape[1] // 128):
        part = part + sq[:, j * 128:(j + 1) * 128]
    ssq[...] += part
    acc[...] += lax.dot_general(
        wsc[...], block, (((1,), (1,)), ((), ())), preferred_element_type=F32
    )

    @pl.when(i == steps - 1)
    def _():
        sums = lax.dot_general(
            jnp.ones((8, 128), F32), ssq[...], (((1,), (1,)), ((), ())),
            preferred_element_type=F32, precision=lax.Precision.HIGHEST,
        )[:1]
        scale = lax.rsqrt(sums / (steps * hid.shape[2]) + EPS)
        for j, ref in ((0, own_ref), (2, par_ref)):
            gate = acc[pl.ds(j * n, n), :] * scale
            up = acc[pl.ds((j + 1) * n, n), :] * scale
            ref[...] = (gate / (1.0 + jnp.exp(-gate)) * up).astype(BF)


def gate_up(pos, blk, pieces, weights, gain):
    n, depth = weights[0].shape
    kb = 1024
    any_spec = pl.BlockSpec(memory_space=pl.ANY)
    wspec = pl.BlockSpec((n, kb), lambda i, pos, blk: (0, blk[i]))
    tokens = 1024
    ospec = pl.BlockSpec((n, tokens), lambda i, pos, blk: (0, 0))
    return pl.pallas_call(
        gate_kernel,
        out_shape=[jax.ShapeDtypeStruct((n, tokens), BF)] * 2,
        grid_spec=pltpu.PrefetchScalarGridSpec(
            num_scalar_prefetch=2,
            grid=(depth // kb,),
            in_specs=[any_spec] * len(pieces)
            + [wspec] * 4
            + [pl.BlockSpec((1, kb), lambda i, pos, blk: (0, blk[i]))],
            out_specs=[ospec] * 2,
            scratch_shapes=[
                pltpu.VMEM((depth // kb, tokens, kb), BF),
                pltpu.VMEM((4 * n, kb), BF),
                pltpu.VMEM((4 * n, tokens), F32),
                pltpu.VMEM((tokens, 128), F32),
                pltpu.SemaphoreType.DMA((depth // kb,)),
            ],
        ),
        compiler_params=pltpu.CompilerParams(
            vmem_limit_bytes=56 << 20, dimension_semantics=("arbitrary",)
        ),
        cost_estimate=pl.CostEstimate(
            flops=2 * 4 * n * tokens * depth, bytes_accessed=32 << 20, transcendentals=1 << 20
        ),
        name="gate_up",
    )(pos, blk, *pieces, *weights, gain)


def gather_axis(block, axis):
    return jnp.stack([block] + [shift(block, axis, s) for s in (1, -1, 2)])


def gather_last(block, axis):
    half = block.shape[0] // 2
    low, high = block[:half], block[half:]
    l1 = shift(low, axis, 1)
    r1 = shift(high, axis, -1)
    l2 = shift(high, axis, 1)
    r2 = shift(low, axis, -1)
    o1 = shift(l1, axis, 1)
    o2 = shift(r1, axis, -1)
    return (block, l1, l2, r1, r2, o1, o2)


def gather_hidden(hidden):
    cur = [hidden[:, s:s + w] for s, w in zip(STARTS, WIDTHS)]
    for phase in range(2):
        cur = [gather_axis(c, ORDERS[k][phase]) for k, c in enumerate(cur)]
    cur = [c.reshape((16,) + c.shape[2:]) for c in cur]
    out = []
    for k in range(3):
        out.extend(gather_last(cur[k], ORDERS[k][2]))
    return out


def per_device(queries, key_rows, value_rows, out_weight, residual, norm_gain, gate_weight, up_weight):
    y_at, xh, core = lax.axis_index("y"), lax.axis_index("xh"), lax.axis_index("c")
    z_at, xl = lax.axis_index("z"), lax.axis_index("xl")
    x_at = xh * 2 + xl
    group = y_at * 2 + xh

    pair = jnp.concatenate([key_rows, value_rows], axis=1)
    spread = jnp.broadcast_to(pair[None], (8,) + pair.shape)
    own = lax.all_to_all(spread, ("y", "xh"), 0, 0, tiled=True)
    oth = swap_core(own)

    pos = jnp.stack([group, core]).astype(jnp.int32)
    partial = attend_project(pos, queries, own, oth, out_weight, 8)
    terms = lax.all_to_all(partial, HEAD, 0, 0, tiled=True)
    hidden = (residual.astype(F32) + jnp.sum(terms.astype(F32), axis=0)).astype(BF)

    gate_t, up_t = gate_weight.T, up_weight.T
    weights = (gate_t, up_t, swap_core(gate_t), swap_core(up_t))

    pieces = gather_hidden(hidden)
    blk = jnp.stack(
        [((z_at + OFFSETS[sz] + 4) % 4) * 2 + (xl + par) % 2 for sz, par in rel_heads()]
    ).astype(jnp.int32)
    pos2 = jnp.stack([x_at, y_at]).astype(jnp.int32)
    mine, theirs = gate_up(pos2, blk, pieces, weights, norm_gain[None, :])
    got = swap_core(theirs)
    n = mine.shape[0]
    a = mine.reshape(n, 8, 1, 128)
    b = got.reshape(n, 8, 1, 128)
    merged = jnp.where(core == 0, jnp.concatenate([a, b], 2), jnp.concatenate([b, a], 2))
    return merged.reshape(n, 2048).T, hidden


def solution(mesh):
    devices = mesh.devices.reshape(4, 2, 2, 4, 2)
    fine = Mesh(devices, ("y", "xh", "c", "z", "xl"))
    both = P(SEQ, HEAD)
    cols = P(None, SEQ + HEAD)
    return jax.shard_map(
        per_device,
        mesh=fine,
        in_specs=(both, both, both, P(HEAD, None), both, P(), cols, cols),
        out_specs=(cols, both),
        check_vma=False,
    )
```

```python
import functools
import math

import jax
import jax.numpy as jnp
from jax import lax
from jax.experimental import pallas as pl
from jax.experimental.pallas import tpu as pltpu
from jax.sharding import Mesh, PartitionSpec as P

HD = 128
LOW = -1e30
EPS = 1e-5
SEQ = ("y", "xh", "c")
HEAD = ("z", "xl")
MESH = ("y", "xh", "c", "z", "xl")
MAIN = ("yzx", "zxy")
SIDE = ("xyz", "xyz")
OFFSETS = (0, -1, 1, 2)
MROWS, MCOLS = 224, 384
BF = jnp.bfloat16
F32 = jnp.float32


def shift(x, axes, by):
    pairs = []
    for core in range(2):
        for n in range(64):
            at = {"x": n // 16, "y": n // 4 % 4, "z": n % 4}
            to = dict(at)
            to[axes[core]] = (to[axes[core]] + by) % 4
            pairs.append(tuple(
                (((p["y"] * 2 + p["x"] // 2) * 2 + core) * 4 + p["z"]) * 2 + p["x"] % 2
                for p in (at, to)
            ))
    return lax.ppermute(x, MESH, pairs)


def swap_core(x):
    return lax.ppermute(x, "c", [(0, 1), (1, 0)])


def attend_kernel(pos_ref, q_ref, own_ref, oth_ref, w_hbm, out_ref, w_buf, qs, acc, att, sems):
    blocks = w_buf.shape[0]
    width = w_buf.shape[2]
    for b in range(blocks):
        pltpu.make_async_copy(w_hbm.at[:, pl.ds(b * width, width)], w_buf.at[b], sems.at[b]).start()
    heads = q_ref.shape[1] // HD
    rows = q_ref.shape[0]
    cols = heads * rows
    for h in range(heads):
        qs[pl.ds(h * rows, rows), :] = q_ref[:, h * HD:(h + 1) * HD]
    group = pos_ref[0]
    core = pos_ref[1]
    factor = math.log2(math.e) / math.sqrt(HD)
    qv = qs[...]

    def scores(ref, g):
        return lax.dot_general(
            ref[g, :, :HD], qv, (((1,), (1,)), ((), ())), preferred_element_type=F32
        ) * factor

    def weigh(ref, g, p):
        return lax.dot_general(
            ref[g, :, HD:], p.astype(BF), (((0,), (0,)), ((), ())), preferred_element_type=F32
        )

    key_at = lax.broadcasted_iota(jnp.int32, (rows, cols), 0)
    row_at = lax.broadcasted_iota(jnp.int32, (rows, cols), 1) % rows
    s1 = jnp.where(key_at <= row_at, scores(own_ref, group), LOW)
    s2 = jnp.where(core == 1, scores(oth_ref, group), LOW)
    top = jnp.maximum(jnp.max(s1, axis=0, keepdims=True), jnp.max(s2, axis=0, keepdims=True))
    p1 = jnp.exp2(s1 - top)
    p2 = jnp.where(core == 1, jnp.exp2(s2 - top), 0.0)
    total = jnp.sum(p1, axis=0, keepdims=True) + jnp.sum(p2, axis=0, keepdims=True)
    acc[...] = weigh(own_ref, group, p1) + weigh(oth_ref, group, p2)

    def step(g, carry):
        top, total = carry
        s1 = scores(own_ref, g)
        s2 = scores(oth_ref, g)
        new = jnp.maximum(
            top, jnp.maximum(jnp.max(s1, axis=0, keepdims=True), jnp.max(s2, axis=0, keepdims=True))
        )
        alpha = jnp.exp2(top - new)
        p1 = jnp.exp2(s1 - new)
        p2 = jnp.exp2(s2 - new)
        total = total * alpha + jnp.sum(p1, axis=0, keepdims=True) + jnp.sum(p2, axis=0, keepdims=True)
        acc[...] = acc[...] * alpha + weigh(own_ref, g, p1) + weigh(oth_ref, g, p2)
        return new, total

    top, total = lax.fori_loop(0, group, step, (top, total))
    final = acc[...] / total
    for h in range(heads):
        att[:, h * HD:(h + 1) * HD] = final[:, h * rows:(h + 1) * rows].T.astype(BF)

    def project(b, _):
        pltpu.make_async_copy(w_hbm.at[:, pl.ds(0, width)], w_buf.at[b], sems.at[b]).wait()
        out_ref[b] = jnp.dot(att[...], w_buf[b], preferred_element_type=F32).astype(BF)
        return 0

    lax.fori_loop(0, blocks, project, 0)


def attend_project(pos, q, own, oth, w, blocks):
    rows, cols = q.shape
    depth, wide = w.shape
    width = wide // blocks
    vm = pl.BlockSpec(memory_space=pltpu.VMEM)
    return pl.pallas_call(
        attend_kernel,
        out_shape=jax.ShapeDtypeStruct((blocks, rows, width), BF),
        in_specs=[pl.BlockSpec(memory_space=pltpu.SMEM), vm, vm, vm, pl.BlockSpec(memory_space=pl.ANY)],
        out_specs=vm,
        scratch_shapes=[
            pltpu.VMEM((blocks, depth, width), BF),
            pltpu.VMEM((rows * cols // HD, HD), BF),
            pltpu.VMEM((HD, rows * cols // HD), F32),
            pltpu.VMEM((rows, cols), BF),
            pltpu.SemaphoreType.DMA((blocks,)),
        ],
        compiler_params=pltpu.CompilerParams(vmem_limit_bytes=48 << 20),
        cost_estimate=pl.CostEstimate(flops=4 << 30, bytes_accessed=20 << 20, transcendentals=2 << 20),
        name="attend_project",
    )(pos, q, own, oth, w)


def gate_kernel(pos_ref, *refs):
    main, side = refs[:8], refs[8:16]
    g_ref, u_ref, pg_ref, pu_ref, gain_ref = refs[16:21]
    own_ref, own_ss, par_ref = refs[21:24]
    hid, wsc, acc, ssq, sems = refs[24:]
    i = pl.program_id(0)
    core = pos_ref[3]

    def place(order, slots):
        at = {}
        for n, axis in enumerate("xyz"):
            off0 = OFFSETS[slots[order[0].index(axis)]]
            off1 = OFFSETS[slots[order[1].index(axis)]]
            off = off0 if off0 == off1 else jnp.where(core == 0, off0, off1)
            at[axis] = (pos_ref[n] + off + 4) & 3
        block = at["z"] * 2 + (at["x"] & 1)
        row = pl.multiple_of((at["y"] * 2 + at["x"] // 2) * 256, 256)
        return block, row

    def source(names, slots):
        a, b, c = slots
        half = b // 2
        return names[((0, 1), (2, 3), (5, 4), (6, 7))[c][half]].at[(b % 2) * 4 + a]

    @pl.when(i == 0)
    def _():
        for c in range(4):
            for b in range(4):
                for a in range(4):
                    slots = (a, b, c)
                    src = source(main, slots)
                    t, row = place(MAIN, slots)
                    pltpu.make_async_copy(
                        src, hid.at[t, pl.ds(row, MROWS), pl.ds(0, MCOLS)], sems.at[t]
                    ).start()
                    src = source(side, slots)
                    t, row = place(SIDE, slots)
                    pltpu.make_async_copy(
                        src.at[pl.ds(0, 256)],
                        hid.at[t, pl.ds(row, 256), pl.ds(MCOLS, 128)],
                        sems.at[t],
                    ).start()
                    for j in range(3):
                        pltpu.make_async_copy(
                            src.at[pl.ds(256 + 32 * j, 32)],
                            hid.at[t, pl.ds(row + MROWS, 32), pl.ds(128 * j, 128)],
                            sems.at[t],
                        ).start()
        own_ref[...] = jnp.zeros_like(own_ref)
        acc[...] = jnp.zeros_like(acc)
        ssq[...] = jnp.zeros_like(ssq)

    gain = gain_ref[...]
    n = g_ref.shape[0]
    for j, ref in enumerate((g_ref, u_ref, pg_ref, pu_ref)):
        wsc[pl.ds(j * n, n), :] = (ref[...].astype(F32) * gain).astype(BF)
    pltpu.make_async_copy(hid.at[i], hid.at[i], sems.at[i]).wait()
    piece = 512

    def tokens(p, _):
        at = pl.multiple_of(p * piece, piece)
        block = hid[i, pl.ds(at, piece), :]
        wide = block.astype(F32)
        sq = wide * wide
        part = sq[:, :128]
        for j in range(1, sq.shape[1] // 128):
            part = part + sq[:, j * 128:(j + 1) * 128]
        ssq[pl.ds(at, piece), :] += part
        prod = lax.dot_general(
            wsc[...], block, (((1,), (1,)), ((), ())), preferred_element_type=F32
        )
        own_ref[:, pl.ds(at, piece)] += prod[:2 * n]
        acc[:, pl.ds(at, piece)] += prod[2 * n:]
        return 0

    lax.fori_loop(0, hid.shape[1] // piece, tokens, 0)

    @pl.when(i == pl.num_programs(0) - 1)
    def _():
        sums = lax.dot_general(
            jnp.ones((8, 128), F32), ssq[...], (((1,), (1,)), ((), ())),
            preferred_element_type=F32, precision=lax.Precision.HIGHEST,
        )
        own_ss[...] = sums
        first = sums.astype(BF)
        par_ref[:2 * n, :] = acc[...].astype(BF)
        par_ref[2 * n:, :] = jnp.concatenate(
            [first.astype(F32), sums - first.astype(F32)], axis=0
        ).astype(BF)


def gate_up(pos, main, side, weights, gain):
    n, depth = weights[0].shape
    kb = 512
    blocks = depth // 1024
    tokens = 2048
    any_spec = pl.BlockSpec(memory_space=pl.ANY)
    wspec = pl.BlockSpec((n, kb), lambda i, pos: (0, i * 2 + pos[3]))
    return pl.pallas_call(
        gate_kernel,
        out_shape=[
            jax.ShapeDtypeStruct((2 * n, tokens), F32),
            jax.ShapeDtypeStruct((8, tokens), F32),
            jax.ShapeDtypeStruct((2 * n + 16, tokens), BF),
        ],
        grid_spec=pltpu.PrefetchScalarGridSpec(
            num_scalar_prefetch=1,
            grid=(blocks,),
            in_specs=[any_spec] * 16
            + [wspec] * 4
            + [pl.BlockSpec((1, kb), lambda i, pos: (0, i * 2 + pos[3]))],
            out_specs=[
                pl.BlockSpec((2 * n, tokens), lambda i, pos: (0, 0), pipeline_mode=pl.Buffered(1)),
                pl.BlockSpec((8, tokens), lambda i, pos: (0, 0)),
                pl.BlockSpec((2 * n + 16, tokens), lambda i, pos: (0, 0), pipeline_mode=pl.Buffered(1)),
            ],
            scratch_shapes=[
                pltpu.VMEM((blocks, tokens, kb), BF),
                pltpu.VMEM((4 * n, kb), BF),
                pltpu.VMEM((2 * n, tokens), F32),
                pltpu.VMEM((tokens, 128), F32),
                pltpu.SemaphoreType.DMA((blocks,)),
            ],
        ),
        compiler_params=pltpu.CompilerParams(
            vmem_limit_bytes=56 << 20, dimension_semantics=("arbitrary",)
        ),
        cost_estimate=pl.CostEstimate(
            flops=4 * n * tokens * depth, bytes_accessed=32 << 20, transcendentals=0
        ),
        name="gate_up",
    )(pos, *main, *side, *weights, gain)


def finish_kernel(own_ref, ss_ref, got_ref, out_ref, *, depth):
    n = out_ref.shape[0]
    got = got_ref[...].astype(F32)
    total = ss_ref[:1] + got[2 * n:2 * n + 1] + got[2 * n + 8:2 * n + 9]
    scale = lax.rsqrt(total / depth + EPS)
    gate = (own_ref[:n] + got[:n]) * scale
    up = (own_ref[n:] + got[n:2 * n]) * scale
    out_ref[...] = (gate / (1.0 + jnp.exp(-gate)) * up).astype(BF)


def finish(own, ss, got, depth):
    rows, tokens = own.shape
    n = rows // 2
    piece = 512
    spec = lambda r: pl.BlockSpec((r, piece), lambda i: (0, i))
    return pl.pallas_call(
        functools.partial(finish_kernel, depth=depth),
        out_shape=jax.ShapeDtypeStruct((n, tokens), BF),
        grid=(tokens // piece,),
        in_specs=[spec(rows), spec(8), spec(rows + 16)],
        out_specs=spec(n),
        cost_estimate=pl.CostEstimate(flops=8 << 20, bytes_accessed=7 << 20, transcendentals=1 << 20),
        name="finish",
    )(own, ss, got)


def gather(block, order):
    axes = [(order[0][p], order[1][p]) for p in range(3)]
    a = axes[0]
    cur = jnp.stack([block, shift(block, a, 1), shift(block, a, -1), shift(block, a, 2)])
    b = axes[1]
    low = jnp.stack([cur, shift(cur, b, 1)]).reshape((8,) + block.shape)
    high = jnp.stack([shift(cur, b, -1), shift(cur, b, 2)]).reshape((8,) + block.shape)
    c = axes[2]
    l1 = shift(low, c, 1)
    r1 = shift(high, c, -1)
    l2 = shift(high, c, 1)
    r2 = shift(low, c, -1)
    o1 = shift(l1, c, 1)
    o2 = shift(r1, c, -1)
    return low, high, l1, l2, r1, r2, o1, o2


def per_device(queries, key_rows, value_rows, out_weight, residual, norm_gain, gate_weight, up_weight):
    y_at, xh, core = lax.axis_index("y"), lax.axis_index("xh"), lax.axis_index("c")
    z_at, xl = lax.axis_index("z"), lax.axis_index("xl")
    x_at = xh * 2 + xl
    group = y_at * 2 + xh

    pair = jnp.concatenate([key_rows, value_rows], axis=1)
    spread = jnp.broadcast_to(pair[None], (8,) + pair.shape)
    own = lax.all_to_all(spread, ("y", "xh"), 0, 0, tiled=True)
    oth = swap_core(own)

    pos = jnp.stack([group, core]).astype(jnp.int32)
    partial = attend_project(pos, queries, own, oth, out_weight, 8)
    terms = lax.all_to_all(partial, HEAD, 0, 0, tiled=True)
    hidden = (residual.astype(F32) + jnp.sum(terms.astype(F32), axis=0)).astype(BF)

    gate_t, up_t = gate_weight.T, up_weight.T
    weights = (gate_t, up_t, swap_core(gate_t), swap_core(up_t))

    keep = jnp.where(core == 0, hidden[:, :512], hidden[:, 512:])
    got = swap_core(jnp.where(core == 0, hidden[:, 512:], hidden[:, :512]))
    chip = jnp.where(
        core == 0, jnp.concatenate([keep, got], 0), jnp.concatenate([got, keep], 0)
    )
    main_part = chip[:MROWS, :MCOLS]
    side_part = jnp.concatenate(
        [chip[:, MCOLS:]] + [chip[MROWS:, 128 * j:128 * (j + 1)] for j in range(3)], 0
    )
    main = gather(main_part, MAIN)
    side = gather(side_part, SIDE)
    pos2 = jnp.stack([x_at, y_at, z_at, core]).astype(jnp.int32)
    own_sums, own_ss, theirs = gate_up(pos2, main, side, weights, norm_gain[None, :])
    out = finish(own_sums, own_ss, swap_core(theirs), norm_gain.shape[0])
    return out.T, hidden


def solution(mesh):
    devices = mesh.devices.reshape(4, 2, 2, 4, 2)
    fine = Mesh(devices, MESH)
    both = P(SEQ, HEAD)
    cols = P(None, SEQ + HEAD)
    return jax.shard_map(
        per_device,
        mesh=fine,
        in_specs=(both, both, both, P(HEAD, None), both, P(), cols, cols),
        out_specs=(cols, both),
        check_vma=False,
    )
```

```python
import functools
import math

import jax
import jax.numpy as jnp
from jax import lax
from jax.experimental import pallas as pl
from jax.experimental.pallas import tpu as pltpu
from jax.sharding import Mesh, PartitionSpec as P


HD = 128
LOW = -1e30
EPS = 1e-5
SEQ = ("y", "xh", "c")
HEAD = ("z", "xl")
MESH = ("y", "xh", "c", "z", "xl")
MAIN = ("yzx", "zxy")
SIDE = ("xyz", "xyz")
OFFSETS = (0, -1, 1, 2)
MROWS, MCOLS = 224, 384
BF = jnp.bfloat16
F32 = jnp.float32


def shift(x, axes, by):
    pairs = []
    for core in range(2):
        for n in range(64):
            at = {"x": n // 16, "y": n // 4 % 4, "z": n % 4}
            to = dict(at)
            to[axes[core]] = (to[axes[core]] + by) % 4
            pairs.append(tuple(
                (((p["y"] * 2 + p["x"] // 2) * 2 + core) * 4 + p["z"]) * 2 + p["x"] % 2
                for p in (at, to)
            ))
    return lax.ppermute(x, MESH, pairs)


def swap_core(x):
    return lax.ppermute(x, "c", [(0, 1), (1, 0)])


def attend_kernel(pos_ref, q_ref, own_ref, oth_ref, w_hbm, out_ref, w_buf, qs, acc, att, sems):
    blocks = w_buf.shape[0]
    width = w_buf.shape[2]
    for b in range(blocks):
        pltpu.make_async_copy(w_hbm.at[:, pl.ds(b * width, width)], w_buf.at[b], sems.at[b]).start()
    heads = q_ref.shape[1] // HD
    rows = q_ref.shape[0]
    cols = heads * rows
    for h in range(heads):
        qs[pl.ds(h * rows, rows), :] = q_ref[:, h * HD:(h + 1) * HD]
    group = pos_ref[0]
    core = pos_ref[1]
    factor = math.log2(math.e) / math.sqrt(HD)
    qv = qs[...]

    def scores(ref, g):
        return lax.dot_general(
            ref[g, :, :HD], qv, (((1,), (1,)), ((), ())), preferred_element_type=F32
        ) * factor

    def weigh(ref, g, p):
        return lax.dot_general(
            ref[g, :, HD:], p.astype(BF), (((0,), (0,)), ((), ())), preferred_element_type=F32
        )

    key_at = lax.broadcasted_iota(jnp.int32, (rows, cols), 0)
    row_at = lax.broadcasted_iota(jnp.int32, (rows, cols), 1) % rows
    s1 = jnp.where(key_at <= row_at, scores(own_ref, group), LOW)
    s2 = jnp.where(core == 1, scores(oth_ref, group), LOW)
    top = jnp.maximum(jnp.max(s1, axis=0, keepdims=True), jnp.max(s2, axis=0, keepdims=True))
    p1 = jnp.exp2(s1 - top)
    p2 = jnp.where(core == 1, jnp.exp2(s2 - top), 0.0)
    total = jnp.sum(p1, axis=0, keepdims=True) + jnp.sum(p2, axis=0, keepdims=True)
    acc[...] = weigh(own_ref, group, p1) + weigh(oth_ref, group, p2)

    def step(g, carry):
        top, total = carry
        s1 = scores(own_ref, g)
        s2 = scores(oth_ref, g)
        new = jnp.maximum(
            top, jnp.maximum(jnp.max(s1, axis=0, keepdims=True), jnp.max(s2, axis=0, keepdims=True))
        )
        alpha = jnp.exp2(top - new)
        p1 = jnp.exp2(s1 - new)
        p2 = jnp.exp2(s2 - new)
        total = total * alpha + jnp.sum(p1, axis=0, keepdims=True) + jnp.sum(p2, axis=0, keepdims=True)
        acc[...] = acc[...] * alpha + weigh(own_ref, g, p1) + weigh(oth_ref, g, p2)
        return new, total

    top, total = lax.fori_loop(0, group, step, (top, total))
    final = acc[...] / total
    for h in range(heads):
        att[:, h * HD:(h + 1) * HD] = final[:, h * rows:(h + 1) * rows].T.astype(BF)

    def project(b, _):
        pltpu.make_async_copy(w_hbm.at[:, pl.ds(0, width)], w_buf.at[b], sems.at[b]).wait()
        out_ref[b] = jnp.dot(att[...], w_buf[b], preferred_element_type=F32).astype(BF)
        return 0

    lax.fori_loop(0, blocks, project, 0)


def attend_project(pos, q, own, oth, w, blocks):
    rows, cols = q.shape
    depth, wide = w.shape
    width = wide // blocks
    vm = pl.BlockSpec(memory_space=pltpu.VMEM)
    return pl.pallas_call(
        attend_kernel,
        out_shape=jax.ShapeDtypeStruct((blocks, rows, width), BF),
        in_specs=[pl.BlockSpec(memory_space=pltpu.SMEM), vm, vm, vm, pl.BlockSpec(memory_space=pl.ANY)],
        out_specs=vm,
        scratch_shapes=[
            pltpu.VMEM((blocks, depth, width), BF),
            pltpu.VMEM((rows * cols // HD, HD), BF),
            pltpu.VMEM((HD, rows * cols // HD), F32),
            pltpu.VMEM((rows, cols), BF),
            pltpu.SemaphoreType.DMA((blocks,)),
        ],
        compiler_params=pltpu.CompilerParams(vmem_limit_bytes=48 << 20),
        cost_estimate=pl.CostEstimate(flops=4 << 30, bytes_accessed=20 << 20, transcendentals=2 << 20),
        name="attend_project",
    )(pos, q, own, oth, w)


def gate_kernel(pos_ref, *refs):
    main, side, weights = refs[:8], refs[8:16], refs[16:20]
    own_ref, own_ss, par_ref = refs[20:23]
    hid, wsc, sems, wsem = refs[23:]
    i = pl.program_id(0)
    core = pos_ref[3]
    n = weights[0].shape[0]
    kb = 512
    blocks = wsc.shape[1] // kb

    def place(order, slots):
        at = {}
        for m, axis in enumerate("xyz"):
            off0 = OFFSETS[slots[order[0].index(axis)]]
            off1 = OFFSETS[slots[order[1].index(axis)]]
            off = off0 if off0 == off1 else jnp.where(core == 0, off0, off1)
            at[axis] = (pos_ref[m] + off + 4) & 3
        col = pl.multiple_of((at["z"] * 2 + (at["x"] & 1)) * kb, kb)
        return at["y"] * 2 + at["x"] // 2, col

    def source(names, slots):
        a, b, c = slots
        half = b // 2
        return names[((0, 1), (2, 3), (5, 4), (6, 7))[c][half]].at[(b % 2) * 4 + a]

    @pl.when(i == 0)
    def _():
        for t in range(blocks):
            for j, ref in enumerate(weights):
                pltpu.make_async_copy(
                    ref.at[:, pl.ds(pl.multiple_of(t * 2 * kb + core * kb, kb), kb)],
                    wsc.at[pl.ds(j * n, n), pl.ds(t * kb, kb)],
                    wsem,
                ).start()
        for c in range(4):
            for b in range(4):
                for a in range(4):
                    slots = (a, b, c)
                    src = source(main, slots)
                    g, col = place(MAIN, slots)
                    pltpu.make_async_copy(
                        src, hid.at[g, pl.ds(0, MROWS), pl.ds(col, MCOLS)], sems.at[g]
                    ).start()
                    src = source(side, slots)
                    g, col = place(SIDE, slots)
                    pltpu.make_async_copy(
                        src.at[pl.ds(0, 256)], hid.at[g, :, pl.ds(col + MCOLS, 128)], sems.at[g]
                    ).start()
                    for j in range(3):
                        pltpu.make_async_copy(
                            src.at[pl.ds(256 + 32 * j, 32)],
                            hid.at[g, pl.ds(MROWS, 32), pl.ds(col + 128 * j, 128)],
                            sems.at[g],
                        ).start()
        pltpu.make_async_copy(wsc, wsc, wsem).wait()

    pltpu.make_async_copy(hid.at[i], hid.at[i], sems.at[i]).wait()
    block = hid[i]
    prod = lax.dot_general(wsc[...], block, (((1,), (1,)), ((), ())), preferred_element_type=F32)
    own_ref[...] = prod[:2 * n]
    par_ref[:2 * n, :] = prod[2 * n:].astype(BF)
    part = jnp.zeros((block.shape[0], 128), F32)
    for j in range(block.shape[1] // 128):
        wide = hid[i, :, j * 128:(j + 1) * 128].astype(F32)
        part = part + wide * wide
    sums = lax.dot_general(
        jnp.ones((8, 128), F32), part, (((1,), (1,)), ((), ())),
        preferred_element_type=F32, precision=lax.Precision.HIGHEST,
    )
    own_ss[...] = sums
    first = sums.astype(BF)
    par_ref[2 * n:, :] = jnp.concatenate(
        [first.astype(F32), sums - first.astype(F32)], axis=0
    ).astype(BF)


def gate_up(pos, main, side, weights):
    n, depth = weights[0].shape
    groups, piece, tokens = 8, 256, 2048
    any_spec = pl.BlockSpec(memory_space=pl.ANY)
    ospec = lambda r: pl.BlockSpec((r, piece), lambda i, pos: (0, i))
    return pl.pallas_call(
        gate_kernel,
        out_shape=[
            jax.ShapeDtypeStruct((2 * n, tokens), F32),
            jax.ShapeDtypeStruct((8, tokens), F32),
            jax.ShapeDtypeStruct((2 * n + 16, tokens), BF),
        ],
        grid_spec=pltpu.PrefetchScalarGridSpec(
            num_scalar_prefetch=1,
            grid=(groups,),
            in_specs=[any_spec] * 20,
            out_specs=[ospec(2 * n), ospec(8), ospec(2 * n + 16)],
            scratch_shapes=[
                pltpu.VMEM((groups, piece, depth // 2), BF),
                pltpu.VMEM((4 * n, depth // 2), BF),
                pltpu.SemaphoreType.DMA((groups,)),
                pltpu.SemaphoreType.DMA,
            ],
        ),
        compiler_params=pltpu.CompilerParams(
            vmem_limit_bytes=48 << 20, dimension_semantics=("arbitrary",)
        ),
        cost_estimate=pl.CostEstimate(
            flops=4 * n * tokens * depth, bytes_accessed=32 << 20, transcendentals=0
        ),
        name="gate_up",
    )(pos, *main, *side, *weights)


def finish_kernel(own_ref, ss_ref, got_ref, out_ref, *, depth):
    n = out_ref.shape[0]
    got = got_ref[...].astype(F32)
    total = ss_ref[:1] + got[2 * n:2 * n + 1] + got[2 * n + 8:2 * n + 9]
    scale = lax.rsqrt(total / depth + EPS)
    gate = (own_ref[:n] + got[:n]) * scale
    up = (own_ref[n:] + got[n:2 * n]) * scale
    out_ref[...] = (gate / (1.0 + jnp.exp(-gate)) * up).astype(BF)


def finish(own, ss, got, depth):
    rows, tokens = own.shape
    n = rows // 2
    piece = 512
    spec = lambda r: pl.BlockSpec((r, piece), lambda i: (0, i))
    return pl.pallas_call(
        functools.partial(finish_kernel, depth=depth),
        out_shape=jax.ShapeDtypeStruct((n, tokens), BF),
        grid=(tokens // piece,),
        in_specs=[spec(rows), spec(8), spec(rows + 16)],
        out_specs=spec(n),
        cost_estimate=pl.CostEstimate(flops=8 << 20, bytes_accessed=7 << 20, transcendentals=1 << 20),
        name="finish",
    )(own, ss, got)


def gather(blocks, orders):
    axes = [[(o[0][p], o[1][p]) for p in range(3)] for o in orders]
    near = lax.optimization_barrier(
        [[b] + [shift(b, a[0], by) for by in (1, -1, 2)] for b, a in zip(blocks, axes)]
    )
    cur = [jnp.stack(p) for p in near]
    near = lax.optimization_barrier(
        [[b] + [shift(b, a[1], by) for by in (1, -1, 2)] for b, a in zip(cur, axes)]
    )
    out = []
    lows = [jnp.concatenate(p[:2], 0) for p in near]
    highs = [jnp.concatenate(p[2:], 0) for p in near]
    lows, highs = lax.optimization_barrier((lows, highs))
    for low, high, a in zip(lows, highs, axes):
        c = a[2]
        l1 = shift(low, c, 1)
        r1 = shift(high, c, -1)
        l2 = shift(high, c, 1)
        r2 = shift(low, c, -1)
        o1 = shift(l1, c, 1)
        o2 = shift(r1, c, -1)
        out.append((low, high, l1, l2, r1, r2, o1, o2))
    return out


def per_device(queries, key_rows, value_rows, out_weight, residual, norm_gain, gate_weight, up_weight):
    y_at, xh, core = lax.axis_index("y"), lax.axis_index("xh"), lax.axis_index("c")
    z_at, xl = lax.axis_index("z"), lax.axis_index("xl")
    x_at = xh * 2 + xl
    group = y_at * 2 + xh

    pair = jnp.concatenate([key_rows, value_rows], axis=1)
    spread = jnp.broadcast_to(pair[None], (8,) + pair.shape)
    own = lax.all_to_all(spread, ("y", "xh"), 0, 0, tiled=True)
    oth = swap_core(own)

    pos = jnp.stack([group, core]).astype(jnp.int32)
    partial = attend_project(pos, queries, own, oth, out_weight, 8)
    partial, gate_raw, up_raw = lax.optimization_barrier((partial, gate_weight.T, up_weight.T))
    terms = lax.all_to_all(partial, HEAD, 0, 0, tiled=True)
    gain = norm_gain[None, :]
    gate_t = (gate_raw.astype(F32) * gain).astype(BF)
    up_t = (up_raw.astype(F32) * gain).astype(BF)
    terms, weights = lax.optimization_barrier(
        (terms, (gate_t, up_t, swap_core(gate_t), swap_core(up_t)))
    )
    hidden = (residual.astype(F32) + jnp.sum(terms.astype(F32), axis=0)).astype(BF)

    keep = jnp.where(core == 0, hidden[:, :512], hidden[:, 512:])
    got = swap_core(jnp.where(core == 0, hidden[:, 512:], hidden[:, :512]))
    chip = jnp.where(
        core == 0, jnp.concatenate([keep, got], 0), jnp.concatenate([got, keep], 0)
    )
    main_part = chip[:MROWS, :MCOLS]
    side_part = jnp.concatenate(
        [chip[:, MCOLS:]] + [chip[MROWS:, 128 * j:128 * (j + 1)] for j in range(3)], 0
    )
    main, side = gather((main_part, side_part), (MAIN, SIDE))
    pos2 = jnp.stack([x_at, y_at, z_at, core]).astype(jnp.int32)
    own_sums, own_ss, theirs = gate_up(pos2, main, side, weights)
    out = finish(own_sums, own_ss, swap_core(theirs), norm_gain.shape[0])
    return out.T, hidden


def solution(mesh):
    devices = mesh.devices.reshape(4, 2, 2, 4, 2)
    fine = Mesh(devices, MESH)
    both = P(SEQ, HEAD)
    cols = P(None, SEQ + HEAD)
    return jax.shard_map(
        per_device,
        mesh=fine,
        in_specs=(both, both, both, P(HEAD, None), both, P(), cols, cols),
        out_specs=(cols, both),
        check_vma=False,
    )
```

```python
import functools
import math

import jax
import jax.numpy as jnp
from jax import lax
from jax.experimental import pallas as pl
from jax.experimental.pallas import tpu as pltpu
from jax.sharding import Mesh, PartitionSpec as P


HD = 128
LOW = -1e30
EPS = 1e-5
SEQ = ("y", "xh", "c")
HEAD = ("z", "xl")
MESH = ("y", "xh", "c", "z", "xl")
MAIN = ("yzx", "zxy")
SIDE = ("xyz", "xyz")
OFFSETS = (0, -1, 1, 2)
MCOLS, SCOLS = 384, 128
BF = jnp.bfloat16
F32 = jnp.float32


def shift(x, axes, by):
    pairs = []
    for core in range(2):
        for n in range(64):
            at = {"x": n // 16, "y": n // 4 % 4, "z": n % 4}
            to = dict(at)
            to[axes[core]] = (to[axes[core]] + by) % 4
            pairs.append(tuple(
                (((p["y"] * 2 + p["x"] // 2) * 2 + core) * 4 + p["z"]) * 2 + p["x"] % 2
                for p in (at, to)
            ))
    return lax.ppermute(x, MESH, pairs)


def swap_core(x):
    return lax.ppermute(x, "c", [(0, 1), (1, 0)])


def attend_kernel(pos_ref, q_ref, own_ref, oth_ref, w_hbm, out_ref, w_buf, qs, acc, att, sems):
    blocks = w_buf.shape[0]
    width = w_buf.shape[2]
    for b in range(blocks):
        pltpu.make_async_copy(w_hbm.at[:, pl.ds(b * width, width)], w_buf.at[b], sems.at[b]).start()
    heads = q_ref.shape[1] // HD
    rows = q_ref.shape[0]
    cols = heads * rows
    for h in range(heads):
        qs[pl.ds(h * rows, rows), :] = q_ref[:, h * HD:(h + 1) * HD]
    group = pos_ref[0]
    core = pos_ref[1]
    factor = math.log2(math.e) / math.sqrt(HD)
    qv = qs[...]

    def scores(ref, g):
        return lax.dot_general(
            ref[g, :, :HD], qv, (((1,), (1,)), ((), ())), preferred_element_type=F32
        ) * factor

    def weigh(ref, g, p):
        return lax.dot_general(
            ref[g, :, HD:], p.astype(BF), (((0,), (0,)), ((), ())), preferred_element_type=F32
        )

    key_at = lax.broadcasted_iota(jnp.int32, (rows, cols), 0)
    row_at = lax.broadcasted_iota(jnp.int32, (rows, cols), 1) % rows
    s1 = jnp.where(key_at <= row_at, scores(own_ref, group), LOW)
    s2 = jnp.where(core == 1, scores(oth_ref, group), LOW)
    top = jnp.maximum(jnp.max(s1, axis=0, keepdims=True), jnp.max(s2, axis=0, keepdims=True))
    p1 = jnp.exp2(s1 - top)
    p2 = jnp.where(core == 1, jnp.exp2(s2 - top), 0.0)
    total = jnp.sum(p1, axis=0, keepdims=True) + jnp.sum(p2, axis=0, keepdims=True)
    acc[...] = weigh(own_ref, group, p1) + weigh(oth_ref, group, p2)

    def step(g, carry):
        top, total = carry
        s1 = scores(own_ref, g)
        s2 = scores(oth_ref, g)
        new = jnp.maximum(
            top, jnp.maximum(jnp.max(s1, axis=0, keepdims=True), jnp.max(s2, axis=0, keepdims=True))
        )
        alpha = jnp.exp2(top - new)
        p1 = jnp.exp2(s1 - new)
        p2 = jnp.exp2(s2 - new)
        total = total * alpha + jnp.sum(p1, axis=0, keepdims=True) + jnp.sum(p2, axis=0, keepdims=True)
        acc[...] = acc[...] * alpha + weigh(own_ref, g, p1) + weigh(oth_ref, g, p2)
        return new, total

    top, total = lax.fori_loop(0, group, step, (top, total))
    final = acc[...] / total
    for h in range(heads):
        att[:, h * HD:(h + 1) * HD] = final[:, h * rows:(h + 1) * rows].T.astype(BF)

    def project(b, _):
        pltpu.make_async_copy(w_hbm.at[:, pl.ds(0, width)], w_buf.at[b], sems.at[b]).wait()
        out_ref[b] = jnp.dot(att[...], w_buf[b], preferred_element_type=F32).astype(BF)
        return 0

    lax.fori_loop(0, blocks, project, 0)


def attend_project(pos, q, own, oth, w, blocks):
    rows, cols = q.shape
    depth, wide = w.shape
    width = wide // blocks
    vm = pl.BlockSpec(memory_space=pltpu.VMEM)
    return pl.pallas_call(
        attend_kernel,
        out_shape=jax.ShapeDtypeStruct((blocks, rows, width), BF),
        in_specs=[pl.BlockSpec(memory_space=pltpu.SMEM), vm, vm, vm, pl.BlockSpec(memory_space=pl.ANY)],
        out_specs=vm,
        scratch_shapes=[
            pltpu.VMEM((blocks, depth, width), BF),
            pltpu.VMEM((rows * cols // HD, HD), BF),
            pltpu.VMEM((HD, rows * cols // HD), F32),
            pltpu.VMEM((rows, cols), BF),
            pltpu.SemaphoreType.DMA((blocks,)),
        ],
        compiler_params=pltpu.CompilerParams(vmem_limit_bytes=48 << 20),
        cost_estimate=pl.CostEstimate(flops=4 << 30, bytes_accessed=20 << 20, transcendentals=2 << 20),
        name="attend_project",
    )(pos, q, own, oth, w)


def prep_kernel(pos_ref, g_ref, u_ref, gain_ref, km_ref, ks_ref, sm_ref, ss_ref):
    first = pos_ref[3] == 0
    n = g_ref.shape[0]
    gain = gain_ref[...]
    for j, ref in enumerate((g_ref, u_ref)):
        scaled = (ref[...].astype(F32) * gain).astype(BF)
        low, high = scaled[:, :512], scaled[:, 512:]
        keep = jnp.where(first, low, high)
        send = jnp.where(first, high, low)
        rows = pl.ds(j * n, n)
        km_ref[0, rows, :] = keep[:, :MCOLS]
        ks_ref[0, rows, :] = keep[:, MCOLS:]
        sm_ref[0, rows, :] = send[:, :MCOLS]
        ss_ref[0, rows, :] = send[:, MCOLS:]


def prepare(pos, gate_t, up_t, gain):
    n, depth = gate_t.shape
    wspec = pl.BlockSpec((n, 1024), lambda i, pos: (0, i))
    mspec = pl.BlockSpec((1, 2 * n, MCOLS), lambda i, pos: (i % 2, 0, i // 2))
    sspec = pl.BlockSpec((1, 2 * n, SCOLS), lambda i, pos: (i // 2, 0, i % 2))
    mshape = jax.ShapeDtypeStruct((2, 2 * n, 4 * MCOLS), BF)
    sshape = jax.ShapeDtypeStruct((4, 2 * n, 2 * SCOLS), BF)
    return pl.pallas_call(
        prep_kernel,
        out_shape=[mshape, sshape, mshape, sshape],
        grid_spec=pltpu.PrefetchScalarGridSpec(
            num_scalar_prefetch=1,
            grid=(depth // 1024,),
            in_specs=[wspec, wspec, pl.BlockSpec((1, 1024), lambda i, pos: (0, i))],
            out_specs=[mspec, sspec, mspec, sspec],
        ),
        compiler_params=pltpu.CompilerParams(vmem_limit_bytes=16 << 20),
        cost_estimate=pl.CostEstimate(flops=8 << 20, bytes_accessed=15 << 20, transcendentals=0),
        name="prepare",
    )(pos, gate_t, up_t, gain)


def gate_kernel(which, first, last, pos_ref, *refs):
    count = len(which)
    refs = list(refs)
    main = {c: (refs.pop(0), refs.pop(0)) for c in which}
    side = {c: (refs.pop(0), refs.pop(0)) for c in which}
    km, ks, gm, gs = (refs.pop(0) for _ in range(4))
    before = None if first else refs.pop(0)
    if last:
        own_ref, own_ss, par_ref = (refs.pop(0) for _ in range(3))
    else:
        after = refs.pop(0)
    acc, wm, ws, hm, hs, table, wsem, asem, msem, ssem, osem = refs
    x_at, y_at, z_at, core = (pos_ref[m] for m in range(4))
    n2 = km.shape[1]
    rows = 2 * n2

    def at(base, slot):
        return (base + OFFSETS[slot] + 4) & 3

    if not first:
        pltpu.make_async_copy(before, acc, asem).start()
    for src, dst, half, sem in ((km, wm, 0, 0), (gm, wm, 1, 0), (ks, ws, 0, 1), (gs, ws, 1, 1)):
        pltpu.make_async_copy(src, dst.at[:, pl.ds(half * n2, n2), :], wsem.at[sem]).start()

    def fetch(u, c, j, on):
        for k in range(4):
            a, b = (j, k) if on == 0 else (k, j)
            col = pl.multiple_of(at(z_at, k) * MCOLS, MCOLS)
            pltpu.make_async_copy(
                main[c][b // 2].at[(b % 2) * 4 + a], hm.at[u, :, pl.ds(col, MCOLS)], msem.at[u]
            ).start()

    for m, c in enumerate(which):
        for j in range(4):
            u = m * 4 + j
            x = jnp.where(core == 0, at(x_at, c), at(x_at, j))
            y = jnp.where(core == 0, at(y_at, j), at(y_at, c))
            table[2 * u] = y * 2 + x // 2
            table[2 * u + 1] = x & 1
            pl.when(core == 0)(functools.partial(fetch, u, c, j, 0))
            pl.when(core != 0)(functools.partial(fetch, u, c, j, 1))
    for m, c in enumerate(which):
        for b in range(4):
            for a in range(4):
                x = at(x_at, a)
                row = pl.multiple_of((at(y_at, b) * 2 + x // 2) * 256, 256)
                col = pl.multiple_of((x & 1) * SCOLS, SCOLS)
                pltpu.make_async_copy(
                    side[c][b // 2].at[(b % 2) * 4 + a],
                    hs.at[m, pl.ds(row, 256), pl.ds(col, SCOLS)],
                    ssem.at[m],
                ).start()
    if first:
        acc[...] = jnp.zeros_like(acc)
    else:
        pltpu.make_async_copy(before, acc, asem).wait()
    ones = jnp.ones((8, 128), F32)

    def squares(block):
        part = jnp.zeros((block.shape[0], 128), F32)
        for j in range(block.shape[1] // 128):
            wide = block[:, j * 128:(j + 1) * 128].astype(F32)
            part = part + wide * wide
        return lax.dot_general(
            ones, part, (((1,), (1,)), ((), ())),
            preferred_element_type=F32, precision=lax.Precision.HIGHEST,
        )

    def unit(u, _):
        pltpu.make_async_copy(hm.at[u], hm.at[u], msem.at[u]).wait()
        cols = pl.ds(pl.multiple_of(table[2 * u] * 256, 256), 256)
        block = hm[u]
        acc[:rows, cols] += lax.dot_general(
            wm[table[2 * u + 1]], block, (((1,), (1,)), ((), ())), preferred_element_type=F32
        )
        acc[rows:, cols] += squares(block)
        return 0

    pltpu.make_async_copy(wm, wm, wsem.at[0]).wait()
    lax.fori_loop(0, 4 * count, unit, 0)
    pltpu.make_async_copy(ws, ws, wsem.at[1]).wait()
    for m in range(count):
        pltpu.make_async_copy(hs.at[m], hs.at[m], ssem.at[m]).wait()
    piece = 512

    def tail(p, _):
        cols = pl.ds(pl.multiple_of(p * piece, piece), piece)
        total = acc[:rows, cols]
        sq = acc[rows:, cols]
        for m, c in enumerate(which):
            block = hs[m, cols, :]
            total = total + lax.dot_general(
                ws[at(z_at, c)], block, (((1,), (1,)), ((), ())), preferred_element_type=F32
            )
            sq = sq + squares(block)
        if last:
            own_ref[:, cols] = total[:n2]
            par_ref[:n2, cols] = total[n2:].astype(BF)
            own_ss[:, cols] = sq
            big = sq.astype(BF)
            par_ref[n2:, cols] = jnp.concatenate(
                [big.astype(F32), sq - big.astype(F32)], axis=0
            ).astype(BF)
        else:
            acc[:rows, cols] = total
            acc[rows:, cols] = sq
            pltpu.make_async_copy(acc.at[:, cols], after.at[:, cols], osem).start()
        return 0

    lax.fori_loop(0, acc.shape[1] // piece, tail, 0)
    if not last:
        pltpu.make_async_copy(acc, after, osem).wait()


def gate_up(pos, which, main, side, weights, before, last):
    n2 = weights[0].shape[1]
    tokens = 2048
    count = len(which)
    first = before is None
    any_spec = pl.BlockSpec(memory_space=pl.ANY)
    vm = pl.BlockSpec(memory_space=pltpu.VMEM)
    pieces = [p for part in (main, side) for c in which for p in part[c]]
    operands = pieces + list(weights) + ([] if first else [before])
    partial = jax.ShapeDtypeStruct((2 * n2 + 8, tokens), F32)
    out_shape = [
        jax.ShapeDtypeStruct((n2, tokens), F32),
        jax.ShapeDtypeStruct((8, tokens), F32),
        jax.ShapeDtypeStruct((n2 + 16, tokens), BF),
    ] if last else partial
    return pl.pallas_call(
        functools.partial(gate_kernel, which, first, last),
        out_shape=out_shape,
        in_specs=[pl.BlockSpec(memory_space=pltpu.SMEM)] + [any_spec] * len(operands),
        out_specs=[vm] * 3 if last else any_spec,
        scratch_shapes=[
            pltpu.VMEM(partial.shape, F32),
            pltpu.VMEM((2, 2 * n2, 4 * MCOLS), BF),
            pltpu.VMEM((4, 2 * n2, 2 * SCOLS), BF),
            pltpu.VMEM((4 * count, 256, 4 * MCOLS), BF),
            pltpu.VMEM((count, tokens, 2 * SCOLS), BF),
            pltpu.SMEM((8 * count,), jnp.int32),
            pltpu.SemaphoreType.DMA((2,)),
            pltpu.SemaphoreType.DMA,
            pltpu.SemaphoreType.DMA((4 * count,)),
            pltpu.SemaphoreType.DMA((count,)),
            pltpu.SemaphoreType.DMA,
        ],
        compiler_params=pltpu.CompilerParams(vmem_limit_bytes=48 << 20),
        cost_estimate=pl.CostEstimate(
            flops=count * n2 * tokens * 4096, bytes_accessed=20 << 20, transcendentals=0
        ),
        name="gate_up",
    )(pos, *operands)


def finish_kernel(own_ref, ss_ref, got_ref, out_ref, *, depth):
    n = out_ref.shape[0]
    got = got_ref[...].astype(F32)
    total = ss_ref[:1] + got[2 * n:2 * n + 1] + got[2 * n + 8:2 * n + 9]
    scale = lax.rsqrt(total / depth + EPS)
    gate = (own_ref[:n] + got[:n]) * scale
    up = (own_ref[n:] + got[n:2 * n]) * scale
    out_ref[...] = (gate / (1.0 + jnp.exp(-gate)) * up).astype(BF)


def finish(own, ss, got, depth):
    rows, tokens = own.shape
    n = rows // 2
    piece = 512
    spec = lambda r: pl.BlockSpec((r, piece), lambda i: (0, i))
    return pl.pallas_call(
        functools.partial(finish_kernel, depth=depth),
        out_shape=jax.ShapeDtypeStruct((n, tokens), BF),
        grid=(tokens // piece,),
        in_specs=[spec(rows), spec(8), spec(rows + 16)],
        out_specs=spec(n),
        cost_estimate=pl.CostEstimate(flops=8 << 20, bytes_accessed=7 << 20, transcendentals=1 << 20),
        name="finish",
    )(own, ss, got)


def gather(blocks, orders):
    axes = [[(o[0][p], o[1][p]) for p in range(3)] for o in orders]
    near = lax.optimization_barrier(
        [[b] + [shift(b, a[0], by) for by in (1, -1, 2)] for b, a in zip(blocks, axes)]
    )
    cur = [jnp.stack(p) for p in near]
    near = lax.optimization_barrier(
        [[b] + [shift(b, a[1], by) for by in (1, -1, 2)] for b, a in zip(cur, axes)]
    )
    lows = [jnp.concatenate(p[:2], 0) for p in near]
    highs = [jnp.concatenate(p[2:], 0) for p in near]
    lows, highs = lax.optimization_barrier((lows, highs))
    near = [
        (shift(low, a[2], 1), shift(high, a[2], 1), shift(low, a[2], -1), shift(high, a[2], -1))
        for low, high, a in zip(lows, highs, axes)
    ]
    far = [(shift(t[0], a[2], 1), shift(t[3], a[2], -1)) for t, a in zip(near, axes)]
    return [
        {0: own, 1: t[:2], 2: t[2:], 3: o} for own, t, o in zip(zip(lows, highs), near, far)
    ]


def per_device(queries, key_rows, value_rows, out_weight, residual, norm_gain, gate_weight, up_weight):
    y_at, xh, core = lax.axis_index("y"), lax.axis_index("xh"), lax.axis_index("c")
    z_at, xl = lax.axis_index("z"), lax.axis_index("xl")
    x_at = xh * 2 + xl
    group = y_at * 2 + xh

    pair = jnp.concatenate([key_rows, value_rows], axis=1)
    spread = jnp.broadcast_to(pair[None], (8,) + pair.shape)
    own = lax.all_to_all(spread, ("y", "xh"), 0, 0, tiled=True)
    oth = swap_core(own)

    pos = jnp.stack([group, core]).astype(jnp.int32)
    partial = attend_project(pos, queries, own, oth, out_weight, 8)
    pos2 = jnp.stack([x_at, y_at, z_at, core]).astype(jnp.int32)
    partial, gate_raw, up_raw = lax.optimization_barrier((partial, gate_weight.T, up_weight.T))
    terms = lax.all_to_all(partial, HEAD, 0, 0, tiled=True)
    km, ks, sm, ss = prepare(pos2, gate_raw, up_raw, norm_gain[None, :])
    terms, weights = lax.optimization_barrier((terms, (km, ks, swap_core(sm), swap_core(ss))))
    hidden = (residual.astype(F32) + jnp.sum(terms.astype(F32), axis=0)).astype(BF)

    keep = jnp.where(core == 0, hidden[:, :512], hidden[:, 512:])
    got = swap_core(jnp.where(core == 0, hidden[:, 512:], hidden[:, :512]))
    chip = jnp.where(core == 0, jnp.concatenate([keep, got], 0), jnp.concatenate([got, keep], 0))
    main, side = gather((chip[:, :MCOLS], chip[:, MCOLS:]), (MAIN, SIDE))
    sums = gate_up(pos2, (0,), main, side, weights, None, False)
    sums = gate_up(pos2, (1, 2), main, side, weights, sums, False)
    own_sums, own_ss, theirs = gate_up(pos2, (3,), main, side, weights, sums, True)
    out = finish(own_sums, own_ss, swap_core(theirs), norm_gain.shape[0])
    return out.T, hidden


def solution(mesh):
    devices = mesh.devices.reshape(4, 2, 2, 4, 2)
    fine = Mesh(devices, MESH)
    both = P(SEQ, HEAD)
    cols = P(None, SEQ + HEAD)
    return jax.shard_map(
        per_device,
        mesh=fine,
        in_specs=(both, both, both, P(HEAD, None), both, P(), cols, cols),
        out_specs=(cols, both),
        check_vma=False,
    )
```

```python
import functools
import math

import jax
import jax.numpy as jnp
from jax import lax
from jax.experimental import pallas as pl
from jax.experimental.pallas import tpu as pltpu
from jax.sharding import Mesh, PartitionSpec as P


HD = 128
LOW = -1e30
EPS = 1e-5
SEQ = ("y", "xh", "c")
HEAD = ("z", "xl")
MESH = ("y", "xh", "c", "z", "xl")
MAIN = ("yzx", "zxy")
SIDE = ("xyz", "xyz")
OFFSETS = (0, -1, 1, 2)
MCOLS, SCOLS = 384, 128
BF = jnp.bfloat16
F32 = jnp.float32


def shift(x, axes, by):
    pairs = []
    for core in range(2):
        for n in range(64):
            at = {"x": n // 16, "y": n // 4 % 4, "z": n % 4}
            to = dict(at)
            to[axes[core]] = (to[axes[core]] + by) % 4
            pairs.append(tuple(
                (((p["y"] * 2 + p["x"] // 2) * 2 + core) * 4 + p["z"]) * 2 + p["x"] % 2
                for p in (at, to)
            ))
    return lax.ppermute(x, MESH, pairs)


def swap_core(x):
    return lax.ppermute(x, "c", [(0, 1), (1, 0)])


def attend_kernel(pos_ref, q_ref, own_ref, oth_ref, w_hbm, out_ref, w_buf, qs, acc, att, sems):
    blocks = w_buf.shape[0]
    width = w_buf.shape[2]
    for b in range(blocks):
        pltpu.make_async_copy(w_hbm.at[:, pl.ds(b * width, width)], w_buf.at[b], sems.at[b]).start()
    heads = q_ref.shape[1] // HD
    rows = q_ref.shape[0]
    cols = heads * rows
    for h in range(heads):
        qs[pl.ds(h * rows, rows), :] = q_ref[:, h * HD:(h + 1) * HD]
    group = pos_ref[0]
    core = pos_ref[1]
    factor = math.log2(math.e) / math.sqrt(HD)
    qv = qs[...]

    def scores(ref, g):
        return lax.dot_general(
            ref[g, :, :HD], qv, (((1,), (1,)), ((), ())), preferred_element_type=F32
        ) * factor

    def weigh(ref, g, p):
        return lax.dot_general(
            ref[g, :, HD:], p.astype(BF), (((0,), (0,)), ((), ())), preferred_element_type=F32
        )

    key_at = lax.broadcasted_iota(jnp.int32, (rows, cols), 0)
    row_at = lax.broadcasted_iota(jnp.int32, (rows, cols), 1) % rows
    s1 = jnp.where(key_at <= row_at, scores(own_ref, group), LOW)
    s2 = jnp.where(core == 1, scores(oth_ref, group), LOW)
    top = jnp.maximum(jnp.max(s1, axis=0, keepdims=True), jnp.max(s2, axis=0, keepdims=True))
    p1 = jnp.exp2(s1 - top)
    p2 = jnp.where(core == 1, jnp.exp2(s2 - top), 0.0)
    total = jnp.sum(p1, axis=0, keepdims=True) + jnp.sum(p2, axis=0, keepdims=True)
    acc[...] = weigh(own_ref, group, p1) + weigh(oth_ref, group, p2)

    def step(g, carry):
        top, total = carry
        s1 = scores(own_ref, g)
        s2 = scores(oth_ref, g)
        new = jnp.maximum(
            top, jnp.maximum(jnp.max(s1, axis=0, keepdims=True), jnp.max(s2, axis=0, keepdims=True))
        )
        alpha = jnp.exp2(top - new)
        p1 = jnp.exp2(s1 - new)
        p2 = jnp.exp2(s2 - new)
        total = total * alpha + jnp.sum(p1, axis=0, keepdims=True) + jnp.sum(p2, axis=0, keepdims=True)
        acc[...] = acc[...] * alpha + weigh(own_ref, g, p1) + weigh(oth_ref, g, p2)
        return new, total

    top, total = lax.fori_loop(0, group, step, (top, total))
    final = acc[...] / total
    for h in range(heads):
        att[:, h * HD:(h + 1) * HD] = final[:, h * rows:(h + 1) * rows].T.astype(BF)

    def project(b, _):
        pltpu.make_async_copy(w_hbm.at[:, pl.ds(0, width)], w_buf.at[b], sems.at[b]).wait()
        out_ref[b] = jnp.dot(att[...], w_buf[b], preferred_element_type=F32).astype(BF)
        return 0

    lax.fori_loop(0, blocks, project, 0)


def attend_project(pos, q, own, oth, w, blocks):
    rows, cols = q.shape
    depth, wide = w.shape
    width = wide // blocks
    vm = pl.BlockSpec(memory_space=pltpu.VMEM)
    return pl.pallas_call(
        attend_kernel,
        out_shape=jax.ShapeDtypeStruct((blocks, rows, width), BF),
        in_specs=[pl.BlockSpec(memory_space=pltpu.SMEM), vm, vm, vm, pl.BlockSpec(memory_space=pl.ANY)],
        out_specs=vm,
        scratch_shapes=[
            pltpu.VMEM((blocks, depth, width), BF),
            pltpu.VMEM((rows * cols // HD, HD), BF),
            pltpu.VMEM((HD, rows * cols // HD), F32),
            pltpu.VMEM((rows, cols), BF),
            pltpu.SemaphoreType.DMA((blocks,)),
        ],
        compiler_params=pltpu.CompilerParams(vmem_limit_bytes=48 << 20),
        cost_estimate=pl.CostEstimate(flops=4 << 30, bytes_accessed=20 << 20, transcendentals=2 << 20),
        name="attend_project",
    )(pos, q, own, oth, w)


def prep_kernel(pos_ref, g_ref, u_ref, gain_ref, km_ref, ks_ref, sm_ref, ss_ref):
    first = pos_ref[3] == 0
    n = g_ref.shape[0]
    gain = gain_ref[...]
    for j, ref in enumerate((g_ref, u_ref)):
        scaled = (ref[...].astype(F32) * gain).astype(BF)
        low, high = scaled[:, :512], scaled[:, 512:]
        keep = jnp.where(first, low, high)
        send = jnp.where(first, high, low)
        rows = pl.ds(j * n, n)
        km_ref[0, rows, :] = keep[:, :MCOLS]
        ks_ref[0, rows, :] = keep[:, MCOLS:]
        sm_ref[0, rows, :] = send[:, :MCOLS]
        ss_ref[0, rows, :] = send[:, MCOLS:]


def prepare(pos, gate_t, up_t, gain):
    n, depth = gate_t.shape
    wspec = pl.BlockSpec((n, 1024), lambda i, pos: (0, i))
    mspec = pl.BlockSpec((1, 2 * n, MCOLS), lambda i, pos: (i % 2, 0, i // 2))
    sspec = pl.BlockSpec((1, 2 * n, SCOLS), lambda i, pos: (i // 2, 0, i % 2))
    mshape = jax.ShapeDtypeStruct((2, 2 * n, 4 * MCOLS), BF)
    sshape = jax.ShapeDtypeStruct((4, 2 * n, 2 * SCOLS), BF)
    return pl.pallas_call(
        prep_kernel,
        out_shape=[mshape, sshape, mshape, sshape],
        grid_spec=pltpu.PrefetchScalarGridSpec(
            num_scalar_prefetch=1,
            grid=(depth // 1024,),
            in_specs=[wspec, wspec, pl.BlockSpec((1, 1024), lambda i, pos: (0, i))],
            out_specs=[mspec, sspec, mspec, sspec],
        ),
        compiler_params=pltpu.CompilerParams(vmem_limit_bytes=16 << 20),
        cost_estimate=pl.CostEstimate(flops=8 << 20, bytes_accessed=15 << 20, transcendentals=0),
        name="prepare",
    )(pos, gate_t, up_t, gain)


def gate_kernel(which, first, last, pos_ref, *refs):
    count = len(which)
    refs = list(refs)
    main = {c: (refs.pop(0), refs.pop(0)) for c in which}
    side = {c: (refs.pop(0), refs.pop(0)) for c in which}
    wm, ws = refs.pop(0), refs.pop(0)
    before = None if first else refs.pop(0)
    if last:
        own_ref, own_ss, par_ref = (refs.pop(0) for _ in range(3))
        acc = before
    else:
        acc = refs.pop(0)
    hm, hs, ssq, table, msem, ssem = refs
    x_at, y_at, z_at, core = (pos_ref[m] for m in range(4))
    rows = wm.shape[1]
    n2 = rows // 2

    def at(base, slot):
        return (base + OFFSETS[slot] + 4) & 3

    def fetch(u, c, j, on):
        for k in range(4):
            a, b = (j, k) if on == 0 else (k, j)
            col = pl.multiple_of(at(z_at, k) * MCOLS, MCOLS)
            pltpu.make_async_copy(
                main[c][b // 2].at[(b % 2) * 4 + a], hm.at[u, :, pl.ds(col, MCOLS)], msem.at[u]
            ).start()

    for m, c in enumerate(which):
        for j in range(4):
            u = m * 4 + j
            x = jnp.where(core == 0, at(x_at, c), at(x_at, j))
            y = jnp.where(core == 0, at(y_at, j), at(y_at, c))
            table[2 * u] = y * 2 + x // 2
            table[2 * u + 1] = x & 1
            pl.when(core == 0)(functools.partial(fetch, u, c, j, 0))
            pl.when(core != 0)(functools.partial(fetch, u, c, j, 1))
    for m, c in enumerate(which):
        for b in range(4):
            for a in range(4):
                x = at(x_at, a)
                row = pl.multiple_of((at(y_at, b) * 2 + x // 2) * 256, 256)
                col = pl.multiple_of((x & 1) * SCOLS, SCOLS)
                pltpu.make_async_copy(
                    side[c][b // 2].at[(b % 2) * 4 + a],
                    hs.at[m, pl.ds(row, 256), pl.ds(col, SCOLS)],
                    ssem.at[m],
                ).start()
    if first:
        acc[...] = jnp.zeros_like(acc)
    ssq[...] = jnp.zeros_like(ssq)
    ones = jnp.ones((8, 128), BF)

    def squares(block):
        part = jnp.zeros((block.shape[0], 128), F32)
        for j in range(block.shape[1] // 128):
            wide = block[:, j * 128:(j + 1) * 128].astype(F32)
            part = part + wide * wide
        return part

    def lane_sums(part):
        big = part.astype(BF)
        small = (part - big.astype(F32)).astype(BF)
        return sum(
            lax.dot_general(ones, t, (((1,), (1,)), ((), ())), preferred_element_type=F32)
            for t in (big, small)
        )

    def unit(u, _):
        pltpu.make_async_copy(hm.at[u], hm.at[u], msem.at[u]).wait()
        cols = pl.ds(pl.multiple_of(table[2 * u] * 256, 256), 256)
        block = hm[u]
        acc[:rows, cols] += lax.dot_general(
            wm[table[2 * u + 1]], block, (((1,), (1,)), ((), ())), preferred_element_type=F32
        )
        ssq[cols, :] += squares(block)
        return 0

    lax.fori_loop(0, 4 * count, unit, 0)
    for m in range(count):
        pltpu.make_async_copy(hs.at[m], hs.at[m], ssem.at[m]).wait()
    piece = 512

    def tail(p, _):
        cols = pl.ds(pl.multiple_of(p * piece, piece), piece)
        total = acc[:rows, cols]
        part = ssq[cols, :]
        for m, c in enumerate(which):
            block = hs[m, cols, :]
            total = total + lax.dot_general(
                ws[at(z_at, c)], block, (((1,), (1,)), ((), ())), preferred_element_type=F32
            )
            part = part + squares(block)
        sq = acc[rows:, cols] + lane_sums(part)
        if last:
            own_ref[:, cols] = total[:n2]
            par_ref[:n2, cols] = total[n2:].astype(BF)
            own_ss[:, cols] = sq
            big = sq.astype(BF)
            par_ref[n2:, cols] = jnp.concatenate(
                [big.astype(F32), sq - big.astype(F32)], axis=0
            ).astype(BF)
        else:
            acc[:rows, cols] = total
            acc[rows:, cols] = sq
        return 0

    lax.fori_loop(0, acc.shape[1] // piece, tail, 0)


def gate_up(pos, which, main, side, weights, before, last):
    n2 = weights[0].shape[1] // 2
    tokens = 2048
    count = len(which)
    first = before is None
    any_spec = pl.BlockSpec(memory_space=pl.ANY)
    vm = pl.BlockSpec(memory_space=pltpu.VMEM)
    pieces = [p for part in (main, side) for c in which for p in part[c]]
    operands = pieces + list(weights) + ([] if first else [before])
    partial = jax.ShapeDtypeStruct((2 * n2 + 8, tokens), F32)
    out_shape = [
        jax.ShapeDtypeStruct((n2, tokens), F32),
        jax.ShapeDtypeStruct((8, tokens), F32),
        jax.ShapeDtypeStruct((n2 + 16, tokens), BF),
    ] if last else partial
    return pl.pallas_call(
        functools.partial(gate_kernel, which, first, last),
        out_shape=out_shape,
        in_specs=[pl.BlockSpec(memory_space=pltpu.SMEM)]
        + [any_spec] * len(pieces)
        + [vm] * (len(operands) - len(pieces)),
        out_specs=[vm] * 3 if last else vm,
        scratch_shapes=[
            pltpu.VMEM((4 * count, 256, 4 * MCOLS), BF),
            pltpu.VMEM((count, tokens, 2 * SCOLS), BF),
            pltpu.VMEM((tokens, 128), F32),
            pltpu.SMEM((8 * count,), jnp.int32),
            pltpu.SemaphoreType.DMA((4 * count,)),
            pltpu.SemaphoreType.DMA((count,)),
        ],
        input_output_aliases={} if first or last else {len(operands): 0},
        compiler_params=pltpu.CompilerParams(vmem_limit_bytes=(10 + 8 * count) << 20),
        cost_estimate=pl.CostEstimate(
            flops=count * n2 * tokens * 4096, bytes_accessed=20 << 20, transcendentals=0
        ),
        name="gate_up",
    )(pos, *operands)


def finish_kernel(own_ref, ss_ref, got_ref, out_ref, buf, sems, *, depth):
    n = buf.shape[0]
    piece = 512

    def put(p):
        cols = pl.ds(p * piece, piece)
        return pltpu.make_async_copy(buf.at[:, cols], out_ref.at[:, cols], sems.at[p])

    for p in range(buf.shape[1] // piece):
        cols = pl.ds(p * piece, piece)
        got = got_ref[:, cols].astype(F32)
        total = ss_ref[:1, cols] + got[2 * n:2 * n + 1] + got[2 * n + 8:2 * n + 9]
        scale = lax.rsqrt(total / depth + EPS)
        gate = (own_ref[:n, cols] + got[:n]) * scale
        up = (own_ref[n:, cols] + got[n:2 * n]) * scale
        buf[:, cols] = (gate / (1.0 + jnp.exp(-gate)) * up).astype(BF)
        put(p).start()
    for p in range(buf.shape[1] // piece):
        put(p).wait()


def finish(own, ss, got, depth):
    rows, tokens = own.shape
    n = rows // 2
    vm = pl.BlockSpec(memory_space=pltpu.VMEM)
    return pl.pallas_call(
        functools.partial(finish_kernel, depth=depth),
        out_shape=jax.ShapeDtypeStruct((n, tokens), BF),
        in_specs=[vm] * 3,
        out_specs=pl.BlockSpec(memory_space=pl.ANY),
        scratch_shapes=[pltpu.VMEM((n, tokens), BF), pltpu.SemaphoreType.DMA((tokens // 512,))],
        compiler_params=pltpu.CompilerParams(vmem_limit_bytes=16 << 20),
        cost_estimate=pl.CostEstimate(flops=8 << 20, bytes_accessed=7 << 20, transcendentals=1 << 20),
        name="finish",
    )(own, ss, got)


def gather(blocks, orders):
    axes = [[(o[0][p], o[1][p]) for p in range(3)] for o in orders]
    near = lax.optimization_barrier(
        [[b] + [shift(b, a[0], by) for by in (1, -1, 2)] for b, a in zip(blocks, axes)]
    )
    cur = lax.optimization_barrier([jnp.stack(p) for p in near])
    ahead = [shift(b, a[1], 1) for b, a in zip(cur, axes)]
    rest = [[shift(b, a[1], by) for by in (-1, 2)] for b, a in zip(cur, axes)]
    lows = [jnp.concatenate([b, n], 0) for b, n in zip(cur, ahead)]
    lows = lax.optimization_barrier(lows)
    low_near = [(shift(b, a[2], 1), shift(b, a[2], -1)) for b, a in zip(lows, axes)]
    highs = [jnp.concatenate(p, 0) for p in rest]
    highs = lax.optimization_barrier(highs)
    high_near = [(shift(b, a[2], 1), shift(b, a[2], -1)) for b, a in zip(highs, axes)]
    near = [(l[0], h[0], l[1], h[1]) for l, h in zip(low_near, high_near)]
    far = [(shift(t[0], a[2], 1), shift(t[3], a[2], -1)) for t, a in zip(near, axes)]
    return [
        {0: own, 1: t[:2], 2: t[2:], 3: o} for own, t, o in zip(zip(lows, highs), near, far)
    ]


def per_device(queries, key_rows, value_rows, out_weight, residual, norm_gain, gate_weight, up_weight):
    y_at, xh, core = lax.axis_index("y"), lax.axis_index("xh"), lax.axis_index("c")
    z_at, xl = lax.axis_index("z"), lax.axis_index("xl")
    x_at = xh * 2 + xl
    group = y_at * 2 + xh

    pair = jnp.concatenate([key_rows, value_rows], axis=1)
    spread = jnp.broadcast_to(pair[None], (8,) + pair.shape)
    own = lax.all_to_all(spread, ("y", "xh"), 0, 0, tiled=True)
    oth = swap_core(own)

    pos = jnp.stack([group, core]).astype(jnp.int32)
    partial = attend_project(pos, queries, own, oth, out_weight, 8)
    pos2 = jnp.stack([x_at, y_at, z_at, core]).astype(jnp.int32)
    partial, gate_raw, up_raw = lax.optimization_barrier((partial, gate_weight.T, up_weight.T))
    terms = lax.all_to_all(partial, HEAD, 0, 0, tiled=True)
    km, ks, sm, ss = prepare(pos2, gate_raw, up_raw, norm_gain[None, :])
    weights = [jnp.concatenate([k, swap_core(t)], 1) for k, t in ((km, sm), (ks, ss))]
    terms, weights = lax.optimization_barrier((terms, weights))
    hidden = (residual.astype(F32) + jnp.sum(terms.astype(F32), axis=0)).astype(BF)

    keep = jnp.where(core == 0, hidden[:, :512], hidden[:, 512:])
    got = swap_core(jnp.where(core == 0, hidden[:, 512:], hidden[:, :512]))
    chip = jnp.where(core == 0, jnp.concatenate([keep, got], 0), jnp.concatenate([got, keep], 0))
    main, side = gather((chip[:, :MCOLS], chip[:, MCOLS:]), (MAIN, SIDE))
    sums = gate_up(pos2, (0,), main, side, weights, None, False)
    sums = gate_up(pos2, (1, 2), main, side, weights, sums, False)
    own_sums, own_ss, theirs = gate_up(pos2, (3,), main, side, weights, sums, True)
    out = finish(own_sums, own_ss, swap_core(theirs), norm_gain.shape[0])
    return out.T, hidden


def solution(mesh):
    devices = mesh.devices.reshape(4, 2, 2, 4, 2)
    fine = Mesh(devices, MESH)
    both = P(SEQ, HEAD)
    cols = P(None, SEQ + HEAD)
    return jax.shard_map(
        per_device,
        mesh=fine,
        in_specs=(both, both, both, P(HEAD, None), both, P(), cols, cols),
        out_specs=(cols, both),
        check_vma=False,
    )
```

```python
import functools
import math

import jax
import jax.numpy as jnp
from jax import lax
from jax.experimental import pallas as pl
from jax.experimental.pallas import tpu as pltpu
from jax.sharding import Mesh, PartitionSpec as P


HD = 128
LOW = -1e30
EPS = 1e-5
SEQ = ("y", "xh", "c")
HEAD = ("z", "xl")
MESH = ("y", "xh", "c", "z", "xl")
MAIN = ("yzx", "zxy")
SIDE = ("xyz", "xyz")
OFFSETS = (0, -1, 1, 2)
MCOLS, SCOLS = 384, 128
BF = jnp.bfloat16
F32 = jnp.float32


def shift(x, axes, by):
    pairs = []
    for core in range(2):
        for n in range(64):
            at = {"x": n // 16, "y": n // 4 % 4, "z": n % 4}
            to = dict(at)
            to[axes[core]] = (to[axes[core]] + by) % 4
            pairs.append(tuple(
                (((p["y"] * 2 + p["x"] // 2) * 2 + core) * 4 + p["z"]) * 2 + p["x"] % 2
                for p in (at, to)
            ))
    return lax.ppermute(x, MESH, pairs)


def swap_core(x):
    return lax.ppermute(x, "c", [(0, 1), (1, 0)])


def attend_kernel(pos_ref, q_ref, own_ref, oth_ref, w_hbm, out_ref, w_buf, qs, acc, att, sems):
    blocks = w_buf.shape[0]
    width = w_buf.shape[2]
    for b in range(blocks):
        pltpu.make_async_copy(w_hbm.at[:, pl.ds(b * width, width)], w_buf.at[b], sems.at[b]).start()
    heads = q_ref.shape[1] // HD
    rows = q_ref.shape[0]
    cols = heads * rows
    for h in range(heads):
        qs[pl.ds(h * rows, rows), :] = q_ref[:, h * HD:(h + 1) * HD]
    group = pos_ref[0]
    core = pos_ref[1]
    factor = math.log2(math.e) / math.sqrt(HD)
    qv = qs[...]

    def scores(ref, g):
        return lax.dot_general(
            ref[g, :, :HD], qv, (((1,), (1,)), ((), ())), preferred_element_type=F32
        ) * factor

    def weigh(ref, g, p):
        return lax.dot_general(
            ref[g, :, HD:], p.astype(BF), (((0,), (0,)), ((), ())), preferred_element_type=F32
        )

    key_at = lax.broadcasted_iota(jnp.int32, (rows, cols), 0)
    row_at = lax.broadcasted_iota(jnp.int32, (rows, cols), 1) % rows
    s1 = jnp.where(key_at <= row_at, scores(own_ref, group), LOW)
    s2 = jnp.where(core == 1, scores(oth_ref, group), LOW)
    top = jnp.maximum(jnp.max(s1, axis=0, keepdims=True), jnp.max(s2, axis=0, keepdims=True))
    p1 = jnp.exp2(s1 - top)
    p2 = jnp.where(core == 1, jnp.exp2(s2 - top), 0.0)
    total = jnp.sum(p1, axis=0, keepdims=True) + jnp.sum(p2, axis=0, keepdims=True)
    acc[...] = weigh(own_ref, group, p1) + weigh(oth_ref, group, p2)

    def step(g, carry):
        top, total = carry
        s1 = scores(own_ref, g)
        s2 = scores(oth_ref, g)
        new = jnp.maximum(
            top, jnp.maximum(jnp.max(s1, axis=0, keepdims=True), jnp.max(s2, axis=0, keepdims=True))
        )
        alpha = jnp.exp2(top - new)
        p1 = jnp.exp2(s1 - new)
        p2 = jnp.exp2(s2 - new)
        total = total * alpha + jnp.sum(p1, axis=0, keepdims=True) + jnp.sum(p2, axis=0, keepdims=True)
        acc[...] = acc[...] * alpha + weigh(own_ref, g, p1) + weigh(oth_ref, g, p2)
        return new, total

    top, total = lax.fori_loop(0, group, step, (top, total))
    final = acc[...] / total
    for h in range(heads):
        att[:, h * HD:(h + 1) * HD] = final[:, h * rows:(h + 1) * rows].T.astype(BF)

    def project(b, _):
        pltpu.make_async_copy(w_hbm.at[:, pl.ds(0, width)], w_buf.at[b], sems.at[b]).wait()
        out_ref[b] = jnp.dot(att[...], w_buf[b], preferred_element_type=F32).astype(BF)
        return 0

    lax.fori_loop(0, blocks, project, 0)


def attend_project(pos, q, own, oth, w, blocks):
    rows, cols = q.shape
    depth, wide = w.shape
    width = wide // blocks
    vm = pl.BlockSpec(memory_space=pltpu.VMEM)
    return pl.pallas_call(
        attend_kernel,
        out_shape=jax.ShapeDtypeStruct((blocks, rows, width), BF),
        in_specs=[pl.BlockSpec(memory_space=pltpu.SMEM), vm, vm, vm, pl.BlockSpec(memory_space=pl.ANY)],
        out_specs=vm,
        scratch_shapes=[
            pltpu.VMEM((blocks, depth, width), BF),
            pltpu.VMEM((rows * cols // HD, HD), BF),
            pltpu.VMEM((HD, rows * cols // HD), F32),
            pltpu.VMEM((rows, cols), BF),
            pltpu.SemaphoreType.DMA((blocks,)),
        ],
        compiler_params=pltpu.CompilerParams(vmem_limit_bytes=48 << 20),
        cost_estimate=pl.CostEstimate(flops=4 << 30, bytes_accessed=20 << 20, transcendentals=2 << 20),
        name="attend_project",
    )(pos, q, own, oth, w)


def prep_kernel(pos_ref, g_ref, u_ref, gain_ref, km_ref, ks_ref, sm_ref, ss_ref):
    first = pos_ref[3] == 0
    n = g_ref.shape[0]
    gain = gain_ref[...]
    for j, ref in enumerate((g_ref, u_ref)):
        scaled = (ref[...].astype(F32) * gain).astype(BF)
        low, high = scaled[:, :512], scaled[:, 512:]
        keep = jnp.where(first, low, high)
        send = jnp.where(first, high, low)
        rows = pl.ds(j * n, n)
        km_ref[0, rows, :] = keep[:, :MCOLS]
        ks_ref[0, rows, :] = keep[:, MCOLS:]
        sm_ref[0, rows, :] = send[:, :MCOLS]
        ss_ref[0, rows, :] = send[:, MCOLS:]


def prepare(pos, gate_t, up_t, gain):
    n, depth = gate_t.shape
    wspec = pl.BlockSpec((n, 1024), lambda i, pos: (0, i))
    mspec = pl.BlockSpec((1, 2 * n, MCOLS), lambda i, pos: (i % 2, 0, i // 2))
    sspec = pl.BlockSpec((1, 2 * n, SCOLS), lambda i, pos: (i // 2, 0, i % 2))
    mshape = jax.ShapeDtypeStruct((2, 2 * n, 4 * MCOLS), BF)
    sshape = jax.ShapeDtypeStruct((4, 2 * n, 2 * SCOLS), BF)
    return pl.pallas_call(
        prep_kernel,
        out_shape=[mshape, sshape, mshape, sshape],
        grid_spec=pltpu.PrefetchScalarGridSpec(
            num_scalar_prefetch=1,
            grid=(depth // 1024,),
            in_specs=[wspec, wspec, pl.BlockSpec((1, 1024), lambda i, pos: (0, i))],
            out_specs=[mspec, sspec, mspec, sspec],
        ),
        compiler_params=pltpu.CompilerParams(vmem_limit_bytes=58 << 20),
        cost_estimate=pl.CostEstimate(flops=8 << 20, bytes_accessed=15 << 20, transcendentals=0),
        name="prepare",
    )(pos, gate_t, up_t, gain)


def gate_kernel(which, first, last, pos_ref, *refs):
    count = len(which)
    refs = list(refs)
    main = {c: (refs.pop(0), refs.pop(0)) for c in which}
    side = {c: (refs.pop(0), refs.pop(0)) for c in which}
    wm, ws = refs.pop(0), refs.pop(0)
    before = None if first else refs.pop(0)
    if last:
        own_ref, own_ss, par_ref = (refs.pop(0) for _ in range(3))
        acc = before
    else:
        acc = refs.pop(0)
    hm, hs, ssq, table, msem, ssem = refs
    x_at, y_at, z_at, core = (pos_ref[m] for m in range(4))
    rows = wm.shape[1]
    n2 = rows // 2

    def at(base, slot):
        return (base + OFFSETS[slot] + 4) & 3

    def fetch(u, c, j, on):
        for k in range(4):
            a, b = (j, k) if on == 0 else (k, j)
            col = pl.multiple_of(at(z_at, k) * MCOLS, MCOLS)
            pltpu.make_async_copy(
                main[c][b // 2].at[(b % 2) * 4 + a], hm.at[u, :, pl.ds(col, MCOLS)], msem.at[u]
            ).start()

    for m, c in enumerate(which):
        for j in range(4):
            u = m * 4 + j
            x = jnp.where(core == 0, at(x_at, c), at(x_at, j))
            y = jnp.where(core == 0, at(y_at, j), at(y_at, c))
            table[2 * u] = y * 2 + x // 2
            table[2 * u + 1] = x & 1
            pl.when(core == 0)(functools.partial(fetch, u, c, j, 0))
            pl.when(core != 0)(functools.partial(fetch, u, c, j, 1))
    for m, c in enumerate(which):
        for b in range(4):
            for a in range(4):
                x = at(x_at, a)
                row = pl.multiple_of((at(y_at, b) * 2 + x // 2) * 256, 256)
                col = pl.multiple_of((x & 1) * SCOLS, SCOLS)
                pltpu.make_async_copy(
                    side[c][b // 2].at[(b % 2) * 4 + a],
                    hs.at[m, pl.ds(row, 256), pl.ds(col, SCOLS)],
                    ssem.at[m],
                ).start()
    if first:
        acc[...] = jnp.zeros_like(acc)
    ssq[...] = jnp.zeros_like(ssq)
    ones = jnp.ones((8, 128), BF)

    def squares(block):
        part = jnp.zeros((block.shape[0], 128), F32)
        for j in range(block.shape[1] // 128):
            wide = block[:, j * 128:(j + 1) * 128].astype(F32)
            part = part + wide * wide
        return part

    def lane_sums(part):
        big = part.astype(BF)
        small = (part - big.astype(F32)).astype(BF)
        return sum(
            lax.dot_general(ones, t, (((1,), (1,)), ((), ())), preferred_element_type=F32)
            for t in (big, small)
        )

    def unit(u, _):
        pltpu.make_async_copy(hm.at[u], hm.at[u], msem.at[u]).wait()
        cols = pl.ds(pl.multiple_of(table[2 * u] * 256, 256), 256)
        block = hm[u]
        acc[:rows, cols] += lax.dot_general(
            wm[table[2 * u + 1]], block, (((1,), (1,)), ((), ())), preferred_element_type=F32
        )
        ssq[cols, :] += squares(block)
        return 0

    lax.fori_loop(0, 4 * count, unit, 0)
    for m in range(count):
        pltpu.make_async_copy(hs.at[m], hs.at[m], ssem.at[m]).wait()
    piece = 512

    def tail(p, _):
        cols = pl.ds(pl.multiple_of(p * piece, piece), piece)
        total = acc[:rows, cols]
        part = ssq[cols, :]
        for m, c in enumerate(which):
            block = hs[m, cols, :]
            total = total + lax.dot_general(
                ws[at(z_at, c)], block, (((1,), (1,)), ((), ())), preferred_element_type=F32
            )
            part = part + squares(block)
        sq = acc[rows:, cols] + lane_sums(part)
        if last:
            own_ref[:, cols] = total[:n2]
            par_ref[:n2, cols] = total[n2:].astype(BF)
            own_ss[:, cols] = sq
            big = sq.astype(BF)
            par_ref[n2:, cols] = jnp.concatenate(
                [big.astype(F32), sq - big.astype(F32)], axis=0
            ).astype(BF)
        else:
            acc[:rows, cols] = total
            acc[rows:, cols] = sq
        return 0

    lax.fori_loop(0, acc.shape[1] // piece, tail, 0)


def gate_up(pos, which, main, side, weights, before, last):
    n2 = weights[0].shape[1] // 2
    tokens = 2048
    count = len(which)
    first = before is None
    any_spec = pl.BlockSpec(memory_space=pl.ANY)
    vm = pl.BlockSpec(memory_space=pltpu.VMEM)
    pieces = [p for part in (main, side) for c in which for p in part[c]]
    operands = pieces + list(weights) + ([] if first else [before])
    partial = jax.ShapeDtypeStruct((2 * n2 + 8, tokens), F32)
    out_shape = [
        jax.ShapeDtypeStruct((n2, tokens), F32),
        jax.ShapeDtypeStruct((8, tokens), F32),
        jax.ShapeDtypeStruct((n2 + 16, tokens), BF),
    ] if last else partial
    return pl.pallas_call(
        functools.partial(gate_kernel, which, first, last),
        out_shape=out_shape,
        in_specs=[pl.BlockSpec(memory_space=pltpu.SMEM)]
        + [any_spec] * len(pieces)
        + [vm] * (len(operands) - len(pieces)),
        out_specs=[vm] * 3 if last else vm,
        scratch_shapes=[
            pltpu.VMEM((4 * count, 256, 4 * MCOLS), BF),
            pltpu.VMEM((count, tokens, 2 * SCOLS), BF),
            pltpu.VMEM((tokens, 128), F32),
            pltpu.SMEM((8 * count,), jnp.int32),
            pltpu.SemaphoreType.DMA((4 * count,)),
            pltpu.SemaphoreType.DMA((count,)),
        ],
        input_output_aliases={} if first or last else {len(operands): 0},
        compiler_params=pltpu.CompilerParams(vmem_limit_bytes=(10 + 8 * count) << 20),
        cost_estimate=pl.CostEstimate(
            flops=count * n2 * tokens * 4096, bytes_accessed=20 << 20, transcendentals=0
        ),
        name="gate_up",
    )(pos, *operands)


def finish_kernel(own_ref, ss_ref, got_ref, out_ref, buf, sems, *, depth):
    n = buf.shape[0]
    piece = 512

    def put(p):
        cols = pl.ds(p * piece, piece)
        return pltpu.make_async_copy(buf.at[:, cols], out_ref.at[:, cols], sems.at[p])

    for p in range(buf.shape[1] // piece):
        cols = pl.ds(p * piece, piece)
        got = got_ref[:, cols].astype(F32)
        total = ss_ref[:1, cols] + got[2 * n:2 * n + 1] + got[2 * n + 8:2 * n + 9]
        scale = lax.rsqrt(total / depth + EPS)
        gate = (own_ref[:n, cols] + got[:n]) * scale
        up = (own_ref[n:, cols] + got[n:2 * n]) * scale
        buf[:, cols] = (gate / (1.0 + jnp.exp(-gate)) * up).astype(BF)
        put(p).start()
    for p in range(buf.shape[1] // piece):
        put(p).wait()


def finish(own, ss, got, depth):
    rows, tokens = own.shape
    n = rows // 2
    vm = pl.BlockSpec(memory_space=pltpu.VMEM)
    return pl.pallas_call(
        functools.partial(finish_kernel, depth=depth),
        out_shape=jax.ShapeDtypeStruct((n, tokens), BF),
        in_specs=[vm] * 3,
        out_specs=pl.BlockSpec(memory_space=pl.ANY),
        scratch_shapes=[pltpu.VMEM((n, tokens), BF), pltpu.SemaphoreType.DMA((tokens // 512,))],
        compiler_params=pltpu.CompilerParams(vmem_limit_bytes=16 << 20),
        cost_estimate=pl.CostEstimate(flops=8 << 20, bytes_accessed=7 << 20, transcendentals=1 << 20),
        name="finish",
    )(own, ss, got)


def gather(blocks, orders):
    axes = [[(o[0][p], o[1][p]) for p in range(3)] for o in orders]
    near = lax.optimization_barrier(
        [[b] + [shift(b, a[0], by) for by in (1, -1, 2)] for b, a in zip(blocks, axes)]
    )
    cur = lax.optimization_barrier([jnp.stack(p) for p in near])
    ahead = [shift(b, a[1], 1) for b, a in zip(cur, axes)]
    rest = [[shift(b, a[1], by) for by in (-1, 2)] for b, a in zip(cur, axes)]

    def both_ways(block, a):
        return shift(block, a[2], 1), shift(block, a[2], -1)

    low = jnp.concatenate([cur[0], ahead[0]], 0)
    low = lax.optimization_barrier(low)
    first_near = both_ways(low, axes[0])
    highs = [jnp.concatenate(p, 0) for p in rest]
    highs, side_low = lax.optimization_barrier((highs, jnp.concatenate([cur[1], ahead[1]], 0)))
    lows = [low, side_low]
    low_near = [first_near, both_ways(side_low, axes[1])]
    high_near = [both_ways(b, a) for b, a in zip(highs, axes)]
    near = [(l[0], h[0], l[1], h[1]) for l, h in zip(low_near, high_near)]
    far = [(shift(t[0], a[2], 1), shift(t[3], a[2], -1)) for t, a in zip(near, axes)]
    return [
        {0: own, 1: t[:2], 2: t[2:], 3: o} for own, t, o in zip(zip(lows, highs), near, far)
    ]


def per_device(queries, key_rows, value_rows, out_weight, residual, norm_gain, gate_weight, up_weight):
    y_at, xh, core = lax.axis_index("y"), lax.axis_index("xh"), lax.axis_index("c")
    z_at, xl = lax.axis_index("z"), lax.axis_index("xl")
    x_at = xh * 2 + xl
    group = y_at * 2 + xh

    pair = jnp.concatenate([key_rows, value_rows], axis=1)
    spread = jnp.broadcast_to(pair[None], (8,) + pair.shape)
    pos2 = jnp.stack([x_at, y_at, z_at, core]).astype(jnp.int32)
    pos = jnp.stack([group, core]).astype(jnp.int32)
    own = lax.all_to_all(spread, ("y", "xh"), 0, 0, tiled=True)
    km, ks, sm, ss = prepare(pos2, gate_weight.T, up_weight.T, norm_gain[None, :])
    oth = swap_core(own)
    partial = attend_project(pos, queries, own, oth, out_weight, 8)
    terms = lax.all_to_all(partial, HEAD, 0, 0, tiled=True)
    weights = [jnp.concatenate([k, swap_core(t)], 1) for k, t in ((km, sm), (ks, ss))]
    terms, weights = lax.optimization_barrier((terms, weights))
    hidden = (residual.astype(F32) + jnp.sum(terms.astype(F32), axis=0)).astype(BF)

    keep = jnp.where(core == 0, hidden[:, :512], hidden[:, 512:])
    got = swap_core(jnp.where(core == 0, hidden[:, 512:], hidden[:, :512]))
    chip = jnp.where(core == 0, jnp.concatenate([keep, got], 0), jnp.concatenate([got, keep], 0))
    main, side = gather((chip[:, :MCOLS], chip[:, MCOLS:]), (MAIN, SIDE))
    sums = gate_up(pos2, (0,), main, side, weights, None, False)
    sums = gate_up(pos2, (1, 2), main, side, weights, sums, False)
    own_sums, own_ss, theirs = gate_up(pos2, (3,), main, side, weights, sums, True)
    out = finish(own_sums, own_ss, swap_core(theirs), norm_gain.shape[0])
    return out.T, hidden


def solution(mesh):
    devices = mesh.devices.reshape(4, 2, 2, 4, 2)
    fine = Mesh(devices, MESH)
    both = P(SEQ, HEAD)
    cols = P(None, SEQ + HEAD)
    return jax.shard_map(
        per_device,
        mesh=fine,
        in_specs=(both, both, both, P(HEAD, None), both, P(), cols, cols),
        out_specs=(cols, both),
        check_vma=False,
    )
```

```python
import functools
import math

import jax
import jax.numpy as jnp
from jax import lax
from jax.experimental import pallas as pl
from jax.experimental.pallas import tpu as pltpu
from jax.sharding import Mesh, PartitionSpec as P


HD = 128
LOW = -1e30
EPS = 1e-5
SEQ = ("y", "xh", "c")
HEAD = ("z", "xl")
MESH = ("y", "xh", "c", "z", "xl")
MAIN = ("yzx", "zxy")
SIDE = ("xyz", "xyz")
OFFSETS = (0, -1, 1, 2)
MCOLS, SCOLS = 384, 128
BF = jnp.bfloat16
F32 = jnp.float32


def shift(x, axes, by):
    pairs = []
    for core in range(2):
        for n in range(64):
            at = {"x": n // 16, "y": n // 4 % 4, "z": n % 4}
            to = dict(at)
            to[axes[core]] = (to[axes[core]] + by) % 4
            pairs.append(tuple(
                (((p["y"] * 2 + p["x"] // 2) * 2 + core) * 4 + p["z"]) * 2 + p["x"] % 2
                for p in (at, to)
            ))
    return lax.ppermute(x, MESH, pairs)


def swap_core(x):
    return lax.ppermute(x, "c", [(0, 1), (1, 0)])


def attend_kernel(pos_ref, q_ref, own_ref, oth_ref, w_hbm, out_ref, w_buf, qs, acc, att, sems):
    blocks = w_buf.shape[0]
    width = w_buf.shape[2]
    for b in range(blocks):
        pltpu.make_async_copy(w_hbm.at[:, pl.ds(b * width, width)], w_buf.at[b], sems.at[b]).start()
    heads = q_ref.shape[1] // HD
    rows = q_ref.shape[0]
    cols = heads * rows
    for h in range(heads):
        qs[pl.ds(h * rows, rows), :] = q_ref[:, h * HD:(h + 1) * HD]
    group = pos_ref[0]
    core = pos_ref[1]
    factor = math.log2(math.e) / math.sqrt(HD)
    qv = qs[...]

    def scores(ref, g):
        return lax.dot_general(
            ref[g, :, :HD], qv, (((1,), (1,)), ((), ())), preferred_element_type=F32
        ) * factor

    def weigh(ref, g, p):
        return lax.dot_general(
            ref[g, :, HD:], p.astype(BF), (((0,), (0,)), ((), ())), preferred_element_type=F32
        )

    key_at = lax.broadcasted_iota(jnp.int32, (rows, cols), 0)
    row_at = lax.broadcasted_iota(jnp.int32, (rows, cols), 1) % rows
    s1 = jnp.where(key_at <= row_at, scores(own_ref, group), LOW)
    s2 = jnp.where(core == 1, scores(oth_ref, group), LOW)
    top = jnp.maximum(jnp.max(s1, axis=0, keepdims=True), jnp.max(s2, axis=0, keepdims=True))
    p1 = jnp.exp2(s1 - top)
    p2 = jnp.where(core == 1, jnp.exp2(s2 - top), 0.0)
    total = jnp.sum(p1, axis=0, keepdims=True) + jnp.sum(p2, axis=0, keepdims=True)
    acc[...] = weigh(own_ref, group, p1) + weigh(oth_ref, group, p2)

    def step(g, carry):
        top, total = carry
        s1 = scores(own_ref, g)
        s2 = scores(oth_ref, g)
        new = jnp.maximum(
            top, jnp.maximum(jnp.max(s1, axis=0, keepdims=True), jnp.max(s2, axis=0, keepdims=True))
        )
        alpha = jnp.exp2(top - new)
        p1 = jnp.exp2(s1 - new)
        p2 = jnp.exp2(s2 - new)
        total = total * alpha + jnp.sum(p1, axis=0, keepdims=True) + jnp.sum(p2, axis=0, keepdims=True)
        acc[...] = acc[...] * alpha + weigh(own_ref, g, p1) + weigh(oth_ref, g, p2)
        return new, total

    top, total = lax.fori_loop(0, group, step, (top, total))
    final = acc[...] / total
    for h in range(heads):
        att[:, h * HD:(h + 1) * HD] = final[:, h * rows:(h + 1) * rows].T.astype(BF)

    def project(b, _):
        pltpu.make_async_copy(w_hbm.at[:, pl.ds(0, width)], w_buf.at[b], sems.at[b]).wait()
        out_ref[b] = jnp.dot(att[...], w_buf[b], preferred_element_type=F32).astype(BF)
        return 0

    lax.fori_loop(0, blocks, project, 0)


def attend_project(pos, q, own, oth, w, blocks):
    rows, cols = q.shape
    depth, wide = w.shape
    width = wide // blocks
    vm = pl.BlockSpec(memory_space=pltpu.VMEM)
    return pl.pallas_call(
        attend_kernel,
        out_shape=jax.ShapeDtypeStruct((blocks, rows, width), BF),
        in_specs=[pl.BlockSpec(memory_space=pltpu.SMEM), vm, vm, vm, pl.BlockSpec(memory_space=pl.ANY)],
        out_specs=vm,
        scratch_shapes=[
            pltpu.VMEM((blocks, depth, width), BF),
            pltpu.VMEM((rows * cols // HD, HD), BF),
            pltpu.VMEM((HD, rows * cols // HD), F32),
            pltpu.VMEM((rows, cols), BF),
            pltpu.SemaphoreType.DMA((blocks,)),
        ],
        compiler_params=pltpu.CompilerParams(vmem_limit_bytes=48 << 20),
        cost_estimate=pl.CostEstimate(flops=4 << 30, bytes_accessed=20 << 20, transcendentals=2 << 20),
        name="attend_project",
    )(pos, q, own, oth, w)


def prep_kernel(pos_ref, g_ref, u_ref, gain_ref, km_ref, ks_ref, sm_ref, ss_ref):
    first = pos_ref[3] == 0
    n = g_ref.shape[0]
    gain = gain_ref[...]
    for j, ref in enumerate((g_ref, u_ref)):
        scaled = (ref[...].astype(F32) * gain).astype(BF)
        low, high = scaled[:, :512], scaled[:, 512:]
        keep = jnp.where(first, low, high)
        send = jnp.where(first, high, low)
        rows = pl.ds(j * n, n)
        km_ref[0, rows, :] = keep[:, :MCOLS]
        ks_ref[0, rows, :] = keep[:, MCOLS:]
        sm_ref[0, rows, :] = send[:, :MCOLS]
        ss_ref[0, rows, :] = send[:, MCOLS:]


def prepare(pos, gate_t, up_t, gain):
    n, depth = gate_t.shape
    wspec = pl.BlockSpec((n, 1024), lambda i, pos: (0, i))
    mspec = pl.BlockSpec((1, 2 * n, MCOLS), lambda i, pos: (i % 2, 0, i // 2))
    sspec = pl.BlockSpec((1, 2 * n, SCOLS), lambda i, pos: (i // 2, 0, i % 2))
    mshape = jax.ShapeDtypeStruct((2, 2 * n, 4 * MCOLS), BF)
    sshape = jax.ShapeDtypeStruct((4, 2 * n, 2 * SCOLS), BF)
    return pl.pallas_call(
        prep_kernel,
        out_shape=[mshape, sshape, mshape, sshape],
        grid_spec=pltpu.PrefetchScalarGridSpec(
            num_scalar_prefetch=1,
            grid=(depth // 1024,),
            in_specs=[wspec, wspec, pl.BlockSpec((1, 1024), lambda i, pos: (0, i))],
            out_specs=[mspec, sspec, mspec, sspec],
        ),
        compiler_params=pltpu.CompilerParams(vmem_limit_bytes=16 << 20),
        cost_estimate=pl.CostEstimate(flops=8 << 20, bytes_accessed=15 << 20, transcendentals=0),
        name="prepare",
    )(pos, gate_t, up_t, gain)


def gate_kernel(which, first, last, pos_ref, *refs):
    count = len(which)
    refs = list(refs)
    main = {c: tuple(refs.pop(0) for _ in range(3)) for c in which}
    side = {c: (refs.pop(0), refs.pop(0)) for c in which}
    wm, ws = refs.pop(0), refs.pop(0)
    before = None if first else refs.pop(0)
    if last:
        own_ref, own_ss, par_ref = (refs.pop(0) for _ in range(3))
        acc = before
    else:
        acc = refs.pop(0)
    hm, hs, ssq, table, msem, ssem = refs
    x_at, y_at, z_at, core = (pos_ref[m] for m in range(4))
    rows = wm.shape[1]
    n2 = rows // 2

    def at(base, slot):
        return (base + OFFSETS[slot] + 4) & 3

    def fetch(u, c, j, on):
        for k in range(4):
            a, b = (j, k) if on == 0 else (k, j)
            col = pl.multiple_of(at(z_at, k) * MCOLS, MCOLS)
            src = main[c][max(b - 1, 0)].at[(b % 2) * 4 + a if b < 2 else a]
            pltpu.make_async_copy(src, hm.at[u, :, pl.ds(col, MCOLS)], msem.at[u]).start()

    for m, c in enumerate(which):
        for j in range(4):
            u = m * 4 + j
            x = jnp.where(core == 0, at(x_at, c), at(x_at, j))
            y = jnp.where(core == 0, at(y_at, j), at(y_at, c))
            table[2 * u] = y * 2 + x // 2
            table[2 * u + 1] = x & 1
            pl.when(core == 0)(functools.partial(fetch, u, c, j, 0))
            pl.when(core != 0)(functools.partial(fetch, u, c, j, 1))
    for m, c in enumerate(which):
        for b in range(4):
            for a in range(4):
                x = at(x_at, a)
                row = pl.multiple_of((at(y_at, b) * 2 + x // 2) * 256, 256)
                col = pl.multiple_of((x & 1) * SCOLS, SCOLS)
                pltpu.make_async_copy(
                    side[c][b // 2].at[(b % 2) * 4 + a],
                    hs.at[m, pl.ds(row, 256), pl.ds(col, SCOLS)],
                    ssem.at[m],
                ).start()
    if first:
        acc[...] = jnp.zeros_like(acc)
    ssq[...] = jnp.zeros_like(ssq)
    ones = jnp.ones((8, 128), BF)

    def squares(block):
        part = jnp.zeros((block.shape[0], 128), F32)
        for j in range(block.shape[1] // 128):
            wide = block[:, j * 128:(j + 1) * 128].astype(F32)
            part = part + wide * wide
        return part

    def lane_sums(part):
        big = part.astype(BF)
        small = (part - big.astype(F32)).astype(BF)
        return sum(
            lax.dot_general(ones, t, (((1,), (1,)), ((), ())), preferred_element_type=F32)
            for t in (big, small)
        )

    def unit(u, _):
        pltpu.make_async_copy(hm.at[u], hm.at[u], msem.at[u]).wait()
        cols = pl.ds(pl.multiple_of(table[2 * u] * 256, 256), 256)
        block = hm[u]
        acc[:rows, cols] += lax.dot_general(
            wm[table[2 * u + 1]], block, (((1,), (1,)), ((), ())), preferred_element_type=F32
        )
        ssq[cols, :] += squares(block)
        return 0

    lax.fori_loop(0, 4 * count, unit, 0)
    for m in range(count):
        pltpu.make_async_copy(hs.at[m], hs.at[m], ssem.at[m]).wait()
    piece = 512

    def tail(p, _):
        cols = pl.ds(pl.multiple_of(p * piece, piece), piece)
        total = acc[:rows, cols]
        part = ssq[cols, :]
        for m, c in enumerate(which):
            block = hs[m, cols, :]
            total = total + lax.dot_general(
                ws[at(z_at, c)], block, (((1,), (1,)), ((), ())), preferred_element_type=F32
            )
            part = part + squares(block)
        sq = acc[rows:, cols] + lane_sums(part)
        if last:
            own_ref[:, cols] = total[:n2]
            par_ref[:n2, cols] = total[n2:].astype(BF)
            own_ss[:, cols] = sq
            big = sq.astype(BF)
            par_ref[n2:, cols] = jnp.concatenate(
                [big.astype(F32), sq - big.astype(F32)], axis=0
            ).astype(BF)
        else:
            acc[:rows, cols] = total
            acc[rows:, cols] = sq
        return 0

    lax.fori_loop(0, acc.shape[1] // piece, tail, 0)


def gate_up(pos, which, main, side, weights, before, last):
    n2 = weights[0].shape[1] // 2
    tokens = 2048
    count = len(which)
    first = before is None
    any_spec = pl.BlockSpec(memory_space=pl.ANY)
    vm = pl.BlockSpec(memory_space=pltpu.VMEM)
    pieces = [p for part in (main, side) for c in which for p in part[c]]
    operands = pieces + list(weights) + ([] if first else [before])
    partial = jax.ShapeDtypeStruct((2 * n2 + 8, tokens), F32)
    out_shape = [
        jax.ShapeDtypeStruct((n2, tokens), F32),
        jax.ShapeDtypeStruct((8, tokens), F32),
        jax.ShapeDtypeStruct((n2 + 16, tokens), BF),
    ] if last else partial
    return pl.pallas_call(
        functools.partial(gate_kernel, which, first, last),
        out_shape=out_shape,
        in_specs=[pl.BlockSpec(memory_space=pltpu.SMEM)]
        + [any_spec] * len(pieces)
        + [vm] * (len(operands) - len(pieces)),
        out_specs=[vm] * 3 if last else vm,
        scratch_shapes=[
            pltpu.VMEM((4 * count, 256, 4 * MCOLS), BF),
            pltpu.VMEM((count, tokens, 2 * SCOLS), BF),
            pltpu.VMEM((tokens, 128), F32),
            pltpu.SMEM((8 * count,), jnp.int32),
            pltpu.SemaphoreType.DMA((4 * count,)),
            pltpu.SemaphoreType.DMA((count,)),
        ],
        input_output_aliases={} if first or last else {len(operands): 0},
        compiler_params=pltpu.CompilerParams(vmem_limit_bytes=(10 + 8 * count) << 20),
        cost_estimate=pl.CostEstimate(
            flops=count * n2 * tokens * 4096, bytes_accessed=20 << 20, transcendentals=0
        ),
        name="gate_up",
    )(pos, *operands)


def finish_kernel(own_ref, ss_ref, got_ref, out_ref, buf, sems, *, depth):
    n = buf.shape[0]
    piece = 512

    def put(p):
        cols = pl.ds(p * piece, piece)
        return pltpu.make_async_copy(buf.at[:, cols], out_ref.at[:, cols], sems.at[p])

    for p in range(buf.shape[1] // piece):
        cols = pl.ds(p * piece, piece)
        got = got_ref[:, cols].astype(F32)
        total = ss_ref[:1, cols] + got[2 * n:2 * n + 1] + got[2 * n + 8:2 * n + 9]
        scale = lax.rsqrt(total / depth + EPS)
        gate = (own_ref[:n, cols] + got[:n]) * scale
        up = (own_ref[n:, cols] + got[n:2 * n]) * scale
        buf[:, cols] = (gate / (1.0 + jnp.exp(-gate)) * up).astype(BF)
        put(p).start()
    for p in range(buf.shape[1] // piece):
        put(p).wait()


def finish(own, ss, got, depth):
    rows, tokens = own.shape
    n = rows // 2
    vm = pl.BlockSpec(memory_space=pltpu.VMEM)
    return pl.pallas_call(
        functools.partial(finish_kernel, depth=depth),
        out_shape=jax.ShapeDtypeStruct((n, tokens), BF),
        in_specs=[vm] * 3,
        out_specs=pl.BlockSpec(memory_space=pl.ANY),
        scratch_shapes=[pltpu.VMEM((n, tokens), BF), pltpu.SemaphoreType.DMA((tokens // 512,))],
        compiler_params=pltpu.CompilerParams(vmem_limit_bytes=16 << 20),
        cost_estimate=pl.CostEstimate(flops=8 << 20, bytes_accessed=7 << 20, transcendentals=1 << 20),
        name="finish",
    )(own, ss, got)


def gather(blocks, orders):
    axes = [[(o[0][p], o[1][p]) for p in range(3)] for o in orders]
    near = lax.optimization_barrier(
        [[b] + [shift(b, a[0], by) for by in (1, -1, 2)] for b, a in zip(blocks, axes)]
    )
    cur = lax.optimization_barrier([jnp.stack(p) for p in near])
    ahead = [shift(b, a[1], 1) for b, a in zip(cur, axes)]
    rest = [[shift(b, a[1], by) for by in (-1, 2)] for b, a in zip(cur, axes)]

    def both_ways(block, a):
        return shift(block, a[2], 1), shift(block, a[2], -1)

    low = jnp.concatenate([cur[0], ahead[0]], 0)
    low = lax.optimization_barrier(low)
    third, fourth = rest[0]
    lows = both_ways(low, axes[0])
    thirds = both_ways(third, axes[0])
    fourths = both_ways(fourth, axes[0])
    side_low = jnp.concatenate([cur[1], ahead[1]], 0)
    side_high = jnp.concatenate(rest[1], 0)
    side_low, side_high = lax.optimization_barrier((side_low, side_high))
    side_lows = both_ways(side_low, axes[1])
    side_highs = both_ways(side_high, axes[1])
    far_low = shift(lows[0], axes[0][2], 1)
    far_side = (shift(side_lows[0], axes[1][2], 1), shift(side_highs[1], axes[1][2], -1))
    far_third = shift(thirds[1], axes[0][2], -1)
    far_fourth = shift(fourths[1], axes[0][2], -1)
    main = {
        0: (low, third, fourth),
        1: (lows[0], thirds[0], fourths[0]),
        2: (lows[1], thirds[1], fourths[1]),
        3: (far_low, far_third, far_fourth),
    }
    side = {
        0: (side_low, side_high),
        1: (side_lows[0], side_highs[0]),
        2: (side_lows[1], side_highs[1]),
        3: far_side,
    }
    return main, side


def per_device(queries, key_rows, value_rows, out_weight, residual, norm_gain, gate_weight, up_weight):
    y_at, xh, core = lax.axis_index("y"), lax.axis_index("xh"), lax.axis_index("c")
    z_at, xl = lax.axis_index("z"), lax.axis_index("xl")
    x_at = xh * 2 + xl
    group = y_at * 2 + xh

    pair = jnp.concatenate([key_rows, value_rows], axis=1)
    spread = jnp.broadcast_to(pair[None], (8,) + pair.shape)
    own = lax.all_to_all(spread, ("y", "xh"), 0, 0, tiled=True)
    oth = swap_core(own)

    pos = jnp.stack([group, core]).astype(jnp.int32)
    partial = attend_project(pos, queries, own, oth, out_weight, 8)
    pos2 = jnp.stack([x_at, y_at, z_at, core]).astype(jnp.int32)
    partial, gate_raw, up_raw = lax.optimization_barrier((partial, gate_weight.T, up_weight.T))
    terms = lax.all_to_all(partial, HEAD, 0, 0, tiled=True)
    km, ks, sm, ss = prepare(pos2, gate_raw, up_raw, norm_gain[None, :])
    weights = [jnp.concatenate([k, swap_core(t)], 1) for k, t in ((km, sm), (ks, ss))]
    terms, weights = lax.optimization_barrier((terms, weights))
    hidden = (residual.astype(F32) + jnp.sum(terms.astype(F32), axis=0)).astype(BF)

    keep = jnp.where(core == 0, hidden[:, :512], hidden[:, 512:])
    got = swap_core(jnp.where(core == 0, hidden[:, 512:], hidden[:, :512]))
    chip = jnp.where(core == 0, jnp.concatenate([keep, got], 0), jnp.concatenate([got, keep], 0))
    main, side = gather((chip[:, :MCOLS], chip[:, MCOLS:]), (MAIN, SIDE))
    sums = gate_up(pos2, (0,), main, side, weights, None, False)
    sums = gate_up(pos2, (1, 2), main, side, weights, sums, False)
    own_sums, own_ss, theirs = gate_up(pos2, (3,), main, side, weights, sums, True)
    out = finish(own_sums, own_ss, swap_core(theirs), norm_gain.shape[0])
    return out.T, hidden


def solution(mesh):
    devices = mesh.devices.reshape(4, 2, 2, 4, 2)
    fine = Mesh(devices, MESH)
    both = P(SEQ, HEAD)
    cols = P(None, SEQ + HEAD)
    return jax.shard_map(
        per_device,
        mesh=fine,
        in_specs=(both, both, both, P(HEAD, None), both, P(), cols, cols),
        out_specs=(cols, both),
        check_vma=False,
    )
```

```python
import functools
import math

import jax
import jax.numpy as jnp
from jax import lax
from jax.experimental import pallas as pl
from jax.experimental.pallas import tpu as pltpu
from jax.sharding import Mesh, PartitionSpec as P


HD = 128
LOW = -1e30
EPS = 1e-5
SEQ = ("y", "xh", "c")
HEAD = ("z", "xl")
MESH = ("y", "xh", "c", "z", "xl")
MAIN = ("yzx", "zxy")
SIDE = ("xyz", "xyz")
OFFSETS = (0, -1, 1, 2)
MCOLS, SCOLS = 384, 128
BF = jnp.bfloat16
F32 = jnp.float32


def shift(x, axes, by):
    pairs = []
    for core in range(2):
        for n in range(64):
            at = {"x": n // 16, "y": n // 4 % 4, "z": n % 4}
            to = dict(at)
            to[axes[core]] = (to[axes[core]] + by) % 4
            pairs.append(tuple(
                (((p["y"] * 2 + p["x"] // 2) * 2 + core) * 4 + p["z"]) * 2 + p["x"] % 2
                for p in (at, to)
            ))
    return lax.ppermute(x, MESH, pairs)


def swap_core(x):
    return lax.ppermute(x, "c", [(0, 1), (1, 0)])


def attend_kernel(pos_ref, q_ref, own_ref, oth_ref, w_hbm, out_ref, w_buf, qs, acc, att, sems):
    blocks = w_buf.shape[0]
    width = w_buf.shape[2]
    for b in range(blocks):
        pltpu.make_async_copy(w_hbm.at[:, pl.ds(b * width, width)], w_buf.at[b], sems.at[b]).start()
    heads = q_ref.shape[1] // HD
    rows = q_ref.shape[0]
    cols = heads * rows
    for h in range(heads):
        qs[pl.ds(h * rows, rows), :] = q_ref[:, h * HD:(h + 1) * HD]
    group = pos_ref[0]
    core = pos_ref[1]
    factor = math.log2(math.e) / math.sqrt(HD)
    qv = qs[...]

    def scores(ref, g):
        return lax.dot_general(
            ref[g, :, :HD], qv, (((1,), (1,)), ((), ())), preferred_element_type=F32
        ) * factor

    def weigh(ref, g, p):
        return lax.dot_general(
            ref[g, :, HD:], p.astype(BF), (((0,), (0,)), ((), ())), preferred_element_type=F32
        )

    key_at = lax.broadcasted_iota(jnp.int32, (rows, cols), 0)
    row_at = lax.broadcasted_iota(jnp.int32, (rows, cols), 1) % rows
    s1 = jnp.where(key_at <= row_at, scores(own_ref, group), LOW)
    s2 = jnp.where(core == 1, scores(oth_ref, group), LOW)
    top = jnp.maximum(jnp.max(s1, axis=0, keepdims=True), jnp.max(s2, axis=0, keepdims=True))
    p1 = jnp.exp2(s1 - top)
    p2 = jnp.where(core == 1, jnp.exp2(s2 - top), 0.0)
    total = jnp.sum(p1, axis=0, keepdims=True) + jnp.sum(p2, axis=0, keepdims=True)
    acc[...] = weigh(own_ref, group, p1) + weigh(oth_ref, group, p2)

    def step(g, carry):
        top, total = carry
        s1 = scores(own_ref, g)
        s2 = scores(oth_ref, g)
        new = jnp.maximum(
            top, jnp.maximum(jnp.max(s1, axis=0, keepdims=True), jnp.max(s2, axis=0, keepdims=True))
        )
        alpha = jnp.exp2(top - new)
        p1 = jnp.exp2(s1 - new)
        p2 = jnp.exp2(s2 - new)
        total = total * alpha + jnp.sum(p1, axis=0, keepdims=True) + jnp.sum(p2, axis=0, keepdims=True)
        acc[...] = acc[...] * alpha + weigh(own_ref, g, p1) + weigh(oth_ref, g, p2)
        return new, total

    top, total = lax.fori_loop(0, group, step, (top, total))
    final = acc[...] / total
    for h in range(heads):
        att[:, h * HD:(h + 1) * HD] = final[:, h * rows:(h + 1) * rows].T.astype(BF)

    def project(b, _):
        pltpu.make_async_copy(w_hbm.at[:, pl.ds(0, width)], w_buf.at[b], sems.at[b]).wait()
        out_ref[b] = jnp.dot(att[...], w_buf[b], preferred_element_type=F32).astype(BF)
        return 0

    lax.fori_loop(0, blocks, project, 0)


def attend_project(pos, q, own, oth, w, blocks):
    rows, cols = q.shape
    depth, wide = w.shape
    width = wide // blocks
    vm = pl.BlockSpec(memory_space=pltpu.VMEM)
    return pl.pallas_call(
        attend_kernel,
        out_shape=jax.ShapeDtypeStruct((blocks, rows, width), BF),
        in_specs=[pl.BlockSpec(memory_space=pltpu.SMEM), vm, vm, vm, pl.BlockSpec(memory_space=pl.ANY)],
        out_specs=vm,
        scratch_shapes=[
            pltpu.VMEM((blocks, depth, width), BF),
            pltpu.VMEM((rows * cols // HD, HD), BF),
            pltpu.VMEM((HD, rows * cols // HD), F32),
            pltpu.VMEM((rows, cols), BF),
            pltpu.SemaphoreType.DMA((blocks,)),
        ],
        compiler_params=pltpu.CompilerParams(vmem_limit_bytes=48 << 20),
        cost_estimate=pl.CostEstimate(flops=4 << 30, bytes_accessed=20 << 20, transcendentals=2 << 20),
        name="attend_project",
    )(pos, q, own, oth, w)


def prep_kernel(pos_ref, g_ref, u_ref, gain_ref, km_ref, ks_ref, sm_ref, ss_ref):
    first = pos_ref[3] == 0
    n = g_ref.shape[0]
    gain = gain_ref[...]
    for j, ref in enumerate((g_ref, u_ref)):
        scaled = (ref[...].astype(F32) * gain).astype(BF)
        low, high = scaled[:, :512], scaled[:, 512:]
        keep = jnp.where(first, low, high)
        send = jnp.where(first, high, low)
        rows = pl.ds(j * n, n)
        km_ref[0, rows, :] = keep[:, :MCOLS]
        ks_ref[0, rows, :] = keep[:, MCOLS:]
        sm_ref[0, rows, :] = send[:, :MCOLS]
        ss_ref[0, rows, :] = send[:, MCOLS:]


def prepare(pos, gate_t, up_t, gain):
    n, depth = gate_t.shape
    wspec = pl.BlockSpec((n, 1024), lambda i, pos: (0, i))
    mspec = pl.BlockSpec((1, 2 * n, MCOLS), lambda i, pos: (i % 2, 0, i // 2))
    sspec = pl.BlockSpec((1, 2 * n, SCOLS), lambda i, pos: (i // 2, 0, i % 2))
    mshape = jax.ShapeDtypeStruct((2, 2 * n, 4 * MCOLS), BF)
    sshape = jax.ShapeDtypeStruct((4, 2 * n, 2 * SCOLS), BF)
    return pl.pallas_call(
        prep_kernel,
        out_shape=[mshape, sshape, mshape, sshape],
        grid_spec=pltpu.PrefetchScalarGridSpec(
            num_scalar_prefetch=1,
            grid=(depth // 1024,),
            in_specs=[wspec, wspec, pl.BlockSpec((1, 1024), lambda i, pos: (0, i))],
            out_specs=[mspec, sspec, mspec, sspec],
        ),
        compiler_params=pltpu.CompilerParams(vmem_limit_bytes=16 << 20),
        cost_estimate=pl.CostEstimate(flops=8 << 20, bytes_accessed=15 << 20, transcendentals=0),
        name="prepare",
    )(pos, gate_t, up_t, gain)


def gate_kernel(which, stage, pos_ref, *refs):
    count = len(which)
    refs = list(refs)
    main = {c: tuple(refs.pop(0) for _ in range(3)) for c in which}
    side = {c: (refs.pop(0), refs.pop(0)) for c in which}
    wm, ws = refs.pop(0), refs.pop(0)
    first = stage == "first"
    last = stage in ("theirs", "mine")
    before = None if first else refs.pop(0)
    if stage == "theirs":
        own_ss, par_ref = refs.pop(0), refs.pop(0)
    elif stage == "mine":
        own_ref = refs.pop(0)
    else:
        acc = refs.pop(0)
    if last:
        acc = refs.pop()
    hm, hs, ssq, table, msem, ssem = refs
    x_at, y_at, z_at, core = (pos_ref[m] for m in range(4))
    both = wm.shape[1]
    n2 = both // 2
    lead = n2 if stage == "theirs" else 0
    rows = n2 if last else both
    squared = stage != "mine"

    def at(base, slot):
        return (base + OFFSETS[slot] + 4) & 3

    def fetch(u, c, j, on):
        for k in range(4):
            a, b = (j, k) if on == 0 else (k, j)
            col = pl.multiple_of(at(z_at, k) * MCOLS, MCOLS)
            src = main[c][max(b - 1, 0)].at[(b % 2) * 4 + a if b < 2 else a]
            pltpu.make_async_copy(src, hm.at[u, :, pl.ds(col, MCOLS)], msem.at[u]).start()

    for m, c in enumerate(which):
        for j in range(4):
            u = m * 4 + j
            x = jnp.where(core == 0, at(x_at, c), at(x_at, j))
            y = jnp.where(core == 0, at(y_at, j), at(y_at, c))
            table[2 * u] = y * 2 + x // 2
            table[2 * u + 1] = x & 1
            pl.when(core == 0)(functools.partial(fetch, u, c, j, 0))
            pl.when(core != 0)(functools.partial(fetch, u, c, j, 1))
    for m, c in enumerate(which):
        for b in range(4):
            for a in range(4):
                x = at(x_at, a)
                row = pl.multiple_of((at(y_at, b) * 2 + x // 2) * 256, 256)
                col = pl.multiple_of((x & 1) * SCOLS, SCOLS)
                pltpu.make_async_copy(
                    side[c][b // 2].at[(b % 2) * 4 + a],
                    hs.at[m, pl.ds(row, 256), pl.ds(col, SCOLS)],
                    ssem.at[m],
                ).start()
    if first or last:
        acc[...] = jnp.zeros_like(acc)
    if squared:
        ssq[...] = jnp.zeros_like(ssq)
    ones = jnp.ones((8, 128), BF)

    def squares(block):
        part = jnp.zeros((block.shape[0], 128), F32)
        for j in range(block.shape[1] // 128):
            wide = block[:, j * 128:(j + 1) * 128].astype(F32)
            part = part + wide * wide
        return part

    def lane_sums(part):
        big = part.astype(BF)
        small = (part - big.astype(F32)).astype(BF)
        return sum(
            lax.dot_general(ones, t, (((1,), (1,)), ((), ())), preferred_element_type=F32)
            for t in (big, small)
        )

    def unit(u, _):
        pltpu.make_async_copy(hm.at[u], hm.at[u], msem.at[u]).wait()
        cols = pl.ds(pl.multiple_of(table[2 * u] * 256, 256), 256)
        block = hm[u]
        acc[:rows, cols] += lax.dot_general(
            wm[table[2 * u + 1], pl.ds(lead, rows), :], block, (((1,), (1,)), ((), ())),
            preferred_element_type=F32,
        )
        if squared:
            ssq[cols, :] += squares(block)
        return 0

    lax.fori_loop(0, 4 * count, unit, 0)
    for m in range(count):
        pltpu.make_async_copy(hs.at[m], hs.at[m], ssem.at[m]).wait()
    piece = 512

    def tail(p, _):
        cols = pl.ds(pl.multiple_of(p * piece, piece), piece)
        total = acc[:rows, cols]
        if last:
            total = total + before[pl.ds(lead, rows), cols]
        part = ssq[cols, :] if squared else None
        for m, c in enumerate(which):
            block = hs[m, cols, :]
            total = total + lax.dot_general(
                ws[at(z_at, c), pl.ds(lead, rows), :], block, (((1,), (1,)), ((), ())),
                preferred_element_type=F32,
            )
            if squared:
                part = part + squares(block)
        if squared:
            sq = (before if last else acc)[both:, cols] + lane_sums(part)
        if stage == "theirs":
            par_ref[:n2, cols] = total.astype(BF)
            own_ss[:, cols] = sq
            big = sq.astype(BF)
            par_ref[n2:, cols] = jnp.concatenate(
                [big.astype(F32), sq - big.astype(F32)], axis=0
            ).astype(BF)
        elif stage == "mine":
            own_ref[:, cols] = total
        else:
            acc[:rows, cols] = total
            acc[rows:, cols] = sq
        return 0

    lax.fori_loop(0, hs.shape[1] // piece, tail, 0)


def gate_up(pos, which, main, side, weights, before, stage):
    n2 = weights[0].shape[1] // 2
    tokens = 2048
    count = len(which)
    first = before is None
    last = stage in ("theirs", "mine")
    any_spec = pl.BlockSpec(memory_space=pl.ANY)
    vm = pl.BlockSpec(memory_space=pltpu.VMEM)
    pieces = [p for part in (main, side) for c in which for p in part[c]]
    operands = pieces + list(weights) + ([] if first else [before])
    partial = jax.ShapeDtypeStruct((2 * n2 + 8, tokens), F32)
    out_shape = {
        "theirs": [
            jax.ShapeDtypeStruct((8, tokens), F32),
            jax.ShapeDtypeStruct((n2 + 16, tokens), BF),
        ],
        "mine": jax.ShapeDtypeStruct((n2, tokens), F32),
    }.get(stage, partial)
    return pl.pallas_call(
        functools.partial(gate_kernel, which, stage),
        out_shape=out_shape,
        in_specs=[pl.BlockSpec(memory_space=pltpu.SMEM)]
        + [any_spec] * len(pieces)
        + [vm] * (len(operands) - len(pieces)),
        out_specs=[vm] * 2 if stage == "theirs" else vm,
        scratch_shapes=[
            pltpu.VMEM((4 * count, 256, 4 * MCOLS), BF),
            pltpu.VMEM((count, tokens, 2 * SCOLS), BF),
            pltpu.VMEM((tokens, 128), F32),
            pltpu.SMEM((8 * count,), jnp.int32),
            pltpu.SemaphoreType.DMA((4 * count,)),
            pltpu.SemaphoreType.DMA((count,)),
        ]
        + ([pltpu.VMEM((n2, tokens), F32)] if last else []),
        input_output_aliases={} if first or last else {len(operands): 0},
        compiler_params=pltpu.CompilerParams(vmem_limit_bytes=(10 + 8 * count) << 20),
        cost_estimate=pl.CostEstimate(
            flops=count * n2 * tokens * 4096, bytes_accessed=20 << 20, transcendentals=0
        ),
        name="gate_up",
    )(pos, *operands)


def finish_kernel(own_ref, ss_ref, got_ref, out_ref, buf, sems, *, depth):
    n = buf.shape[0]
    piece = 512

    def put(p):
        cols = pl.ds(p * piece, piece)
        return pltpu.make_async_copy(buf.at[:, cols], out_ref.at[:, cols], sems.at[p])

    for p in range(buf.shape[1] // piece):
        cols = pl.ds(p * piece, piece)
        got = got_ref[:, cols].astype(F32)
        total = ss_ref[:1, cols] + got[2 * n:2 * n + 1] + got[2 * n + 8:2 * n + 9]
        scale = lax.rsqrt(total / depth + EPS)
        gate = (own_ref[:n, cols] + got[:n]) * scale
        up = (own_ref[n:, cols] + got[n:2 * n]) * scale
        buf[:, cols] = (gate / (1.0 + jnp.exp(-gate)) * up).astype(BF)
        put(p).start()
    for p in range(buf.shape[1] // piece):
        put(p).wait()


def finish(own, ss, got, depth):
    rows, tokens = own.shape
    n = rows // 2
    vm = pl.BlockSpec(memory_space=pltpu.VMEM)
    return pl.pallas_call(
        functools.partial(finish_kernel, depth=depth),
        out_shape=jax.ShapeDtypeStruct((n, tokens), BF),
        in_specs=[vm] * 3,
        out_specs=pl.BlockSpec(memory_space=pl.ANY),
        scratch_shapes=[pltpu.VMEM((n, tokens), BF), pltpu.SemaphoreType.DMA((tokens // 512,))],
        compiler_params=pltpu.CompilerParams(vmem_limit_bytes=16 << 20),
        cost_estimate=pl.CostEstimate(flops=8 << 20, bytes_accessed=7 << 20, transcendentals=1 << 20),
        name="finish",
    )(own, ss, got)


def gather(blocks, orders):
    axes = [[(o[0][p], o[1][p]) for p in range(3)] for o in orders]

    def around(block, a):
        return [shift(block, a, by) for by in (1, -1, 2)]

    main_near = around(blocks[0], axes[0][0])
    side_near = around(blocks[1], axes[1][0])
    main_near = lax.optimization_barrier([blocks[0]] + main_near)
    cur_main = lax.optimization_barrier(jnp.stack(main_near))
    ahead = shift(cur_main, axes[0][1], 1)
    third, fourth = (shift(cur_main, axes[0][1], by) for by in (-1, 2))
    side_near = lax.optimization_barrier([blocks[1]] + side_near)
    cur_side = lax.optimization_barrier(jnp.stack(side_near))
    side_next = around(cur_side, axes[1][1])

    def both_ways(block, a):
        return shift(block, a[2], 1), shift(block, a[2], -1)

    low = jnp.concatenate([cur_main, ahead], 0)
    low = lax.optimization_barrier(low)
    lows = both_ways(low, axes[0])
    thirds = both_ways(third, axes[0])
    fourths = both_ways(fourth, axes[0])
    side_low = jnp.concatenate([cur_side, side_next[0]], 0)
    side_high = jnp.concatenate(side_next[1:], 0)
    side_low, side_high = lax.optimization_barrier((side_low, side_high))
    side_lows = both_ways(side_low, axes[1])
    side_highs = both_ways(side_high, axes[1])
    far_low = shift(lows[0], axes[0][2], 1)
    far_side = (shift(side_lows[0], axes[1][2], 1), shift(side_highs[1], axes[1][2], -1))
    far_third = shift(thirds[1], axes[0][2], -1)
    far_fourth = shift(fourths[1], axes[0][2], -1)
    main = {
        0: (low, third, fourth),
        1: (lows[0], thirds[0], fourths[0]),
        2: (lows[1], thirds[1], fourths[1]),
        3: (far_low, far_third, far_fourth),
    }
    side = {
        0: (side_low, side_high),
        1: (side_lows[0], side_highs[0]),
        2: (side_lows[1], side_highs[1]),
        3: far_side,
    }
    return main, side


def per_device(queries, key_rows, value_rows, out_weight, residual, norm_gain, gate_weight, up_weight):
    y_at, xh, core = lax.axis_index("y"), lax.axis_index("xh"), lax.axis_index("c")
    z_at, xl = lax.axis_index("z"), lax.axis_index("xl")
    x_at = xh * 2 + xl
    group = y_at * 2 + xh

    pair = jnp.concatenate([key_rows, value_rows], axis=1)
    spread = jnp.broadcast_to(pair[None], (8,) + pair.shape)
    own = lax.all_to_all(spread, ("y", "xh"), 0, 0, tiled=True)
    oth = swap_core(own)

    pos = jnp.stack([group, core]).astype(jnp.int32)
    partial = attend_project(pos, queries, own, oth, out_weight, 8)
    pos2 = jnp.stack([x_at, y_at, z_at, core]).astype(jnp.int32)
    partial, gate_raw, up_raw = lax.optimization_barrier((partial, gate_weight.T, up_weight.T))
    terms = lax.all_to_all(partial, HEAD, 0, 0, tiled=True)
    km, ks, sm, ss = prepare(pos2, gate_raw, up_raw, norm_gain[None, :])
    weights = [jnp.concatenate([k, swap_core(t)], 1) for k, t in ((km, sm), (ks, ss))]
    terms, weights = lax.optimization_barrier((terms, weights))
    hidden = (residual.astype(F32) + jnp.sum(terms.astype(F32), axis=0)).astype(BF)

    keep = jnp.where(core == 0, hidden[:, :512], hidden[:, 512:])
    got = swap_core(jnp.where(core == 0, hidden[:, 512:], hidden[:, :512]))
    chip = jnp.where(core == 0, jnp.concatenate([keep, got], 0), jnp.concatenate([got, keep], 0))
    main, side = gather((chip[:, :MCOLS], chip[:, MCOLS:]), (MAIN, SIDE))
    sums = gate_up(pos2, (0,), main, side, weights, None, "first")
    sums = gate_up(pos2, (1, 2), main, side, weights, sums, "middle")
    own_ss, theirs = gate_up(pos2, (3,), main, side, weights, sums, "theirs")
    got = swap_core(theirs)
    own_sums = gate_up(pos2, (3,), main, side, weights, sums, "mine")
    out = finish(own_sums, own_ss, got, norm_gain.shape[0])
    return out.T, hidden


def solution(mesh):
    devices = mesh.devices.reshape(4, 2, 2, 4, 2)
    fine = Mesh(devices, MESH)
    both = P(SEQ, HEAD)
    cols = P(None, SEQ + HEAD)
    return jax.shard_map(
        per_device,
        mesh=fine,
        in_specs=(both, both, both, P(HEAD, None), both, P(), cols, cols),
        out_specs=(cols, both),
        check_vma=False,
    )
```

```python
import functools
import math

import jax
import jax.numpy as jnp
from jax import lax
from jax.experimental import pallas as pl
from jax.experimental.pallas import tpu as pltpu
from jax.sharding import Mesh, PartitionSpec as P


HD = 128
LOW = -1e30
EPS = 1e-5
SEQ = ("y", "xh", "c")
HEAD = ("z", "xl")
MESH = ("y", "xh", "c", "z", "xl")
MAIN = ("yzx", "zxy")
SIDE = ("xyz", "xyz")
OFFSETS = (0, -1, 1, 2)
MCOLS, SCOLS = 384, 128
BF = jnp.bfloat16
F32 = jnp.float32


def move(x, axes, by):
    pairs = []
    for core in range(2):
        if axes[core] is None:
            continue
        for n in range(64):
            at = {"x": n // 16, "y": n // 4 % 4, "z": n % 4}
            to = dict(at)
            if axes[core] == "p":
                to["x"] ^= 1
            else:
                to[axes[core]] = (to[axes[core]] + by[core]) % 4
            pairs.append(tuple(
                (((p["y"] * 2 + p["x"] // 2) * 2 + core) * 4 + p["z"]) * 2 + p["x"] % 2
                for p in (at, to)
            ))
    return lax.ppermute(x, MESH, pairs)


def shift(x, axes, by):
    return move(x, axes, (by, by))


def swap_core(x):
    return lax.ppermute(x, "c", [(0, 1), (1, 0)])


def attend_kernel(pos_ref, q_ref, own_ref, oth_ref, w_hbm, *refs):
    outs, (w_buf, qs, acc, att, sems) = refs[:4], refs[4:]
    blocks = w_buf.shape[0]
    width = w_buf.shape[2]
    for b in range(blocks):
        at = pl.multiple_of(pos_ref[2 + b] * width, width)
        pltpu.make_async_copy(w_hbm.at[:, pl.ds(at, width)], w_buf.at[b], sems.at[b]).start()
    heads = q_ref.shape[1] // HD
    rows = q_ref.shape[0]
    cols = heads * rows
    for h in range(heads):
        qs[pl.ds(h * rows, rows), :] = q_ref[:, h * HD:(h + 1) * HD]
    group = pos_ref[0]
    core = pos_ref[1]
    factor = math.log2(math.e) / math.sqrt(HD)
    qv = qs[...]

    def scores(ref, g):
        return lax.dot_general(
            ref[g, :, :HD], qv, (((1,), (1,)), ((), ())), preferred_element_type=F32
        ) * factor

    def weigh(ref, g, p):
        return lax.dot_general(
            ref[g, :, HD:], p.astype(BF), (((0,), (0,)), ((), ())), preferred_element_type=F32
        )

    key_at = lax.broadcasted_iota(jnp.int32, (rows, cols), 0)
    row_at = lax.broadcasted_iota(jnp.int32, (rows, cols), 1) % rows
    s1 = jnp.where(key_at <= row_at, scores(own_ref, group), LOW)
    s2 = jnp.where(core == 1, scores(oth_ref, group), LOW)
    top = jnp.maximum(jnp.max(s1, axis=0, keepdims=True), jnp.max(s2, axis=0, keepdims=True))
    p1 = jnp.exp2(s1 - top)
    p2 = jnp.where(core == 1, jnp.exp2(s2 - top), 0.0)
    total = jnp.sum(p1, axis=0, keepdims=True) + jnp.sum(p2, axis=0, keepdims=True)
    acc[...] = weigh(own_ref, group, p1) + weigh(oth_ref, group, p2)

    def step(g, carry):
        top, total = carry
        s1 = scores(own_ref, g)
        s2 = scores(oth_ref, g)
        new = jnp.maximum(
            top, jnp.maximum(jnp.max(s1, axis=0, keepdims=True), jnp.max(s2, axis=0, keepdims=True))
        )
        alpha = jnp.exp2(top - new)
        p1 = jnp.exp2(s1 - new)
        p2 = jnp.exp2(s2 - new)
        total = total * alpha + jnp.sum(p1, axis=0, keepdims=True) + jnp.sum(p2, axis=0, keepdims=True)
        acc[...] = acc[...] * alpha + weigh(own_ref, g, p1) + weigh(oth_ref, g, p2)
        return new, total

    top, total = lax.fori_loop(0, group, step, (top, total))
    final = acc[...] / total
    for h in range(heads):
        att[:, h * HD:(h + 1) * HD] = final[:, h * rows:(h + 1) * rows].T.astype(BF)

    for j, out_ref in enumerate(outs):

        def project(i, _, j=j, out_ref=out_ref):
            b = j * 2 + i
            pltpu.make_async_copy(w_hbm.at[:, pl.ds(0, width)], w_buf.at[b], sems.at[b]).wait()
            out_ref[i] = jnp.dot(att[...], w_buf[b], preferred_element_type=F32).astype(BF)
            return 0

        lax.fori_loop(0, 2, project, 0)


def attend_project(pos, q, own, oth, w, blocks):
    rows, cols = q.shape
    depth, wide = w.shape
    width = wide // blocks
    vm = pl.BlockSpec(memory_space=pltpu.VMEM)
    return pl.pallas_call(
        attend_kernel,
        out_shape=[jax.ShapeDtypeStruct((2, rows, width), BF)] * 4,
        in_specs=[pl.BlockSpec(memory_space=pltpu.SMEM), vm, vm, vm, pl.BlockSpec(memory_space=pl.ANY)],
        out_specs=[vm] * 4,
        scratch_shapes=[
            pltpu.VMEM((blocks, depth, width), BF),
            pltpu.VMEM((rows * cols // HD, HD), BF),
            pltpu.VMEM((HD, rows * cols // HD), F32),
            pltpu.VMEM((rows, cols), BF),
            pltpu.SemaphoreType.DMA((blocks,)),
        ],
        compiler_params=pltpu.CompilerParams(vmem_limit_bytes=48 << 20),
        cost_estimate=pl.CostEstimate(flops=4 << 30, bytes_accessed=20 << 20, transcendentals=2 << 20),
        name="attend_project",
    )(pos, q, own, oth, w)


def middle_kernel(pos_ref, third, keep, r1, r2, r3, b1, b2, b3, mine, buf):
    z_at, xl = pos_ref[2], pos_ref[0] & 1

    @pl.when(pos_ref[3] == 0)
    def _():
        for i, (kept, got) in enumerate(((third, r1), (keep, r2))):
            for j in range(2):
                buf[2 * i + j] = kept[j].astype(F32) + got[j].astype(F32)
        for ref, off in ((b1, 1), (b2, 3), (b3, 2)):
            ref[...] = buf[(z_at + off) & 3].astype(BF)
        mine[...] = buf[z_at]

    @pl.when(pos_ref[3] != 0)
    def _():
        for j in range(2):
            buf[j] = (
                keep[j].astype(F32) + r1[j].astype(F32) + r2[j].astype(F32) + r3[j].astype(F32)
            )
        b1[...] = buf[1 - xl].astype(BF)
        mine[...] = buf[xl]


def middle(pos, *pieces):
    rows, cols = pieces[0].shape[1:]
    vm = pl.BlockSpec(memory_space=pltpu.VMEM)
    part = jax.ShapeDtypeStruct((rows, cols), BF)
    return pl.pallas_call(
        middle_kernel,
        out_shape=[part, part, part, jax.ShapeDtypeStruct((rows, cols), F32)],
        in_specs=[pl.BlockSpec(memory_space=pltpu.SMEM)] + [vm] * 5,
        out_specs=[vm] * 4,
        scratch_shapes=[pltpu.VMEM((4, rows, cols), F32)],
        compiler_params=pltpu.CompilerParams(vmem_limit_bytes=16 << 20),
        cost_estimate=pl.CostEstimate(flops=1 << 20, bytes_accessed=4 << 20, transcendentals=0),
        name="middle",
    )(pos, *pieces)


def prep_kernel(pos_ref, g_ref, u_ref, gain_ref, km_ref, ks_ref, sm_ref, ss_ref):
    first = pos_ref[3] == 0
    n = g_ref.shape[0]
    gain = gain_ref[...]
    for j, ref in enumerate((g_ref, u_ref)):
        scaled = (ref[...].astype(F32) * gain).astype(BF)
        low, high = scaled[:, :512], scaled[:, 512:]
        keep = jnp.where(first, low, high)
        send = jnp.where(first, high, low)
        rows = pl.ds(j * n, n)
        km_ref[0, rows, :] = keep[:, :MCOLS]
        ks_ref[0, rows, :] = keep[:, MCOLS:]
        sm_ref[0, rows, :] = send[:, :MCOLS]
        ss_ref[0, rows, :] = send[:, MCOLS:]


def prepare(pos, gate_t, up_t, gain):
    n, depth = gate_t.shape
    wspec = pl.BlockSpec((n, 1024), lambda i, pos: (0, i))
    mspec = pl.BlockSpec((1, 2 * n, MCOLS), lambda i, pos: (i % 2, 0, i // 2))
    sspec = pl.BlockSpec((1, 2 * n, SCOLS), lambda i, pos: (i // 2, 0, i % 2))
    mshape = jax.ShapeDtypeStruct((2, 2 * n, 4 * MCOLS), BF)
    sshape = jax.ShapeDtypeStruct((4, 2 * n, 2 * SCOLS), BF)
    return pl.pallas_call(
        prep_kernel,
        out_shape=[mshape, sshape, mshape, sshape],
        grid_spec=pltpu.PrefetchScalarGridSpec(
            num_scalar_prefetch=1,
            grid=(depth // 1024,),
            in_specs=[wspec, wspec, pl.BlockSpec((1, 1024), lambda i, pos: (0, i))],
            out_specs=[mspec, sspec, mspec, sspec],
        ),
        compiler_params=pltpu.CompilerParams(vmem_limit_bytes=58 << 20),
        cost_estimate=pl.CostEstimate(flops=8 << 20, bytes_accessed=15 << 20, transcendentals=0),
        name="prepare",
    )(pos, gate_t, up_t, gain)


def gate_kernel(which, stage, pos_ref, *refs):
    count = len(which)
    refs = list(refs)
    first = stage == "first"
    last = stage in ("theirs", "mine")
    if stage != "mine":
        main = {c: tuple(refs.pop(0) for _ in range(3)) for c in which}
        side = {c: (refs.pop(0), refs.pop(0)) for c in which}
    if first:
        halves = [refs.pop(0) for _ in range(4)]
        acc, wm, ws = (refs.pop(0) for _ in range(3))
        wsem = refs.pop()
        n2 = halves[0].shape[1]
        for j, src in enumerate(halves):
            pltpu.make_async_copy(
                src, (wm, ws)[j // 2].at[:, pl.ds((j % 2) * n2, n2), :], wsem.at[j // 2]
            ).start()
    else:
        wm, ws, before = (refs.pop(0) for _ in range(3))
    if stage == "theirs":
        own_ss, par_ref, hm, hs = (refs.pop(0) for _ in range(4))
    elif stage == "mine":
        hm, hs, own_ref = (refs.pop(0) for _ in range(3))
    elif stage == "middle":
        acc = refs.pop(0)
    if last:
        acc = refs.pop()
    if not last:
        hm, hs = refs.pop(0), refs.pop(0)
    ssq, table, msem, ssem = refs
    x_at, y_at, z_at, core = (pos_ref[m] for m in range(4))
    both = wm.shape[1]
    n2 = both // 2
    lead = n2 if stage == "theirs" else 0
    rows = n2 if last else both
    squared = stage != "mine"

    def at(base, slot):
        return (base + OFFSETS[slot] + 4) & 3

    def fetch(u, c, j, on):
        for k in range(4):
            a, b = (j, k) if on == 0 else (k, j)
            col = pl.multiple_of(at(z_at, k) * MCOLS, MCOLS)
            src = main[c][max(b - 1, 0)].at[(b % 2) * 4 + a if b < 2 else a]
            pltpu.make_async_copy(src, hm.at[u, :, pl.ds(col, MCOLS)], msem.at[u]).start()

    for m, c in enumerate(which):
        for j in range(4):
            u = m * 4 + j
            x = jnp.where(core == 0, at(x_at, c), at(x_at, j))
            y = jnp.where(core == 0, at(y_at, j), at(y_at, c))
            table[2 * u] = y * 2 + x // 2
            table[2 * u + 1] = x & 1
            if stage == "mine":
                continue
            pl.when(core == 0)(functools.partial(fetch, u, c, j, 0))
            pl.when(core != 0)(functools.partial(fetch, u, c, j, 1))
    for m, c in enumerate(which if stage != "mine" else ()):
        for b in range(4):
            for a in range(4):
                x = at(x_at, a)
                row = pl.multiple_of((at(y_at, b) * 2 + x // 2) * 256, 256)
                col = pl.multiple_of((x & 1) * SCOLS, SCOLS)
                pltpu.make_async_copy(
                    side[c][b // 2].at[(b % 2) * 4 + a],
                    hs.at[m, pl.ds(row, 256), pl.ds(col, SCOLS)],
                    ssem.at[m],
                ).start()
    if first or last:
        acc[...] = jnp.zeros_like(acc)
    if squared:
        ssq[...] = jnp.zeros_like(ssq)
    ones = jnp.ones((8, 128), BF)

    def squares(block):
        part = jnp.zeros((block.shape[0], 128), F32)
        for j in range(block.shape[1] // 128):
            wide = block[:, j * 128:(j + 1) * 128].astype(F32)
            part = part + wide * wide
        return part

    def lane_sums(part):
        big = part.astype(BF)
        small = (part - big.astype(F32)).astype(BF)
        return sum(
            lax.dot_general(ones, t, (((1,), (1,)), ((), ())), preferred_element_type=F32)
            for t in (big, small)
        )

    def unit(u, _):
        if stage != "mine":
            pltpu.make_async_copy(hm.at[u], hm.at[u], msem.at[u]).wait()
        cols = pl.ds(pl.multiple_of(table[2 * u] * 256, 256), 256)
        block = hm[u]
        acc[:rows, cols] += lax.dot_general(
            wm[table[2 * u + 1], pl.ds(lead, rows), :], block, (((1,), (1,)), ((), ())),
            preferred_element_type=F32,
        )
        if squared:
            ssq[cols, :] += squares(block)
        return 0

    if first:
        pltpu.make_async_copy(wm, wm, wsem.at[0]).wait()
    lax.fori_loop(0, 4 * count, unit, 0)
    if first:
        pltpu.make_async_copy(ws, ws, wsem.at[1]).wait()
    for m in range(count if stage != "mine" else 0):
        pltpu.make_async_copy(hs.at[m], hs.at[m], ssem.at[m]).wait()
    piece = 512

    def tail(p, _):
        cols = pl.ds(pl.multiple_of(p * piece, piece), piece)
        total = acc[:rows, cols]
        if last:
            total = total + before[pl.ds(lead, rows), cols]
        part = ssq[cols, :] if squared else None
        for m, c in enumerate(which):
            block = hs[m, cols, :]
            total = total + lax.dot_general(
                ws[at(z_at, c), pl.ds(lead, rows), :], block, (((1,), (1,)), ((), ())),
                preferred_element_type=F32,
            )
            if squared:
                part = part + squares(block)
        if squared:
            sq = (before if last else acc)[both:, cols] + lane_sums(part)
        if stage == "theirs":
            par_ref[:n2, cols] = total.astype(BF)
            own_ss[:, cols] = sq
            big = sq.astype(BF)
            par_ref[n2:, cols] = jnp.concatenate(
                [big.astype(F32), sq - big.astype(F32)], axis=0
            ).astype(BF)
        elif stage == "mine":
            own_ref[:, cols] = total
        else:
            acc[:rows, cols] = total
            acc[rows:, cols] = sq
        return 0

    lax.fori_loop(0, hs.shape[1] // piece, tail, 0)


def gate_up(pos, which, pieces, weights, held, stage):
    n2 = weights[0].shape[1] // (1 if stage == "first" else 2)
    tokens = 2048
    count = len(which)
    any_spec = pl.BlockSpec(memory_space=pl.ANY)
    vm = pl.BlockSpec(memory_space=pltpu.VMEM)
    loose = list(pieces) + (list(weights) if stage == "first" else [])
    fixed = ([] if stage == "first" else list(weights)) + list(held)
    blocks = [
        jax.ShapeDtypeStruct((4 * count, 256, 4 * MCOLS), BF),
        jax.ShapeDtypeStruct((count, tokens, 2 * SCOLS), BF),
    ]
    partial = jax.ShapeDtypeStruct((2 * n2 + 8, tokens), F32)
    out_shape = {
        "first": [
            partial,
            jax.ShapeDtypeStruct((2, 2 * n2, 4 * MCOLS), BF),
            jax.ShapeDtypeStruct((4, 2 * n2, 2 * SCOLS), BF),
        ],
        "middle": [partial],
        "theirs": [
            jax.ShapeDtypeStruct((8, tokens), F32),
            jax.ShapeDtypeStruct((n2 + 16, tokens), BF),
        ] + blocks,
        "mine": [jax.ShapeDtypeStruct((n2, tokens), F32)],
    }[stage]
    last = stage in ("theirs", "mine")
    scratch = [] if last else [pltpu.VMEM(t.shape, BF) for t in blocks]
    scratch += [
        pltpu.VMEM((tokens, 128), F32),
        pltpu.SMEM((8 * count,), jnp.int32),
        pltpu.SemaphoreType.DMA((4 * count,)),
        pltpu.SemaphoreType.DMA((count,)),
    ]
    if stage == "first":
        scratch.append(pltpu.SemaphoreType.DMA((2,)))
    if last:
        scratch.append(pltpu.VMEM((n2, tokens), F32))
    return pl.pallas_call(
        functools.partial(gate_kernel, which, stage),
        out_shape=out_shape,
        in_specs=[pl.BlockSpec(memory_space=pltpu.SMEM)]
        + [any_spec] * len(loose)
        + [vm] * len(fixed),
        out_specs=[vm] * len(out_shape),
        scratch_shapes=scratch,
        input_output_aliases={len(loose) + len(fixed): 0} if stage == "middle" else {},
        compiler_params=pltpu.CompilerParams(vmem_limit_bytes=(10 + 8 * count) << 20),
        cost_estimate=pl.CostEstimate(
            flops=count * n2 * tokens * 4096, bytes_accessed=20 << 20, transcendentals=0
        ),
        name="gate_up",
    )(pos, *loose, *fixed)


def finish_kernel(own_ref, ss_ref, got_ref, out_ref, buf, sems, *, depth):
    n = buf.shape[0]
    piece = 512

    def put(p):
        cols = pl.ds(p * piece, piece)
        return pltpu.make_async_copy(buf.at[:, cols], out_ref.at[:, cols], sems.at[p])

    for p in range(buf.shape[1] // piece):
        cols = pl.ds(p * piece, piece)
        got = got_ref[:, cols].astype(F32)
        total = ss_ref[:1, cols] + got[2 * n:2 * n + 1] + got[2 * n + 8:2 * n + 9]
        scale = lax.rsqrt(total / depth + EPS)
        gate = (own_ref[:n, cols] + got[:n]) * scale
        up = (own_ref[n:, cols] + got[n:2 * n]) * scale
        buf[:, cols] = (gate / (1.0 + jnp.exp(-gate)) * up).astype(BF)
        put(p).start()
    for p in range(buf.shape[1] // piece):
        put(p).wait()


def finish(own, ss, got, depth):
    rows, tokens = own.shape
    n = rows // 2
    vm = pl.BlockSpec(memory_space=pltpu.VMEM)
    return pl.pallas_call(
        functools.partial(finish_kernel, depth=depth),
        out_shape=jax.ShapeDtypeStruct((n, tokens), BF),
        in_specs=[vm] * 3,
        out_specs=pl.BlockSpec(memory_space=pl.ANY),
        scratch_shapes=[pltpu.VMEM((n, tokens), BF), pltpu.SemaphoreType.DMA((tokens // 512,))],
        compiler_params=pltpu.CompilerParams(vmem_limit_bytes=16 << 20),
        cost_estimate=pl.CostEstimate(flops=8 << 20, bytes_accessed=7 << 20, transcendentals=1 << 20),
        name="finish",
    )(own, ss, got)


def gather(blocks, orders):
    axes = [[(o[0][p], o[1][p]) for p in range(3)] for o in orders]

    def around(block, a):
        return [shift(block, a, by) for by in (1, -1, 2)]

    main_near = around(blocks[0], axes[0][0])
    side_near = around(blocks[1], axes[1][0])
    main_near = lax.optimization_barrier([blocks[0]] + main_near)
    cur_main = lax.optimization_barrier(jnp.stack(main_near))
    ahead = shift(cur_main, axes[0][1], 1)
    third, fourth = (shift(cur_main, axes[0][1], by) for by in (-1, 2))
    side_near = lax.optimization_barrier([blocks[1]] + side_near)
    cur_side = lax.optimization_barrier(jnp.stack(side_near))
    side_next = around(cur_side, axes[1][1])

    def both_ways(block, a):
        return shift(block, a[2], 1), shift(block, a[2], -1)

    low = jnp.concatenate([cur_main, ahead], 0)
    low = lax.optimization_barrier(low)
    lows = both_ways(low, axes[0])
    thirds = both_ways(third, axes[0])
    fourths = both_ways(fourth, axes[0])
    side_low = jnp.concatenate([cur_side, side_next[0]], 0)
    side_high = jnp.concatenate(side_next[1:], 0)
    side_low, side_high = lax.optimization_barrier((side_low, side_high))
    side_lows = both_ways(side_low, axes[1])
    side_highs = both_ways(side_high, axes[1])
    far_low = shift(lows[0], axes[0][2], 1)
    far_side = (shift(side_lows[0], axes[1][2], 1), shift(side_highs[1], axes[1][2], -1))
    far_third = shift(thirds[1], axes[0][2], -1)
    far_fourth = shift(fourths[1], axes[0][2], -1)
    main = {
        0: (low, third, fourth),
        1: (lows[0], thirds[0], fourths[0]),
        2: (lows[1], thirds[1], fourths[1]),
        3: (far_low, far_third, far_fourth),
    }
    side = {
        0: (side_low, side_high),
        1: (side_lows[0], side_highs[0]),
        2: (side_lows[1], side_highs[1]),
        3: far_side,
    }
    return main, side


def per_device(queries, key_rows, value_rows, out_weight, residual, norm_gain, gate_weight, up_weight):
    y_at, xh, core = lax.axis_index("y"), lax.axis_index("xh"), lax.axis_index("c")
    z_at, xl = lax.axis_index("z"), lax.axis_index("xl")
    x_at = xh * 2 + xl
    group = y_at * 2 + xh

    pair = jnp.concatenate([key_rows, value_rows], axis=1)
    spread = jnp.broadcast_to(pair[None], (8,) + pair.shape)
    own = lax.all_to_all(spread, ("y", "xh"), 0, 0, tiled=True)
    oth = swap_core(own)

    pos2 = jnp.stack([x_at, y_at, z_at, core]).astype(jnp.int32)
    slots = [
        jnp.where(core == 0, p * 2 + q, ((z_at + r) & 3) * 2 + t)
        for p, q, r, t in zip(
            (0, 1, 2, 3) * 2, [1 - xl] * 4 + [xl] * 4, (1, 1, 3, 3, 2, 2, 0, 0), (0, 1) * 4
        )
    ]
    pos = jnp.stack([group, core] + slots).astype(jnp.int32)
    first, second, third, keep = attend_project(pos, queries, own, oth, out_weight, 8)
    first, second, third, keep, gate_raw, up_raw = lax.optimization_barrier(
        (first, second, third, keep, gate_weight.T, up_weight.T)
    )
    r1 = move(first, ("p", "z"), (0, 1))
    r2 = move(second, ("p", "z"), (0, -1))
    r3 = move(third, (None, "z"), (0, 2))
    km, ks, sm, ss = prepare(pos2, gate_raw, up_raw, norm_gain[None, :])
    b1, b2, b3, mine = middle(pos2, third, keep, r1, r2, r3)
    terms = [
        move(b1, ("z", "p"), (1, 0)),
        move(b2, ("z", None), (-1, 0)),
        move(b3, ("z", None), (2, 0)),
    ]
    terms, gm, gs = lax.optimization_barrier((terms, swap_core(sm), swap_core(ss)))
    total = mine + sum(t.astype(F32) for t in terms)
    hidden = (residual.astype(F32) + total).astype(BF)

    keep = jnp.where(core == 0, hidden[:, :512], hidden[:, 512:])
    got = swap_core(jnp.where(core == 0, hidden[:, 512:], hidden[:, :512]))
    chip = jnp.where(core == 0, jnp.concatenate([keep, got], 0), jnp.concatenate([got, keep], 0))
    main, side = gather((chip[:, :MCOLS], chip[:, MCOLS:]), (MAIN, SIDE))

    def pieces(*slots):
        return [p for part in (main, side) for c in slots for p in part[c]]

    sums, wm, ws = gate_up(pos2, (0,), pieces(0), (km, gm, ks, gs), (), "first")
    sums, = gate_up(pos2, (1, 2), pieces(1, 2), (wm, ws), (sums,), "middle")
    own_ss, theirs, hm, hs = gate_up(pos2, (3,), pieces(3), (wm, ws), (sums,), "theirs")
    got = swap_core(theirs)
    own_sums, = gate_up(pos2, (3,), (), (wm, ws), (sums, hm, hs), "mine")
    out = finish(own_sums, own_ss, got, norm_gain.shape[0])
    return out.T, hidden


def solution(mesh):
    devices = mesh.devices.reshape(4, 2, 2, 4, 2)
    fine = Mesh(devices, MESH)
    both = P(SEQ, HEAD)
    cols = P(None, SEQ + HEAD)
    return jax.shard_map(
        per_device,
        mesh=fine,
        in_specs=(both, both, both, P(HEAD, None), both, P(), cols, cols),
        out_specs=(cols, both),
        check_vma=False,
    )
```

```python
import functools
import math

import jax
import jax.numpy as jnp
from jax import lax
from jax.experimental import pallas as pl
from jax.experimental.pallas import tpu as pltpu
from jax.sharding import Mesh, PartitionSpec as P


HD = 128
LOW = -1e30
EPS = 1e-5
SEQ = ("y", "xh", "c")
HEAD = ("z", "xl")
MESH = ("y", "xh", "c", "z", "xl")
MAIN = ("yzx", "zxy")
SIDE = ("xyz", "xyz")
OFFSETS = (0, -1, 1, 2)
MCOLS, SCOLS = 384, 128
BF = jnp.bfloat16
F32 = jnp.float32


def move(x, axes, by):
    pairs = []
    for core in range(2):
        if axes[core] is None:
            continue
        for n in range(64):
            at = {"x": n // 16, "y": n // 4 % 4, "z": n % 4}
            to = dict(at)
            if axes[core] == "p":
                to["x"] ^= 1
            else:
                to[axes[core]] = (to[axes[core]] + by[core]) % 4
            pairs.append(tuple(
                (((p["y"] * 2 + p["x"] // 2) * 2 + core) * 4 + p["z"]) * 2 + p["x"] % 2
                for p in (at, to)
            ))
    return lax.ppermute(x, MESH, pairs)


def shift(x, axes, by):
    return move(x, axes, (by, by))


def swap_core(x):
    return lax.ppermute(x, "c", [(0, 1), (1, 0)])


def attend_kernel(pos_ref, q_ref, own_ref, oth_ref, w_hbm, *refs):
    outs, (w_buf, qs, acc, att, sems) = refs[:4], refs[4:]
    blocks = w_buf.shape[0]
    width = w_buf.shape[2]
    for b in range(blocks):
        at = pl.multiple_of(pos_ref[2 + b] * width, width)
        pltpu.make_async_copy(w_hbm.at[:, pl.ds(at, width)], w_buf.at[b], sems.at[b]).start()
    heads = q_ref.shape[1] // HD
    rows = q_ref.shape[0]
    cols = heads * rows
    for h in range(heads):
        qs[pl.ds(h * rows, rows), :] = q_ref[:, h * HD:(h + 1) * HD]
    group = pos_ref[0]
    core = pos_ref[1]
    factor = math.log2(math.e) / math.sqrt(HD)
    qv = qs[...]

    def scores(ref, g):
        return lax.dot_general(
            ref[g, :, :HD], qv, (((1,), (1,)), ((), ())), preferred_element_type=F32
        ) * factor

    def weigh(ref, g, p):
        return lax.dot_general(
            ref[g, :, HD:], p.astype(BF), (((0,), (0,)), ((), ())), preferred_element_type=F32
        )

    key_at = lax.broadcasted_iota(jnp.int32, (rows, cols), 0)
    row_at = lax.broadcasted_iota(jnp.int32, (rows, cols), 1) % rows
    s1 = jnp.where(key_at <= row_at, scores(own_ref, group), LOW)
    s2 = jnp.where(core == 1, scores(oth_ref, group), LOW)
    top = jnp.maximum(jnp.max(s1, axis=0, keepdims=True), jnp.max(s2, axis=0, keepdims=True))
    p1 = jnp.exp2(s1 - top)
    p2 = jnp.where(core == 1, jnp.exp2(s2 - top), 0.0)
    total = jnp.sum(p1, axis=0, keepdims=True) + jnp.sum(p2, axis=0, keepdims=True)
    acc[...] = weigh(own_ref, group, p1) + weigh(oth_ref, group, p2)

    def step(g, carry):
        top, total = carry
        s1 = scores(own_ref, g)
        s2 = scores(oth_ref, g)
        new = jnp.maximum(
            top, jnp.maximum(jnp.max(s1, axis=0, keepdims=True), jnp.max(s2, axis=0, keepdims=True))
        )
        alpha = jnp.exp2(top - new)
        p1 = jnp.exp2(s1 - new)
        p2 = jnp.exp2(s2 - new)
        total = total * alpha + jnp.sum(p1, axis=0, keepdims=True) + jnp.sum(p2, axis=0, keepdims=True)
        acc[...] = acc[...] * alpha + weigh(own_ref, g, p1) + weigh(oth_ref, g, p2)
        return new, total

    top, total = lax.fori_loop(0, group, step, (top, total))
    final = acc[...] / total
    for h in range(heads):
        att[:, h * HD:(h + 1) * HD] = final[:, h * rows:(h + 1) * rows].T.astype(BF)

    for j, out_ref in enumerate(outs):

        def project(i, _, j=j, out_ref=out_ref):
            b = j * 2 + i
            pltpu.make_async_copy(w_hbm.at[:, pl.ds(0, width)], w_buf.at[b], sems.at[b]).wait()
            out_ref[i] = jnp.dot(att[...], w_buf[b], preferred_element_type=F32).astype(BF)
            return 0

        lax.fori_loop(0, 2, project, 0)


def attend_project(pos, q, own, oth, w, blocks):
    rows, cols = q.shape
    depth, wide = w.shape
    width = wide // blocks
    vm = pl.BlockSpec(memory_space=pltpu.VMEM)
    return pl.pallas_call(
        attend_kernel,
        out_shape=[jax.ShapeDtypeStruct((2, rows, width), BF)] * 4,
        in_specs=[pl.BlockSpec(memory_space=pltpu.SMEM), vm, vm, vm, pl.BlockSpec(memory_space=pl.ANY)],
        out_specs=[vm] * 4,
        scratch_shapes=[
            pltpu.VMEM((blocks, depth, width), BF),
            pltpu.VMEM((rows * cols // HD, HD), BF),
            pltpu.VMEM((HD, rows * cols // HD), F32),
            pltpu.VMEM((rows, cols), BF),
            pltpu.SemaphoreType.DMA((blocks,)),
        ],
        compiler_params=pltpu.CompilerParams(vmem_limit_bytes=48 << 20),
        cost_estimate=pl.CostEstimate(flops=4 << 30, bytes_accessed=20 << 20, transcendentals=2 << 20),
        name="attend_project",
    )(pos, q, own, oth, w)


def middle_kernel(pos_ref, third, keep, r1, r2, r3, b1, b2, b3, mine, buf):
    z_at, xl = pos_ref[2], pos_ref[0] & 1

    @pl.when(pos_ref[3] == 0)
    def _():
        for i, (kept, got) in enumerate(((third, r1), (keep, r2))):
            for j in range(2):
                buf[2 * i + j] = kept[j].astype(F32) + got[j].astype(F32)
        for ref, off in ((b1, 1), (b2, 3), (b3, 2)):
            ref[...] = buf[(z_at + off) & 3].astype(BF)
        mine[...] = buf[z_at]

    @pl.when(pos_ref[3] != 0)
    def _():
        for j in range(2):
            buf[j] = (
                keep[j].astype(F32) + r1[j].astype(F32) + r2[j].astype(F32) + r3[j].astype(F32)
            )
        b1[...] = buf[1 - xl].astype(BF)
        mine[...] = buf[xl]


def middle(pos, *pieces):
    rows, cols = pieces[0].shape[1:]
    vm = pl.BlockSpec(memory_space=pltpu.VMEM)
    part = jax.ShapeDtypeStruct((rows, cols), BF)
    return pl.pallas_call(
        middle_kernel,
        out_shape=[part, part, part, jax.ShapeDtypeStruct((rows, cols), F32)],
        in_specs=[pl.BlockSpec(memory_space=pltpu.SMEM)] + [vm] * 5,
        out_specs=[vm] * 4,
        scratch_shapes=[pltpu.VMEM((4, rows, cols), F32)],
        compiler_params=pltpu.CompilerParams(vmem_limit_bytes=16 << 20),
        cost_estimate=pl.CostEstimate(flops=1 << 20, bytes_accessed=4 << 20, transcendentals=0),
        name="middle",
    )(pos, *pieces)


def prep_kernel(pos_ref, g_ref, u_ref, gain_ref, km_ref, ks_ref, sm_ref, ss_ref):
    first = pos_ref[3] == 0
    n = g_ref.shape[0]
    gain = gain_ref[...]
    for j, ref in enumerate((g_ref, u_ref)):
        scaled = (ref[...].astype(F32) * gain).astype(BF)
        low, high = scaled[:, :512], scaled[:, 512:]
        keep = jnp.where(first, low, high)
        send = jnp.where(first, high, low)
        rows = pl.ds(j * n, n)
        km_ref[0, rows, :] = keep[:, :MCOLS]
        ks_ref[0, rows, :] = keep[:, MCOLS:]
        sm_ref[0, rows, :] = send[:, :MCOLS]
        ss_ref[0, rows, :] = send[:, MCOLS:]


def prepare(pos, gate_t, up_t, gain):
    n, depth = gate_t.shape
    wspec = pl.BlockSpec((n, 1024), lambda i, pos: (0, i))
    mspec = pl.BlockSpec((1, 2 * n, MCOLS), lambda i, pos: (i % 2, 0, i // 2))
    sspec = pl.BlockSpec((1, 2 * n, SCOLS), lambda i, pos: (i // 2, 0, i % 2))
    mshape = jax.ShapeDtypeStruct((2, 2 * n, 4 * MCOLS), BF)
    sshape = jax.ShapeDtypeStruct((4, 2 * n, 2 * SCOLS), BF)
    return pl.pallas_call(
        prep_kernel,
        out_shape=[mshape, sshape, mshape, sshape],
        grid_spec=pltpu.PrefetchScalarGridSpec(
            num_scalar_prefetch=1,
            grid=(depth // 1024,),
            in_specs=[wspec, wspec, pl.BlockSpec((1, 1024), lambda i, pos: (0, i))],
            out_specs=[mspec, sspec, mspec, sspec],
        ),
        compiler_params=pltpu.CompilerParams(vmem_limit_bytes=58 << 20),
        cost_estimate=pl.CostEstimate(flops=8 << 20, bytes_accessed=15 << 20, transcendentals=0),
        name="prepare",
    )(pos, gate_t, up_t, gain)


def gate_kernel(which, stage, pos_ref, *refs):
    count = len(which)
    refs = list(refs)
    first = stage == "first"
    last = stage in ("theirs", "mine")
    if stage != "mine":
        main = {c: tuple(refs.pop(0) for _ in range(3)) for c in which}
        side = {c: (refs.pop(0), refs.pop(0)) for c in which}
    if first:
        halves = [refs.pop(0) for _ in range(4)]
        acc, wm, ws = (refs.pop(0) for _ in range(3))
        wsem = refs.pop()
        n2 = halves[0].shape[1]
        for j, src in enumerate(halves):
            pltpu.make_async_copy(
                src, (wm, ws)[j // 2].at[:, pl.ds((j % 2) * n2, n2), :], wsem.at[j // 2]
            ).start()
    else:
        wm, ws, before = (refs.pop(0) for _ in range(3))
    if stage == "theirs":
        own_ss, par_ref, hm, hs = (refs.pop(0) for _ in range(4))
    elif stage == "mine":
        hm, hs, own_ref = (refs.pop(0) for _ in range(3))
    elif stage == "middle":
        acc = refs.pop(0)
    if last:
        acc = refs.pop()
    if not last:
        hm, hs = refs.pop(0), refs.pop(0)
    ssq, table, msem, ssem = refs
    x_at, y_at, z_at, core = (pos_ref[m] for m in range(4))
    both = wm.shape[1]
    n2 = both // 2
    lead = n2 if stage == "theirs" else 0
    rows = n2 if last else both
    squared = stage != "mine"

    def at(base, slot):
        return (base + OFFSETS[slot] + 4) & 3

    def fetch(u, c, j, on):
        for k in range(4):
            a, b = (j, k) if on == 0 else (k, j)
            col = pl.multiple_of(at(z_at, k) * MCOLS, MCOLS)
            src = main[c][max(b - 1, 0)].at[(b % 2) * 4 + a if b < 2 else a]
            pltpu.make_async_copy(src, hm.at[u, :, pl.ds(col, MCOLS)], msem.at[u]).start()

    for m, c in enumerate(which):
        for j in range(4):
            u = m * 4 + j
            x = jnp.where(core == 0, at(x_at, c), at(x_at, j))
            y = jnp.where(core == 0, at(y_at, j), at(y_at, c))
            table[2 * u] = y * 2 + x // 2
            table[2 * u + 1] = x & 1
            if stage == "mine":
                continue
            pl.when(core == 0)(functools.partial(fetch, u, c, j, 0))
            pl.when(core != 0)(functools.partial(fetch, u, c, j, 1))
    for m, c in enumerate(which if stage != "mine" else ()):
        for b in range(4):
            for a in range(4):
                x = at(x_at, a)
                row = pl.multiple_of((at(y_at, b) * 2 + x // 2) * 256, 256)
                col = pl.multiple_of((x & 1) * SCOLS, SCOLS)
                pltpu.make_async_copy(
                    side[c][b // 2].at[(b % 2) * 4 + a],
                    hs.at[m, pl.ds(row, 256), pl.ds(col, SCOLS)],
                    ssem.at[m],
                ).start()
    if first or last:
        acc[...] = jnp.zeros_like(acc)
    if squared:
        ssq[...] = jnp.zeros_like(ssq)
    ones = jnp.ones((8, 128), BF)

    def squares(block):
        part = jnp.zeros((block.shape[0], 128), F32)
        for j in range(block.shape[1] // 128):
            wide = block[:, j * 128:(j + 1) * 128].astype(F32)
            part = part + wide * wide
        return part

    def lane_sums(part):
        big = part.astype(BF)
        small = (part - big.astype(F32)).astype(BF)
        return sum(
            lax.dot_general(ones, t, (((1,), (1,)), ((), ())), preferred_element_type=F32)
            for t in (big, small)
        )

    def unit(u, _):
        if stage != "mine":
            pltpu.make_async_copy(hm.at[u], hm.at[u], msem.at[u]).wait()
        cols = pl.ds(pl.multiple_of(table[2 * u] * 256, 256), 256)
        block = hm[u]
        acc[:rows, cols] += lax.dot_general(
            wm[table[2 * u + 1], pl.ds(lead, rows), :], block, (((1,), (1,)), ((), ())),
            preferred_element_type=F32,
        )
        if squared:
            ssq[cols, :] += squares(block)
        return 0

    if first:
        pltpu.make_async_copy(wm, wm, wsem.at[0]).wait()
    lax.fori_loop(0, 4 * count, unit, 0)
    if first:
        pltpu.make_async_copy(ws, ws, wsem.at[1]).wait()
    for m in range(count if stage != "mine" else 0):
        pltpu.make_async_copy(hs.at[m], hs.at[m], ssem.at[m]).wait()
    piece = 512

    def tail(p, _):
        cols = pl.ds(pl.multiple_of(p * piece, piece), piece)
        total = acc[:rows, cols]
        if last:
            total = total + before[pl.ds(lead, rows), cols]
        part = ssq[cols, :] if squared else None
        for m, c in enumerate(which):
            block = hs[m, cols, :]
            total = total + lax.dot_general(
                ws[at(z_at, c), pl.ds(lead, rows), :], block, (((1,), (1,)), ((), ())),
                preferred_element_type=F32,
            )
            if squared:
                part = part + squares(block)
        if squared:
            sq = (before if last else acc)[both:, cols] + lane_sums(part)
        if stage == "theirs":
            par_ref[:n2, cols] = total.astype(BF)
            own_ss[:, cols] = sq
            big = sq.astype(BF)
            par_ref[n2:, cols] = jnp.concatenate(
                [big.astype(F32), sq - big.astype(F32)], axis=0
            ).astype(BF)
        elif stage == "mine":
            own_ref[:, cols] = total
        else:
            acc[:rows, cols] = total
            acc[rows:, cols] = sq
        return 0

    lax.fori_loop(0, hs.shape[1] // piece, tail, 0)


def gate_up(pos, which, pieces, weights, held, stage):
    n2 = weights[0].shape[1] // (1 if stage == "first" else 2)
    tokens = 2048
    count = len(which)
    any_spec = pl.BlockSpec(memory_space=pl.ANY)
    vm = pl.BlockSpec(memory_space=pltpu.VMEM)
    loose = list(pieces) + (list(weights) if stage == "first" else [])
    fixed = ([] if stage == "first" else list(weights)) + list(held)
    blocks = [
        jax.ShapeDtypeStruct((4 * count, 256, 4 * MCOLS), BF),
        jax.ShapeDtypeStruct((count, tokens, 2 * SCOLS), BF),
    ]
    partial = jax.ShapeDtypeStruct((2 * n2 + 8, tokens), F32)
    out_shape = {
        "first": [
            partial,
            jax.ShapeDtypeStruct((2, 2 * n2, 4 * MCOLS), BF),
            jax.ShapeDtypeStruct((4, 2 * n2, 2 * SCOLS), BF),
        ],
        "middle": [partial],
        "theirs": [
            jax.ShapeDtypeStruct((8, tokens), F32),
            jax.ShapeDtypeStruct((n2 + 16, tokens), BF),
        ] + blocks,
        "mine": [jax.ShapeDtypeStruct((n2, tokens), F32)],
    }[stage]
    last = stage in ("theirs", "mine")
    scratch = [] if last else [pltpu.VMEM(t.shape, BF) for t in blocks]
    scratch += [
        pltpu.VMEM((tokens, 128), F32),
        pltpu.SMEM((8 * count,), jnp.int32),
        pltpu.SemaphoreType.DMA((4 * count,)),
        pltpu.SemaphoreType.DMA((count,)),
    ]
    if stage == "first":
        scratch.append(pltpu.SemaphoreType.DMA((2,)))
    if last:
        scratch.append(pltpu.VMEM((n2, tokens), F32))
    return pl.pallas_call(
        functools.partial(gate_kernel, which, stage),
        out_shape=out_shape,
        in_specs=[pl.BlockSpec(memory_space=pltpu.SMEM)]
        + [any_spec] * len(loose)
        + [vm] * len(fixed),
        out_specs=[vm] * len(out_shape),
        scratch_shapes=scratch,
        input_output_aliases={len(loose) + len(fixed): 0} if stage == "middle" else {},
        compiler_params=pltpu.CompilerParams(vmem_limit_bytes=(10 + 8 * count) << 20),
        cost_estimate=pl.CostEstimate(
            flops=count * n2 * tokens * 4096, bytes_accessed=20 << 20, transcendentals=0
        ),
        name="gate_up",
    )(pos, *loose, *fixed)


def finish_kernel(own_ref, ss_ref, got_ref, out_ref, buf, sems, *, depth):
    n = buf.shape[0]
    piece = 512

    def put(p):
        cols = pl.ds(p * piece, piece)
        return pltpu.make_async_copy(buf.at[:, cols], out_ref.at[:, cols], sems.at[p])

    for p in range(buf.shape[1] // piece):
        cols = pl.ds(p * piece, piece)
        got = got_ref[:, cols].astype(F32)
        total = ss_ref[:1, cols] + got[2 * n:2 * n + 1] + got[2 * n + 8:2 * n + 9]
        scale = lax.rsqrt(total / depth + EPS)
        gate = (own_ref[:n, cols] + got[:n]) * scale
        up = (own_ref[n:, cols] + got[n:2 * n]) * scale
        buf[:, cols] = (gate / (1.0 + jnp.exp(-gate)) * up).astype(BF)
        put(p).start()
    for p in range(buf.shape[1] // piece):
        put(p).wait()


def finish(own, ss, got, depth):
    rows, tokens = own.shape
    n = rows // 2
    vm = pl.BlockSpec(memory_space=pltpu.VMEM)
    return pl.pallas_call(
        functools.partial(finish_kernel, depth=depth),
        out_shape=jax.ShapeDtypeStruct((n, tokens), BF),
        in_specs=[vm] * 3,
        out_specs=pl.BlockSpec(memory_space=pl.ANY),
        scratch_shapes=[pltpu.VMEM((n, tokens), BF), pltpu.SemaphoreType.DMA((tokens // 512,))],
        compiler_params=pltpu.CompilerParams(vmem_limit_bytes=16 << 20),
        cost_estimate=pl.CostEstimate(flops=8 << 20, bytes_accessed=7 << 20, transcendentals=1 << 20),
        name="finish",
    )(own, ss, got)


def gather(blocks, orders):
    axes = [[(o[0][p], o[1][p]) for p in range(3)] for o in orders]

    def around(block, a):
        return [shift(block, a, by) for by in (1, -1, 2)]

    main_near = around(blocks[0], axes[0][0])
    side_near = around(blocks[1], axes[1][0])
    main_near = lax.optimization_barrier([blocks[0]] + main_near)
    cur_main = jnp.stack(main_near)
    cur_main = lax.optimization_barrier(cur_main)
    ahead = shift(cur_main, axes[0][1], 1)
    third, fourth = (shift(cur_main, axes[0][1], by) for by in (-1, 2))
    side_near = lax.optimization_barrier([blocks[1]] + side_near)
    cur_side = jnp.stack(side_near)
    cur_side = lax.optimization_barrier(cur_side)
    side_next = around(cur_side, axes[1][1])

    def both_ways(block, a):
        return shift(block, a[2], 1), shift(block, a[2], -1)

    low = jnp.concatenate([cur_main, ahead], 0)
    low = lax.optimization_barrier(low)
    lows = both_ways(low, axes[0])
    thirds = both_ways(third, axes[0])
    fourths = both_ways(fourth, axes[0])
    side_low = jnp.concatenate([cur_side, side_next[0]], 0)
    side_high = jnp.concatenate(side_next[1:], 0)
    side_low, side_high = lax.optimization_barrier((side_low, side_high))
    side_lows = both_ways(side_low, axes[1])
    side_highs = both_ways(side_high, axes[1])
    far_low = shift(lows[0], axes[0][2], 1)
    far_side = (shift(side_lows[0], axes[1][2], 1), shift(side_highs[1], axes[1][2], -1))
    far_third = shift(thirds[1], axes[0][2], -1)
    far_fourth = shift(fourths[1], axes[0][2], -1)
    main = {
        0: (low, third, fourth),
        1: (lows[0], thirds[0], fourths[0]),
        2: (lows[1], thirds[1], fourths[1]),
        3: (far_low, far_third, far_fourth),
    }
    side = {
        0: (side_low, side_high),
        1: (side_lows[0], side_highs[0]),
        2: (side_lows[1], side_highs[1]),
        3: far_side,
    }
    return main, side


def per_device(queries, key_rows, value_rows, out_weight, residual, norm_gain, gate_weight, up_weight):
    y_at, xh, core = lax.axis_index("y"), lax.axis_index("xh"), lax.axis_index("c")
    z_at, xl = lax.axis_index("z"), lax.axis_index("xl")
    x_at = xh * 2 + xl
    group = y_at * 2 + xh

    pair = jnp.concatenate([key_rows, value_rows], axis=1)
    spread = jnp.broadcast_to(pair[None], (8,) + pair.shape)
    own = lax.all_to_all(spread, ("y", "xh"), 0, 0, tiled=True)
    oth = swap_core(own)

    pos2 = jnp.stack([x_at, y_at, z_at, core]).astype(jnp.int32)
    slots = [
        jnp.where(core == 0, p * 2 + q, ((z_at + r) & 3) * 2 + t)
        for p, q, r, t in zip(
            (0, 1, 2, 3) * 2, [1 - xl] * 4 + [xl] * 4, (1, 1, 3, 3, 2, 2, 0, 0), (0, 1) * 4
        )
    ]
    pos = jnp.stack([group, core] + slots).astype(jnp.int32)
    first, second, third, keep = attend_project(pos, queries, own, oth, out_weight, 8)
    first, second, third, keep, gate_raw, up_raw = lax.optimization_barrier(
        (first, second, third, keep, gate_weight.T, up_weight.T)
    )
    r1 = move(first, ("p", "z"), (0, 1))
    r2 = move(second, ("p", "z"), (0, -1))
    r3 = move(third, (None, "z"), (0, 2))
    km, ks, sm, ss = prepare(pos2, gate_raw, up_raw, norm_gain[None, :])
    b1, b2, b3, mine = middle(pos2, third, keep, r1, r2, r3)
    terms = [
        move(b1, ("z", "p"), (1, 0)),
        move(b2, ("z", None), (-1, 0)),
        move(b3, ("z", None), (2, 0)),
    ]
    gm, gs = swap_core(sm), swap_core(ss)
    total = mine + sum(t.astype(F32) for t in terms)
    hidden = (residual.astype(F32) + total).astype(BF)

    keep = jnp.where(core == 0, hidden[:, :512], hidden[:, 512:])
    got = swap_core(jnp.where(core == 0, hidden[:, 512:], hidden[:, :512]))
    chip = jnp.where(core == 0, jnp.concatenate([keep, got], 0), jnp.concatenate([got, keep], 0))
    main, side = gather((chip[:, :MCOLS], chip[:, MCOLS:]), (MAIN, SIDE))

    def pieces(*slots):
        return [p for part in (main, side) for c in slots for p in part[c]]

    sums, wm, ws = gate_up(pos2, (0,), pieces(0), (km, gm, ks, gs), (), "first")
    sums, = gate_up(pos2, (1, 2), pieces(1, 2), (wm, ws), (sums,), "middle")
    own_ss, theirs, hm, hs = gate_up(pos2, (3,), pieces(3), (wm, ws), (sums,), "theirs")
    got = swap_core(theirs)
    own_sums, = gate_up(pos2, (3,), (), (wm, ws), (sums, hm, hs), "mine")
    out = finish(own_sums, own_ss, got, norm_gain.shape[0])
    return out.T, hidden


def solution(mesh):
    devices = mesh.devices.reshape(4, 2, 2, 4, 2)
    fine = Mesh(devices, MESH)
    both = P(SEQ, HEAD)
    cols = P(None, SEQ + HEAD)
    return jax.shard_map(
        per_device,
        mesh=fine,
        in_specs=(both, both, both, P(HEAD, None), both, P(), cols, cols),
        out_specs=(cols, both),
        check_vma=False,
    )
```

```python
import functools
import math

import jax
import jax.numpy as jnp
from jax import lax
from jax.experimental import pallas as pl
from jax.experimental.pallas import tpu as pltpu
from jax.sharding import Mesh, PartitionSpec as P


HD = 128
LOW = -1e30
EPS = 1e-5
SEQ = ("y", "xh", "c")
HEAD = ("z", "xl")
MESH = ("y", "xh", "c", "z", "xl")
MAIN = ("yzx", "zxy")
SIDE = ("xyz", "xyz")
OFFSETS = (0, -1, 1, 2)
MCOLS, SCOLS = 384, 128
BF = jnp.bfloat16
F32 = jnp.float32


def move(x, axes, by):
    pairs = []
    for core in range(2):
        if axes[core] is None:
            continue
        for n in range(64):
            at = {"x": n // 16, "y": n // 4 % 4, "z": n % 4}
            to = dict(at)
            if axes[core] == "p":
                to["x"] ^= 1
            else:
                to[axes[core]] = (to[axes[core]] + by[core]) % 4
            pairs.append(tuple(
                (((p["y"] * 2 + p["x"] // 2) * 2 + core) * 4 + p["z"]) * 2 + p["x"] % 2
                for p in (at, to)
            ))
    return lax.ppermute(x, MESH, pairs)


def shift(x, axes, by):
    return move(x, axes, (by, by))


def swap_core(x):
    return lax.ppermute(x, "c", [(0, 1), (1, 0)])


def attend_kernel(pos_ref, q_ref, own_ref, oth_ref, w_hbm, *refs):
    outs, (w_buf, qs, acc, att, sems) = refs[:4], refs[4:]
    blocks = w_buf.shape[0]
    width = w_buf.shape[2]
    for b in range(blocks):
        at = pl.multiple_of(pos_ref[2 + b] * width, width)
        pltpu.make_async_copy(w_hbm.at[:, pl.ds(at, width)], w_buf.at[b], sems.at[b]).start()
    heads = q_ref.shape[1] // HD
    rows = q_ref.shape[0]
    cols = heads * rows
    for h in range(heads):
        qs[pl.ds(h * rows, rows), :] = q_ref[:, h * HD:(h + 1) * HD]
    group = pos_ref[0]
    core = pos_ref[1]
    factor = math.log2(math.e) / math.sqrt(HD)
    qv = qs[...]

    def scores(ref, g):
        return lax.dot_general(
            ref[g, :, :HD], qv, (((1,), (1,)), ((), ())), preferred_element_type=F32
        ) * factor

    def weigh(ref, g, p):
        return lax.dot_general(
            ref[g, :, HD:], p.astype(BF), (((0,), (0,)), ((), ())), preferred_element_type=F32
        )

    key_at = lax.broadcasted_iota(jnp.int32, (rows, cols), 0)
    row_at = lax.broadcasted_iota(jnp.int32, (rows, cols), 1) % rows
    s1 = jnp.where(key_at <= row_at, scores(own_ref, group), LOW)
    s2 = jnp.where(core == 1, scores(oth_ref, group), LOW)
    top = jnp.maximum(jnp.max(s1, axis=0, keepdims=True), jnp.max(s2, axis=0, keepdims=True))
    p1 = jnp.exp2(s1 - top)
    p2 = jnp.where(core == 1, jnp.exp2(s2 - top), 0.0)
    total = jnp.sum(p1, axis=0, keepdims=True) + jnp.sum(p2, axis=0, keepdims=True)
    acc[...] = weigh(own_ref, group, p1) + weigh(oth_ref, group, p2)

    def step(g, carry):
        top, total = carry
        s1 = scores(own_ref, g)
        s2 = scores(oth_ref, g)
        new = jnp.maximum(
            top, jnp.maximum(jnp.max(s1, axis=0, keepdims=True), jnp.max(s2, axis=0, keepdims=True))
        )
        alpha = jnp.exp2(top - new)
        p1 = jnp.exp2(s1 - new)
        p2 = jnp.exp2(s2 - new)
        total = total * alpha + jnp.sum(p1, axis=0, keepdims=True) + jnp.sum(p2, axis=0, keepdims=True)
        acc[...] = acc[...] * alpha + weigh(own_ref, g, p1) + weigh(oth_ref, g, p2)
        return new, total

    top, total = lax.fori_loop(0, group, step, (top, total))
    final = acc[...] / total
    for h in range(heads):
        att[:, h * HD:(h + 1) * HD] = final[:, h * rows:(h + 1) * rows].T.astype(BF)

    for j, out_ref in enumerate(outs):

        def project(i, _, j=j, out_ref=out_ref):
            b = j * 2 + i
            pltpu.make_async_copy(w_hbm.at[:, pl.ds(0, width)], w_buf.at[b], sems.at[b]).wait()
            out_ref[i] = jnp.dot(att[...], w_buf[b], preferred_element_type=F32).astype(BF)
            return 0

        lax.fori_loop(0, 2, project, 0)


def attend_project(pos, q, own, oth, w, blocks):
    rows, cols = q.shape
    depth, wide = w.shape
    width = wide // blocks
    vm = pl.BlockSpec(memory_space=pltpu.VMEM)
    return pl.pallas_call(
        attend_kernel,
        out_shape=[jax.ShapeDtypeStruct((2, rows, width), BF)] * 4,
        in_specs=[pl.BlockSpec(memory_space=pltpu.SMEM), vm, vm, vm, pl.BlockSpec(memory_space=pl.ANY)],
        out_specs=[vm] * 4,
        scratch_shapes=[
            pltpu.VMEM((blocks, depth, width), BF),
            pltpu.VMEM((rows * cols // HD, HD), BF),
            pltpu.VMEM((HD, rows * cols // HD), F32),
            pltpu.VMEM((rows, cols), BF),
            pltpu.SemaphoreType.DMA((blocks,)),
        ],
        compiler_params=pltpu.CompilerParams(vmem_limit_bytes=48 << 20),
        cost_estimate=pl.CostEstimate(flops=4 << 30, bytes_accessed=20 << 20, transcendentals=2 << 20),
        name="attend_project",
    )(pos, q, own, oth, w)


def middle_kernel(pos_ref, third, keep, r1, r2, r3, b1, b2, b3, mine, buf):
    z_at, xl = pos_ref[2], pos_ref[0] & 1

    @pl.when(pos_ref[3] == 0)
    def _():
        for i, (kept, got) in enumerate(((third, r1), (keep, r2))):
            for j in range(2):
                buf[2 * i + j] = kept[j].astype(F32) + got[j].astype(F32)
        for ref, off in ((b1, 1), (b2, 3), (b3, 2)):
            ref[...] = buf[(z_at + off) & 3].astype(BF)
        mine[...] = buf[z_at]

    @pl.when(pos_ref[3] != 0)
    def _():
        for j in range(2):
            buf[j] = (
                keep[j].astype(F32) + r1[j].astype(F32) + r2[j].astype(F32) + r3[j].astype(F32)
            )
        b1[...] = buf[1 - xl].astype(BF)
        mine[...] = buf[xl]


def middle(pos, *pieces):
    rows, cols = pieces[0].shape[1:]
    vm = pl.BlockSpec(memory_space=pltpu.VMEM)
    part = jax.ShapeDtypeStruct((rows, cols), BF)
    return pl.pallas_call(
        middle_kernel,
        out_shape=[part, part, part, jax.ShapeDtypeStruct((rows, cols), F32)],
        in_specs=[pl.BlockSpec(memory_space=pltpu.SMEM)] + [vm] * 5,
        out_specs=[vm] * 4,
        scratch_shapes=[pltpu.VMEM((4, rows, cols), F32)],
        compiler_params=pltpu.CompilerParams(vmem_limit_bytes=16 << 20),
        cost_estimate=pl.CostEstimate(flops=1 << 20, bytes_accessed=4 << 20, transcendentals=0),
        name="middle",
    )(pos, *pieces)


def prep_kernel(pos_ref, g_ref, u_ref, gain_ref, km_ref, ks_ref, sm_ref, ss_ref):
    first = pos_ref[3] == 0
    n = g_ref.shape[0]
    gain = gain_ref[...]
    for j, ref in enumerate((g_ref, u_ref)):
        scaled = (ref[...].astype(F32) * gain).astype(BF)
        low, high = scaled[:, :512], scaled[:, 512:]
        keep = jnp.where(first, low, high)
        send = jnp.where(first, high, low)
        rows = pl.ds(j * n, n)
        km_ref[0, rows, :] = keep[:, :MCOLS]
        ks_ref[0, rows, :] = keep[:, MCOLS:]
        sm_ref[0, rows, :] = send[:, :MCOLS]
        ss_ref[0, rows, :] = send[:, MCOLS:]


def prepare(pos, gate_t, up_t, gain):
    n, depth = gate_t.shape
    wspec = pl.BlockSpec((n, 1024), lambda i, pos: (0, i))
    mspec = pl.BlockSpec((1, 2 * n, MCOLS), lambda i, pos: (i % 2, 0, i // 2))
    sspec = pl.BlockSpec((1, 2 * n, SCOLS), lambda i, pos: (i // 2, 0, i % 2))
    mshape = jax.ShapeDtypeStruct((2, 2 * n, 4 * MCOLS), BF)
    sshape = jax.ShapeDtypeStruct((4, 2 * n, 2 * SCOLS), BF)
    return pl.pallas_call(
        prep_kernel,
        out_shape=[mshape, sshape, mshape, sshape],
        grid_spec=pltpu.PrefetchScalarGridSpec(
            num_scalar_prefetch=1,
            grid=(depth // 1024,),
            in_specs=[wspec, wspec, pl.BlockSpec((1, 1024), lambda i, pos: (0, i))],
            out_specs=[mspec, sspec, mspec, sspec],
        ),
        compiler_params=pltpu.CompilerParams(vmem_limit_bytes=58 << 20),
        cost_estimate=pl.CostEstimate(flops=8 << 20, bytes_accessed=15 << 20, transcendentals=0),
        name="prepare",
    )(pos, gate_t, up_t, gain)


def gate_kernel(which, stage, pos_ref, *refs):
    count = len(which)
    refs = list(refs)
    first = stage == "first"
    last = stage in ("theirs", "mine")
    if stage != "mine":
        main = {c: tuple(refs.pop(0) for _ in range(3)) for c in which}
        side = {c: (refs.pop(0), refs.pop(0)) for c in which}
    if first:
        halves = [refs.pop(0) for _ in range(4)]
        acc, wm, ws = (refs.pop(0) for _ in range(3))
        wsem = refs.pop()
        n2 = halves[0].shape[1]
        for j, src in enumerate(halves):
            pltpu.make_async_copy(
                src, (wm, ws)[j // 2].at[:, pl.ds((j % 2) * n2, n2), :], wsem.at[j // 2]
            ).start()
    else:
        wm, ws, before = (refs.pop(0) for _ in range(3))
    if stage == "theirs":
        own_ss, par_ref, hm, hs = (refs.pop(0) for _ in range(4))
    elif stage == "mine":
        hm, hs, own_ref = (refs.pop(0) for _ in range(3))
    elif stage == "middle":
        acc = refs.pop(0)
    if last:
        acc = refs.pop()
    if not last:
        hm, hs = refs.pop(0), refs.pop(0)
    ssq, table, msem, ssem = refs
    x_at, y_at, z_at, core = (pos_ref[m] for m in range(4))
    both = wm.shape[1]
    n2 = both // 2
    lead = n2 if stage == "theirs" else 0
    rows = n2 if last else both
    squared = stage != "mine"

    def at(base, slot):
        return (base + OFFSETS[slot] + 4) & 3

    def fetch(u, c, j, on):
        for k in range(4):
            a, b = (j, k) if on == 0 else (k, j)
            col = pl.multiple_of(at(z_at, k) * MCOLS, MCOLS)
            src = main[c][max(b - 1, 0)].at[(b % 2) * 4 + a if b < 2 else a]
            pltpu.make_async_copy(src, hm.at[u, :, pl.ds(col, MCOLS)], msem.at[u]).start()

    for m, c in enumerate(which):
        for j in range(4):
            u = m * 4 + j
            x = jnp.where(core == 0, at(x_at, c), at(x_at, j))
            y = jnp.where(core == 0, at(y_at, j), at(y_at, c))
            table[2 * u] = y * 2 + x // 2
            table[2 * u + 1] = x & 1
            if stage == "mine":
                continue
            pl.when(core == 0)(functools.partial(fetch, u, c, j, 0))
            pl.when(core != 0)(functools.partial(fetch, u, c, j, 1))
    for m, c in enumerate(which if stage != "mine" else ()):
        for b in range(4):
            for a in range(4):
                x = at(x_at, a)
                row = pl.multiple_of((at(y_at, b) * 2 + x // 2) * 256, 256)
                col = pl.multiple_of((x & 1) * SCOLS, SCOLS)
                pltpu.make_async_copy(
                    side[c][b // 2].at[(b % 2) * 4 + a],
                    hs.at[m, pl.ds(row, 256), pl.ds(col, SCOLS)],
                    ssem.at[m],
                ).start()
    if first or last:
        acc[...] = jnp.zeros_like(acc)
    if squared:
        ssq[...] = jnp.zeros_like(ssq)
    ones = jnp.ones((8, 128), BF)

    def squares(block):
        part = jnp.zeros((block.shape[0], 128), F32)
        for j in range(block.shape[1] // 128):
            wide = block[:, j * 128:(j + 1) * 128].astype(F32)
            part = part + wide * wide
        return part

    def lane_sums(part):
        big = part.astype(BF)
        small = (part - big.astype(F32)).astype(BF)
        return sum(
            lax.dot_general(ones, t, (((1,), (1,)), ((), ())), preferred_element_type=F32)
            for t in (big, small)
        )

    def unit(u, _):
        if stage != "mine":
            pltpu.make_async_copy(hm.at[u], hm.at[u], msem.at[u]).wait()
        cols = pl.ds(pl.multiple_of(table[2 * u] * 256, 256), 256)
        block = hm[u]
        acc[:rows, cols] += lax.dot_general(
            wm[table[2 * u + 1], pl.ds(lead, rows), :], block, (((1,), (1,)), ((), ())),
            preferred_element_type=F32,
        )
        if squared:
            ssq[cols, :] += squares(block)
        return 0

    if first:
        pltpu.make_async_copy(wm, wm, wsem.at[0]).wait()
    lax.fori_loop(0, 4 * count, unit, 0)
    if first:
        pltpu.make_async_copy(ws, ws, wsem.at[1]).wait()
    for m in range(count if stage != "mine" else 0):
        pltpu.make_async_copy(hs.at[m], hs.at[m], ssem.at[m]).wait()
    piece = 512

    def tail(p, _):
        cols = pl.ds(pl.multiple_of(p * piece, piece), piece)
        total = acc[:rows, cols]
        if last:
            total = total + before[pl.ds(lead, rows), cols]
        part = ssq[cols, :] if squared else None
        for m, c in enumerate(which):
            block = hs[m, cols, :]
            total = total + lax.dot_general(
                ws[at(z_at, c), pl.ds(lead, rows), :], block, (((1,), (1,)), ((), ())),
                preferred_element_type=F32,
            )
            if squared:
                part = part + squares(block)
        if squared:
            sq = (before if last else acc)[both:, cols] + lane_sums(part)
        if stage == "theirs":
            par_ref[:n2, cols] = total.astype(BF)
            own_ss[:, cols] = sq
            big = sq.astype(BF)
            par_ref[n2:, cols] = jnp.concatenate(
                [big.astype(F32), sq - big.astype(F32)], axis=0
            ).astype(BF)
        elif stage == "mine":
            own_ref[:, cols] = total
        else:
            acc[:rows, cols] = total
            acc[rows:, cols] = sq
        return 0

    lax.fori_loop(0, hs.shape[1] // piece, tail, 0)


def gate_up(pos, which, pieces, weights, held, stage):
    n2 = weights[0].shape[1] // (1 if stage == "first" else 2)
    tokens = 2048
    count = len(which)
    any_spec = pl.BlockSpec(memory_space=pl.ANY)
    vm = pl.BlockSpec(memory_space=pltpu.VMEM)
    loose = list(pieces) + (list(weights) if stage == "first" else [])
    fixed = ([] if stage == "first" else list(weights)) + list(held)
    blocks = [
        jax.ShapeDtypeStruct((4 * count, 256, 4 * MCOLS), BF),
        jax.ShapeDtypeStruct((count, tokens, 2 * SCOLS), BF),
    ]
    partial = jax.ShapeDtypeStruct((2 * n2 + 8, tokens), F32)
    out_shape = {
        "first": [
            partial,
            jax.ShapeDtypeStruct((2, 2 * n2, 4 * MCOLS), BF),
            jax.ShapeDtypeStruct((4, 2 * n2, 2 * SCOLS), BF),
        ],
        "middle": [partial],
        "theirs": [
            jax.ShapeDtypeStruct((8, tokens), F32),
            jax.ShapeDtypeStruct((n2 + 16, tokens), BF),
        ] + blocks,
        "mine": [jax.ShapeDtypeStruct((n2, tokens), F32)],
    }[stage]
    last = stage in ("theirs", "mine")
    scratch = [] if last else [pltpu.VMEM(t.shape, BF) for t in blocks]
    scratch += [
        pltpu.VMEM((tokens, 128), F32),
        pltpu.SMEM((8 * count,), jnp.int32),
        pltpu.SemaphoreType.DMA((4 * count,)),
        pltpu.SemaphoreType.DMA((count,)),
    ]
    if stage == "first":
        scratch.append(pltpu.SemaphoreType.DMA((2,)))
    if last:
        scratch.append(pltpu.VMEM((n2, tokens), F32))
    return pl.pallas_call(
        functools.partial(gate_kernel, which, stage),
        out_shape=out_shape,
        in_specs=[pl.BlockSpec(memory_space=pltpu.SMEM)]
        + [any_spec] * len(loose)
        + [vm] * len(fixed),
        out_specs=[vm] * len(out_shape),
        scratch_shapes=scratch,
        input_output_aliases={len(loose) + len(fixed): 0} if stage == "middle" else {},
        compiler_params=pltpu.CompilerParams(vmem_limit_bytes=(10 + 8 * count) << 20),
        cost_estimate=pl.CostEstimate(
            flops=count * n2 * tokens * 4096, bytes_accessed=20 << 20, transcendentals=0
        ),
        name="gate_up",
    )(pos, *loose, *fixed)


def finish_kernel(own_ref, ss_ref, got_ref, out_ref, buf, sems, *, depth):
    n = buf.shape[0]
    piece = 512

    def put(p):
        cols = pl.ds(p * piece, piece)
        return pltpu.make_async_copy(buf.at[:, cols], out_ref.at[:, cols], sems.at[p])

    for p in range(buf.shape[1] // piece):
        cols = pl.ds(p * piece, piece)
        got = got_ref[:, cols].astype(F32)
        total = ss_ref[:1, cols] + got[2 * n:2 * n + 1] + got[2 * n + 8:2 * n + 9]
        scale = lax.rsqrt(total / depth + EPS)
        gate = (own_ref[:n, cols] + got[:n]) * scale
        up = (own_ref[n:, cols] + got[n:2 * n]) * scale
        buf[:, cols] = (gate / (1.0 + jnp.exp(-gate)) * up).astype(BF)
        put(p).start()
    for p in range(buf.shape[1] // piece):
        put(p).wait()


def finish(own, ss, got, depth):
    rows, tokens = own.shape
    n = rows // 2
    vm = pl.BlockSpec(memory_space=pltpu.VMEM)
    return pl.pallas_call(
        functools.partial(finish_kernel, depth=depth),
        out_shape=jax.ShapeDtypeStruct((n, tokens), BF),
        in_specs=[vm] * 3,
        out_specs=pl.BlockSpec(memory_space=pl.ANY),
        scratch_shapes=[pltpu.VMEM((n, tokens), BF), pltpu.SemaphoreType.DMA((tokens // 512,))],
        compiler_params=pltpu.CompilerParams(vmem_limit_bytes=16 << 20),
        cost_estimate=pl.CostEstimate(flops=8 << 20, bytes_accessed=7 << 20, transcendentals=1 << 20),
        name="finish",
    )(own, ss, got)


def gather(blocks, orders):
    axes = [[(o[0][p], o[1][p]) for p in range(3)] for o in orders]

    def around(block, a):
        return [shift(block, a, by) for by in (1, -1, 2)]

    main_near = around(blocks[0], axes[0][0])
    side_near = around(blocks[1], axes[1][0])
    main_near = lax.optimization_barrier([blocks[0]] + main_near)
    cur_main = jnp.stack(main_near)
    cur_main = lax.optimization_barrier(cur_main)
    ahead = shift(cur_main, axes[0][1], 1)
    third = shift(cur_main, axes[0][1], -1)
    fourth = shift(cur_main, axes[0][1], 2)
    side_near = lax.optimization_barrier([blocks[1]] + side_near)
    cur_side = jnp.stack(side_near)
    cur_side = lax.optimization_barrier(cur_side)
    side_next = around(cur_side, axes[1][1])

    def both_ways(block, a):
        return shift(block, a[2], 1), shift(block, a[2], -1)

    low = jnp.concatenate([cur_main, ahead], 0)
    low = lax.optimization_barrier(low)
    low_minus = shift(low, axes[0][2], -1)
    low_plus = shift(low, axes[0][2], 1)
    lows = (low_plus, low_minus)
    thirds = both_ways(third, axes[0])
    fourths = both_ways(fourth, axes[0])
    side_low = jnp.concatenate([cur_side, side_next[0]], 0)
    side_high = jnp.concatenate(side_next[1:], 0)
    side_low, side_high = lax.optimization_barrier((side_low, side_high))
    side_lows = both_ways(side_low, axes[1])
    side_highs = both_ways(side_high, axes[1])
    far_low = shift(lows[0], axes[0][2], 1)
    far_side = (shift(side_lows[0], axes[1][2], 1), shift(side_highs[1], axes[1][2], -1))
    far_third = shift(thirds[1], axes[0][2], -1)
    far_fourth = shift(fourths[1], axes[0][2], -1)
    main = {
        0: (low, third, fourth),
        1: (lows[0], thirds[0], fourths[0]),
        2: (lows[1], thirds[1], fourths[1]),
        3: (far_low, far_third, far_fourth),
    }
    side = {
        0: (side_low, side_high),
        1: (side_lows[0], side_highs[0]),
        2: (side_lows[1], side_highs[1]),
        3: far_side,
    }
    return main, side


def per_device(queries, key_rows, value_rows, out_weight, residual, norm_gain, gate_weight, up_weight):
    y_at, xh, core = lax.axis_index("y"), lax.axis_index("xh"), lax.axis_index("c")
    z_at, xl = lax.axis_index("z"), lax.axis_index("xl")
    x_at = xh * 2 + xl
    group = y_at * 2 + xh

    pair = jnp.concatenate([key_rows, value_rows], axis=1)
    spread = jnp.broadcast_to(pair[None], (8,) + pair.shape)
    own = lax.all_to_all(spread, ("y", "xh"), 0, 0, tiled=True)
    oth = swap_core(own)

    pos2 = jnp.stack([x_at, y_at, z_at, core]).astype(jnp.int32)
    slots = [
        jnp.where(core == 0, p * 2 + q, ((z_at + r) & 3) * 2 + t)
        for p, q, r, t in zip(
            (0, 1, 2, 3) * 2, [1 - xl] * 4 + [xl] * 4, (1, 1, 3, 3, 2, 2, 0, 0), (0, 1) * 4
        )
    ]
    pos = jnp.stack([group, core] + slots).astype(jnp.int32)
    first, second, third, keep = attend_project(pos, queries, own, oth, out_weight, 8)
    first, second, third, keep, gate_raw, up_raw = lax.optimization_barrier(
        (first, second, third, keep, gate_weight.T, up_weight.T)
    )
    r1 = move(first, ("p", "z"), (0, 1))
    r2 = move(second, ("p", "z"), (0, -1))
    r3 = move(third, (None, "z"), (0, 2))
    km, ks, sm, ss = prepare(pos2, gate_raw, up_raw, norm_gain[None, :])
    b1, b2, b3, mine = middle(pos2, third, keep, r1, r2, r3)
    terms = [
        move(b1, ("z", "p"), (1, 0)),
        move(b2, ("z", None), (-1, 0)),
        move(b3, ("z", None), (2, 0)),
    ]
    gm, gs = swap_core(sm), swap_core(ss)
    total = mine + sum(t.astype(F32) for t in terms)
    hidden = (residual.astype(F32) + total).astype(BF)

    keep = jnp.where(core == 0, hidden[:, :512], hidden[:, 512:])
    got = swap_core(jnp.where(core == 0, hidden[:, 512:], hidden[:, :512]))
    chip = jnp.where(core == 0, jnp.concatenate([keep, got], 0), jnp.concatenate([got, keep], 0))
    main, side = gather((chip[:, :MCOLS], chip[:, MCOLS:]), (MAIN, SIDE))

    def pieces(*slots):
        return [p for part in (main, side) for c in slots for p in part[c]]

    sums, wm, ws = gate_up(pos2, (0,), pieces(0), (km, gm, ks, gs), (), "first")
    sums, = gate_up(pos2, (1, 2), pieces(1, 2), (wm, ws), (sums,), "middle")
    own_ss, theirs, hm, hs = gate_up(pos2, (3,), pieces(3), (wm, ws), (sums,), "theirs")
    got = swap_core(theirs)
    own_sums, = gate_up(pos2, (3,), (), (wm, ws), (sums, hm, hs), "mine")
    out = finish(own_sums, own_ss, got, norm_gain.shape[0])
    return out.T, hidden


def solution(mesh):
    devices = mesh.devices.reshape(4, 2, 2, 4, 2)
    fine = Mesh(devices, MESH)
    both = P(SEQ, HEAD)
    cols = P(None, SEQ + HEAD)
    return jax.shard_map(
        per_device,
        mesh=fine,
        in_specs=(both, both, both, P(HEAD, None), both, P(), cols, cols),
        out_specs=(cols, both),
        check_vma=False,
    )
```
